32 devices in a mesh: fsdp: 8 (over z, core), context: 2 (over x), tensor: 2 (over y).
Axes of the slice: x: 2, y: 2, z: 4, core: 2. Of those that a mesh axis runs over, the one named last changes fastest.
Arguments:
- tokens: bfloat16 [16, 2048, 1024], P('fsdp', 'context'), may hold values from -6 to 6
- segment_ids: int32 [16, 2048], P('fsdp', 'context'), may hold values from 0 to 7, never falling along the last dimension, each value on 1 to 1024 neighbouring positions
- qkv_weight: bfloat16 [3, 1024, 1024], P(None, 'fsdp', 'tensor'), may hold values from -0.1875 to 0.1875
- qv_bias: bfloat16 [2, 16, 64], P(None, 'tensor', 'fsdp'), may hold values from -1.5 to 1.5
- proj_weight: bfloat16 [1024, 1024], P('tensor', 'fsdp'), may hold values from -0.75 to 0.75
- proj_bias: bfloat16 [1024], P('fsdp'), may hold values from -1.5 to 1.5
- first_gain: bfloat16 [1024], P('fsdp'), may hold values from 0.5 to 1.5
- first_shift: bfloat16 [1024], P('fsdp'), may hold values from -1.5 to 1.5
- up_weight: bfloat16 [1024, 4096], P('fsdp', 'tensor'), may hold values from -0.1875 to 0.1875
- up_bias: bfloat16 [64, 64], P('tensor', 'fsdp'), may hold values from -1.5 to 1.5
- down_weight: bfloat16 [4096, 1024], P('tensor', 'fsdp'), may hold values from -0.09375 to 0.09375
- down_bias: bfloat16 [1024], P('fsdp'), may hold values from -1.5 to 1.5
- second_gain: bfloat16 [1024], P('fsdp'), may hold values from 0.5 to 1.5
- second_shift: bfloat16 [1024], P('fsdp'), may hold values from -1.5 to 1.5
- out_grad: bfloat16 [16, 2048, 1024], P('fsdp', 'context'), may hold values from -6 to 6
Outputs:
- layer_output: bfloat16 [16, 2048, 1024], P('fsdp', 'context')
- tokens_grad: bfloat16 [16, 2048, 1024], P('fsdp', 'context')
- qkv_grad: float32 [3, 1024, 1024], P(None, 'fsdp', 'tensor')
- qv_bias_grad: float32 [2, 16, 64], P(None, 'tensor', 'fsdp')
- proj_grad: float32 [1024, 1024], P('tensor', 'fsdp')
- proj_bias_grad: float32 [1024], P('fsdp')
- first_gain_grad: float32 [1024], P('fsdp')
- first_shift_grad: float32 [1024], P('fsdp')
- up_grad: float32 [1024, 4096], P('fsdp', 'tensor')
- up_bias_grad: float32 [64, 64], P('tensor', 'fsdp')
- down_grad: float32 [4096, 1024], P('tensor', 'fsdp')
- down_bias_grad: float32 [1024], P('fsdp')
- second_gain_grad: float32 [1024], P('fsdp')
- second_shift_grad: float32 [1024], P('fsdp')
The draws below stay inside these ranges and needn't reach their ends.
Inputs may be any that keep to these rules, and one draw needn't show every extreme that they name: `segment_ids`: within each sequence the ids never fall; each of the 8 segments covers 1 to 1024 positions and one covers exactly 1024.
All inputs are finite; a program needn't handle non-finite values.
Results may differ from the reference program's by a relative error of at most 0.019.
Values may be sent and summed in bfloat16 or wider, within the bound.
A program may use at most 384 MiB of HBM per device.

```python
import math
import jax
import jax.numpy as jnp
import numpy as np
from jax import lax

D = 1024
HEADS = 16
HD = 64
FF = 4096
LEN = 2048
SEGS = 8
SEG_MOST = 1024
SEQS = 16


def block_scale(own_key, shape, cuts, smallest, largest):
    level, own = 1.0, jax.random.fold_in(own_key, 6)
    for dim, shards_of in cuts:
        draws = jnp.exp(jax.random.uniform(jax.random.fold_in(own, dim), (shards_of,), jnp.float32, smallest / len(cuts), largest / len(cuts)))
        level = level * jnp.repeat(draws, shape[dim] // shards_of).reshape([-1 if axis == dim else 1 for axis in range(len(shape))])
    return level


def profile(number_of, total, most, skew):
    portions = [(1 << 20) // math.isqrt(rank ** skew) + 1 for rank in range(2, number_of + 1)]
    surplus, counts = total - most - (number_of - 1), [1] * (number_of - 1)
    while surplus > 0:
        movable = [i for i in range(number_of - 1) if counts[i] < most]
        whole, left = sum([portions[i] for i in movable]), surplus
        for i in movable:
            extra = min(most - counts[i], max(1, left * portions[i] // whole), surplus)
            counts[i] = counts[i] + extra
            surplus = surplus - extra
    return np.array([most] + counts)


def ragged_sizes(stream_key, count, total, limit, lean):
    if count == 2:
        one = jax.random.randint(stream_key, (), max(1, total - limit), min(limit, total - 1) + 1)
        return jnp.stack([one, total - one])
    sizes = jnp.asarray(profile(count, total, limit, lean), jnp.int32)
    twos = (count - 1) // 2
    giver, taker = sizes[1:1 + 2 * twos:2], sizes[2:2 + 2 * twos:2]
    room = jnp.minimum(giver - 1, limit - taker)
    shifted = jax.random.randint(jax.random.fold_in(stream_key, 1), (twos,), 0, 1 << 20) % (room + 1)
    sizes = sizes.at[1:1 + 2 * twos:2].set(giver - shifted).at[2:2 + 2 * twos:2].set(taker + shifted)
    return sizes[jax.random.permutation(jax.random.fold_in(stream_key, 2), count)]


def scatter_about(own_key, dims, deviation, limit, split=(), kind=jnp.bfloat16):
    drawn = deviation * jax.random.normal(own_key, dims, jnp.float32)
    if split:
        drawn = drawn * block_scale(own_key, dims, split, -0.22, 0.18)
    return jnp.clip(drawn, -limit, limit).astype(kind)


def setup_inputs(seed: int = 0) -> dict:
    arg_keys = jax.random.split(jax.random.key(seed), 16)
    return {
        "tokens": scatter_about(arg_keys[0], (SEQS, LEN, D), 1.0, 6.0, ((0, 8), (1, 2))),
        "segment_ids": jax.vmap(lambda own: jnp.searchsorted(jnp.cumsum(ragged_sizes(own, SEGS, LEN, SEG_MOST, 2)), jnp.arange(LEN), side="right"))(jax.random.split(arg_keys[1], SEQS)).reshape((SEQS, LEN)).astype(jnp.int32),
        "qkv_weight": scatter_about(arg_keys[2], (3, D, D), D ** -0.5, 0.1875, ((1, 8), (2, 2))),
        "qv_bias": scatter_about(arg_keys[3], (2, HEADS, HD), 0.3, 1.5, ((1, 2), (2, 8))),
        "proj_weight": scatter_about(arg_keys[4], (D, D), (D // 16) ** -0.5, 0.75, ((0, 2), (1, 8))),
        "proj_bias": scatter_about(arg_keys[5], (D,), 0.3, 1.5, ((0, 8),)),
        "first_gain": jnp.clip(1.0 + 0.1 * jax.random.normal(arg_keys[6], (D,), jnp.float32), 0.5, 1.5).astype(jnp.bfloat16),
        "first_shift": scatter_about(arg_keys[7], (D,), 0.3, 1.5, ((0, 8),)),
        "up_weight": scatter_about(arg_keys[8], (D, FF), D ** -0.5, 0.1875, ((0, 8), (1, 2))),
        "up_bias": scatter_about(arg_keys[9], (FF // HD, HD), 0.3, 1.5, ((0, 2), (1, 8))),
        "down_weight": scatter_about(arg_keys[10], (FF, D), FF ** -0.5, 0.09375, ((0, 2), (1, 8))),
        "down_bias": scatter_about(arg_keys[11], (D,), 0.3, 1.5, ((0, 8),)),
        "second_gain": jnp.clip(1.0 + 0.1 * jax.random.normal(arg_keys[12], (D,), jnp.float32), 0.5, 1.5).astype(jnp.bfloat16),
        "second_shift": scatter_about(arg_keys[13], (D,), 0.3, 1.5, ((0, 8),)),
        "out_grad": scatter_about(arg_keys[14], (SEQS, LEN, D), 1.0, 6.0, ((0, 8), (1, 2))),
    }


HIGHEST_PRECISION = lax.Precision.HIGHEST
NORM_EPS = 1e-05

@jax.custom_vjp
def low(v):
    return lax.optimization_barrier(v.astype(jnp.bfloat16)).astype(jnp.float32)

@jax.custom_vjp
def low_back(v):
    return v

def low_keep(v):
    return (low(v), None)

def low_pass(kept, grad):
    return (grad,)

def back_keep(v):
    return (v, None)

def back_low(kept, grad):
    return (low(grad),)
low.defvjp(low_keep, low_pass)
low_back.defvjp(back_keep, back_low)

def both_ways(values):
    return low(low_back(values))

def layer_norm(hidden_rows, norm_gain, norm_shift):
    row_mean = lax.optimization_barrier(jnp.mean(hidden_rows, axis=-1, keepdims=True))
    centred = hidden_rows - row_mean
    variance = lax.optimization_barrier(jnp.mean(centred * centred, axis=-1, keepdims=True))
    return centred * lax.rsqrt(variance + NORM_EPS) * norm_gain + norm_shift

def attend_one(pieces):
    query_heads, key_heads, value_heads, seg_row = pieces
    score_scale = float(HD) ** (-0.5)
    logits = low_back(score_scale * jnp.einsum('qhe,khe->hqk', query_heads, key_heads, precision=HIGHEST_PRECISION))
    same_doc = seg_row[:, None] == seg_row[None, :]
    logits = jnp.where(same_doc[None, :, :], logits, -1e+30)
    row_top = lax.optimization_barrier(jnp.max(logits, axis=-1, keepdims=True))
    weights = jnp.exp(logits - row_top)
    soft_weights = low(weights / lax.optimization_barrier(jnp.sum(weights, axis=-1, keepdims=True)))
    return jnp.einsum('hqk,khe->qhe', soft_weights, value_heads, precision=HIGHEST_PRECISION)

def forward(tokens, qkv_weight, qv_bias, proj_weight, proj_bias, first_gain, first_shift, up_weight, up_bias, down_weight, down_bias, second_gain, second_shift, segment_ids):
    group_count = tokens.shape[0]
    token_rows = tokens.reshape(group_count * LEN, D)
    projected = jnp.einsum('rd,cde->cre', token_rows, qkv_weight, precision=HIGHEST_PRECISION)
    bias_rows = qv_bias.reshape(2, D)
    query_rows = both_ways(projected[0] + bias_rows[0])
    key_rows = both_ways(projected[1])
    value_rows = both_ways(projected[2] + bias_rows[1])
    head_shape = (group_count, LEN, HEADS, HD)
    mixed = lax.map(jax.checkpoint(attend_one), (query_rows.reshape(head_shape), key_rows.reshape(head_shape), value_rows.reshape(head_shape), segment_ids))
    context_rows = both_ways(mixed.reshape(group_count * LEN, D))
    attn_out = low_back(jnp.dot(context_rows, proj_weight, precision=HIGHEST_PRECISION) + proj_bias)
    first_norm = layer_norm(token_rows + attn_out, first_gain, first_shift)
    hidden_pre = low_back(jnp.dot(low(first_norm), up_weight, precision=HIGHEST_PRECISION) + up_bias.reshape(FF))
    activation = low(jax.nn.gelu(hidden_pre, approximate=False))
    branch = low_back(jnp.dot(activation, down_weight, precision=HIGHEST_PRECISION) + down_bias)
    return layer_norm(first_norm + branch, second_gain, second_shift).reshape(group_count, LEN, D)

def reference(tokens, segment_ids, qkv_weight, qv_bias, proj_weight, proj_bias, first_gain, first_shift, up_weight, up_bias, down_weight, down_bias, second_gain, second_shift, out_grad):
    group = math.gcd(SEQS, max(1, 4096 // LEN))
    rounds = SEQS // group
    weight_list = (qkv_weight.astype(jnp.float32), qv_bias.astype(jnp.float32), proj_weight.astype(jnp.float32), proj_bias.astype(jnp.float32), first_gain.astype(jnp.float32), first_shift.astype(jnp.float32), up_weight.astype(jnp.float32), up_bias.astype(jnp.float32), down_weight.astype(jnp.float32), down_bias.astype(jnp.float32), second_gain.astype(jnp.float32), second_shift.astype(jnp.float32))

    def advance(totals, pieces):
        tok_group, seg_group, cot_group = pieces

        def run(tok_f, weights_f):
            return forward(tok_f, weights_f[0], weights_f[1], weights_f[2], weights_f[3], weights_f[4], weights_f[5], weights_f[6], weights_f[7], weights_f[8], weights_f[9], weights_f[10], weights_f[11], seg_group)
        result, pull = jax.vjp(run, tok_group.astype(jnp.float32), weight_list)
        tok_grad, weight_grads = pull(cot_group.astype(jnp.float32))
        totals = tuple((total + grad for total, grad in zip(totals, weight_grads)))
        return (totals, (result.astype(jnp.bfloat16), tok_grad.astype(jnp.bfloat16)))
    start = tuple((jnp.zeros(weight.shape, jnp.float32) for weight in weight_list))
    totals, outputs = lax.scan(advance, start, (tokens.reshape(rounds, group, LEN, D), segment_ids.reshape(rounds, group, LEN), out_grad.reshape(rounds, group, LEN, D)))
    layer_output = outputs[0].reshape(SEQS, LEN, D)
    tokens_grad = outputs[1].reshape(SEQS, LEN, D)
    return (layer_output, tokens_grad, totals[0], totals[1], totals[2], totals[3], totals[4], totals[5], totals[6], totals[7], totals[8], totals[9], totals[10], totals[11])
```

```python
import functools

import jax
import jax.numpy as jnp
from jax import lax
from jax.experimental import pallas as pl
from jax.experimental.pallas import tpu as pltpu
from jax.sharding import PartitionSpec as P

NORM_EPS = 1e-05


def layer_norm(hidden_rows, norm_gain, norm_shift):
    row_mean = jnp.mean(hidden_rows, axis=-1, keepdims=True)
    centred = hidden_rows - row_mean
    variance = jnp.mean(centred * centred, axis=-1, keepdims=True)
    return centred * lax.rsqrt(variance + NORM_EPS) * norm_gain + norm_shift


def exact_gelu(values):
    return jax.nn.gelu(values, approximate=False)


def masked_logits(query_heads, key_heads, seg_query, seg_key, score_scale):
    logits = (
        jnp.einsum("qhe,khe->hqk", query_heads, key_heads, preferred_element_type=jnp.float32)
        * score_scale
    )
    same_doc = (seg_query[:, None] == seg_key[None, :])[None, :, :]
    return jnp.where(same_doc, logits, -1e30)


def on_device_general(
    tokens,
    segment_ids,
    qkv_weight,
    qv_bias,
    proj_weight,
    proj_bias,
    first_gain,
    first_shift,
    up_weight,
    up_bias,
    down_weight,
    down_bias,
    second_gain,
    second_shift,
    out_grad,
):
    seq_count, span, width = tokens.shape
    total_rows = seq_count * span
    share = total_rows // lax.axis_size("tensor")
    row_start = lax.axis_index("tensor") * share
    token_rows = tokens.reshape(total_rows, width)
    gathered = (
        lax.all_gather(qkv_weight, "fsdp", axis=1, tiled=True),
        lax.all_gather(qv_bias, "fsdp", axis=2, tiled=True),
        lax.all_gather(proj_weight, "fsdp", axis=1, tiled=True),
        lax.all_gather(proj_bias, "fsdp", axis=0, tiled=True),
        lax.all_gather(first_gain, "fsdp", axis=0, tiled=True),
        lax.all_gather(first_shift, "fsdp", axis=0, tiled=True),
        lax.all_gather(up_weight, "fsdp", axis=0, tiled=True),
        lax.all_gather(up_bias, "fsdp", axis=1, tiled=True),
        lax.all_gather(down_weight, "fsdp", axis=1, tiled=True),
        lax.all_gather(down_bias, "fsdp", axis=0, tiled=True),
        lax.all_gather(second_gain, "fsdp", axis=0, tiled=True),
        lax.all_gather(second_shift, "fsdp", axis=0, tiled=True),
    )
    qkv_full, qv_full, proj_full, proj_add, gain_one, shift_one = (
        gathered[0],
        gathered[1],
        gathered[2],
        gathered[3],
        gathered[4],
        gathered[5],
    )
    up_full, up_add, down_full, down_add, gain_two, shift_two = (
        gathered[6],
        gathered[7],
        gathered[8],
        gathered[9],
        gathered[10],
        gathered[11],
    )
    local_width = qkv_full.shape[2]
    head_count = qv_full.shape[1]
    head_size = qv_full.shape[2]
    score_scale = float(head_size) ** (-0.5)
    projected = jnp.einsum("rd,cde->cre", token_rows, qkv_full, preferred_element_type=jnp.float32)
    bias_rows = qv_full.reshape(2, local_width).astype(jnp.float32)
    head_shape = (seq_count, span, head_count, head_size)
    query_heads = (projected[0] + bias_rows[0]).astype(jnp.bfloat16).reshape(head_shape)
    key_heads = projected[1].astype(jnp.bfloat16).reshape(head_shape)
    value_heads = (projected[2] + bias_rows[1]).astype(jnp.bfloat16).reshape(head_shape)
    key_all, value_all, seg_all = (
        lax.all_gather(key_heads, "context", axis=1, tiled=True),
        lax.all_gather(value_heads, "context", axis=1, tiled=True),
        lax.all_gather(segment_ids, "context", axis=1, tiled=True),
    )

    def attend_forward(pieces):
        query_one, key_one, value_one, seg_query, seg_key = pieces
        logits = masked_logits(query_one, key_one, seg_query, seg_key, score_scale)
        row_top = jnp.max(logits, axis=-1, keepdims=True)
        weights = jnp.exp(logits - row_top)
        row_total = jnp.sum(weights, axis=-1, keepdims=True)
        soft_low = (weights / row_total).astype(jnp.bfloat16)
        mixed_one = jnp.einsum(
            "hqk,khe->qhe", soft_low, value_one, preferred_element_type=jnp.float32
        )
        return (mixed_one.astype(jnp.bfloat16), row_top + jnp.log(row_total))

    mixed, log_totals = lax.map(
        attend_forward, (query_heads, key_all, value_all, segment_ids, seg_all)
    )
    context_low = mixed.reshape(total_rows, local_width)
    attn_part = jnp.dot(context_low, proj_full, preferred_element_type=jnp.float32)
    attn_share = lax.psum_scatter(
        attn_part, "tensor", scatter_dimension=0, tiled=True
    ) + proj_add.astype(jnp.float32)
    token_share = lax.dynamic_slice_in_dim(token_rows, row_start, share, 0).astype(jnp.float32)
    first_share, first_pull = jax.vjp(
        layer_norm,
        token_share + attn_share,
        gain_one.astype(jnp.float32),
        shift_one.astype(jnp.float32),
    )
    first_low = lax.all_gather(first_share.astype(jnp.bfloat16), "tensor", axis=0, tiled=True)
    hidden_pre = jnp.dot(first_low, up_full, preferred_element_type=jnp.float32) + up_add.reshape(
        -1
    ).astype(jnp.float32)
    activation, gelu_pull = jax.vjp(exact_gelu, hidden_pre)
    act_low = activation.astype(jnp.bfloat16)
    down_part = jnp.dot(act_low, down_full, preferred_element_type=jnp.float32)
    branch_share = lax.psum_scatter(
        down_part, "tensor", scatter_dimension=0, tiled=True
    ) + down_add.astype(jnp.float32)
    output_share, second_pull = jax.vjp(
        layer_norm,
        first_share + branch_share,
        gain_two.astype(jnp.float32),
        shift_two.astype(jnp.float32),
    )
    qkv_back, proj_back, up_back, down_back = (
        lax.all_gather(qkv_weight, "fsdp", axis=1, tiled=True),
        lax.all_gather(proj_weight, "fsdp", axis=1, tiled=True),
        lax.all_gather(up_weight, "fsdp", axis=0, tiled=True),
        lax.all_gather(down_weight, "fsdp", axis=1, tiled=True),
    )
    cot_share = lax.dynamic_slice_in_dim(
        out_grad.reshape(total_rows, width), row_start, share, 0
    ).astype(jnp.float32)
    grad_second, gain_two_part, shift_two_part = second_pull(cot_share)
    branch_low = lax.all_gather(grad_second.astype(jnp.bfloat16), "tensor", axis=0, tiled=True)
    grad_down_bias = jnp.sum(branch_low.astype(jnp.float32), axis=0)
    grad_down = jnp.einsum("rf,rd->fd", act_low, branch_low, preferred_element_type=jnp.float32)
    grad_act = jnp.einsum("rd,fd->rf", branch_low, down_back, preferred_element_type=jnp.float32)
    hidden_low = gelu_pull(grad_act)[0].astype(jnp.bfloat16)
    grad_up_bias = jnp.sum(hidden_low.astype(jnp.float32), axis=0).reshape(up_add.shape)
    grad_up = jnp.einsum("rd,rf->df", first_low, hidden_low, preferred_element_type=jnp.float32)
    norm_part = jnp.einsum("rf,df->rd", hidden_low, up_back, preferred_element_type=jnp.float32)
    grad_first = grad_second + lax.psum_scatter(
        norm_part, "tensor", scatter_dimension=0, tiled=True
    )
    grad_in_one, gain_one_part, shift_one_part = first_pull(grad_first)
    attn_low = lax.all_gather(grad_in_one.astype(jnp.bfloat16), "tensor", axis=0, tiled=True)
    grad_proj_bias = jnp.sum(attn_low.astype(jnp.float32), axis=0)
    grad_proj = jnp.einsum("rl,rd->ld", context_low, attn_low, preferred_element_type=jnp.float32)
    grad_context = (
        jnp.einsum("rd,ld->rl", attn_low, proj_back, preferred_element_type=jnp.float32)
        .astype(jnp.bfloat16)
        .reshape(head_shape)
    )

    def attend_backward(pieces):
        query_one, key_one, value_one, seg_query, seg_key, log_total, context_grad = pieces
        logits = masked_logits(query_one, key_one, seg_query, seg_key, score_scale)
        soft_again = jnp.exp(logits - log_total)
        grad_soft = jnp.einsum(
            "qhe,khe->hqk", context_grad, value_one, preferred_element_type=jnp.float32
        )
        row_delta = jnp.sum(grad_soft * soft_again, axis=-1, keepdims=True)
        grad_logits = (soft_again * (grad_soft - row_delta)).astype(jnp.bfloat16)
        query_grad = (
            jnp.einsum("hqk,khe->qhe", grad_logits, key_one, preferred_element_type=jnp.float32)
            * score_scale
        ).astype(jnp.bfloat16)
        key_part = (
            jnp.einsum("hqk,qhe->khe", grad_logits, query_one, preferred_element_type=jnp.float32)
            * score_scale
        )
        value_part = jnp.einsum(
            "hqk,qhe->khe",
            soft_again.astype(jnp.bfloat16),
            context_grad,
            preferred_element_type=jnp.float32,
        )
        return (query_grad, key_part, value_part)

    grad_query, key_terms, value_terms = lax.map(
        attend_backward,
        (query_heads, key_all, value_all, segment_ids, seg_all, log_totals, grad_context),
    )
    key_grad, value_grad = (
        lax.psum_scatter(
            key_terms.astype(jnp.bfloat16), "context", scatter_dimension=1, tiled=True
        ).astype(jnp.float32),
        lax.psum_scatter(
            value_terms.astype(jnp.bfloat16), "context", scatter_dimension=1, tiled=True
        ).astype(jnp.float32),
    )
    grad_stack = jnp.stack(
        [
            grad_query.reshape(total_rows, local_width),
            key_grad.astype(jnp.bfloat16).reshape(total_rows, local_width),
            value_grad.astype(jnp.bfloat16).reshape(total_rows, local_width),
        ]
    )
    stack_sums = jnp.sum(grad_stack.astype(jnp.float32), axis=1)
    grad_qv_bias = jnp.stack([stack_sums[0], stack_sums[2]]).reshape(qv_full.shape)
    grad_qkv = jnp.einsum("rd,cre->cde", token_rows, grad_stack, preferred_element_type=jnp.float32)
    input_part = jnp.einsum("cre,cde->rd", grad_stack, qkv_back, preferred_element_type=jnp.float32)
    norm_parts = jnp.tile(
        jnp.stack([gain_one_part, shift_one_part, gain_two_part, shift_two_part]),
        (lax.axis_size("tensor"), 1),
    )
    input_share, norm_sums = (
        lax.psum_scatter(
            input_part.astype(jnp.bfloat16), "tensor", scatter_dimension=0, tiled=True
        ).astype(jnp.float32),
        lax.psum_scatter(
            norm_parts.astype(jnp.bfloat16), "tensor", scatter_dimension=0, tiled=True
        ).astype(jnp.float32),
    )
    grad_share_low = (grad_in_one + input_share).astype(jnp.bfloat16)
    out_rows, grad_rows = (
        lax.all_gather(output_share.astype(jnp.bfloat16), "tensor", axis=0, tiled=True),
        lax.all_gather(grad_share_low, "tensor", axis=0, tiled=True),
    )
    local_grads = (
        grad_qkv,
        grad_qv_bias,
        grad_proj,
        grad_proj_bias,
        norm_sums[0],
        norm_sums[1],
        grad_up,
        grad_up_bias,
        grad_down,
        grad_down_bias,
        norm_sums[2],
        norm_sums[3],
    )
    summed = (
        lax.psum(local_grads[0].astype(jnp.bfloat16), "context").astype(jnp.float32),
        lax.psum(local_grads[1].astype(jnp.bfloat16), "context").astype(jnp.float32),
        lax.psum(local_grads[2].astype(jnp.bfloat16), "context").astype(jnp.float32),
        lax.psum(local_grads[3].astype(jnp.bfloat16), "context").astype(jnp.float32),
        lax.psum(local_grads[4].astype(jnp.bfloat16), "context").astype(jnp.float32),
        lax.psum(local_grads[5].astype(jnp.bfloat16), "context").astype(jnp.float32),
        lax.psum(local_grads[6].astype(jnp.bfloat16), "context").astype(jnp.float32),
        lax.psum(local_grads[7].astype(jnp.bfloat16), "context").astype(jnp.float32),
        lax.psum(local_grads[8].astype(jnp.bfloat16), "context").astype(jnp.float32),
        lax.psum(local_grads[9].astype(jnp.bfloat16), "context").astype(jnp.float32),
        lax.psum(local_grads[10].astype(jnp.bfloat16), "context").astype(jnp.float32),
        lax.psum(local_grads[11].astype(jnp.bfloat16), "context").astype(jnp.float32),
    )
    owned = (
        lax.psum_scatter(
            summed[0].astype(jnp.bfloat16), "fsdp", scatter_dimension=1, tiled=True
        ).astype(jnp.float32),
        lax.psum_scatter(
            summed[1].astype(jnp.bfloat16), "fsdp", scatter_dimension=2, tiled=True
        ).astype(jnp.float32),
        lax.psum_scatter(
            summed[2].astype(jnp.bfloat16), "fsdp", scatter_dimension=1, tiled=True
        ).astype(jnp.float32),
        lax.psum_scatter(
            summed[3].astype(jnp.bfloat16), "fsdp", scatter_dimension=0, tiled=True
        ).astype(jnp.float32),
        lax.psum_scatter(
            summed[4].astype(jnp.bfloat16), "fsdp", scatter_dimension=0, tiled=True
        ).astype(jnp.float32),
        lax.psum_scatter(
            summed[5].astype(jnp.bfloat16), "fsdp", scatter_dimension=0, tiled=True
        ).astype(jnp.float32),
        lax.psum_scatter(
            summed[6].astype(jnp.bfloat16), "fsdp", scatter_dimension=0, tiled=True
        ).astype(jnp.float32),
        lax.psum_scatter(
            summed[7].astype(jnp.bfloat16), "fsdp", scatter_dimension=1, tiled=True
        ).astype(jnp.float32),
        lax.psum_scatter(
            summed[8].astype(jnp.bfloat16), "fsdp", scatter_dimension=1, tiled=True
        ).astype(jnp.float32),
        lax.psum_scatter(
            summed[9].astype(jnp.bfloat16), "fsdp", scatter_dimension=0, tiled=True
        ).astype(jnp.float32),
        lax.psum_scatter(
            summed[10].astype(jnp.bfloat16), "fsdp", scatter_dimension=0, tiled=True
        ).astype(jnp.float32),
        lax.psum_scatter(
            summed[11].astype(jnp.bfloat16), "fsdp", scatter_dimension=0, tiled=True
        ).astype(jnp.float32),
    )
    layer_output = out_rows.reshape(seq_count, span, width)
    tokens_grad = grad_rows.reshape(seq_count, span, width)
    return (
        layer_output,
        tokens_grad,
        owned[0],
        owned[1],
        owned[2],
        owned[3],
        owned[4],
        owned[5],
        owned[6],
        owned[7],
        owned[8],
        owned[9],
        owned[10],
        owned[11],
    )


AXES = ("z", "core", "context", "tensor")
BF = jnp.bfloat16
F32 = jnp.float32
SUB = 2
MASKED = -1e30
NT = (((1,), (1,)), ((), ()))
NN = (((1,), (0,)), ((), ()))

def _dot(a, b, dims):
    return lax.dot_general(a, b, dims, preferred_element_type=jnp.float32)

def attn_fwd_kernel(lo_ref, hi_ref, shift_ref, q_ref, k_ref, v_ref, segk_ref, segq_ref, o_ref, lse_ref, vt_ref, *, bq, bk, hd, scale, nblk):
    qb = pl.program_id(0)
    shift = shift_ref[0]
    pair = q_ref.shape[1]
    heads = pair // hd

    @pl.when(qb == 0)
    def _():
        for j in range(nblk):
            vt_ref[j] = v_ref[j * bk:(j + 1) * bk, :].T

    gq = lax.rem(qb + shift // (bq // bk), nblk * bk // bq)
    lane = lax.broadcasted_iota(jnp.int32, (bq, pair), 1) // hd
    q = q_ref[...] * jnp.asarray(scale, q_ref.dtype)
    qs = [jnp.where(lane == h, q, jnp.zeros_like(q)) for h in range(heads)]
    segq = segq_ref[0:1, :]

    def body(i, carry):
        j = lo_ref[gq] + i * SUB
        sbs = [lax.rem(j + u + shift, nblk) for u in range(SUB)]
        sc = [[None] * SUB for _ in range(heads)]
        for u in range(SUB):
            ks = pl.multiple_of(sbs[u] * bk, bk)
            kb = k_ref[pl.ds(ks, bk), :]
            same = segk_ref[pl.ds(ks, bk), :]
            same = jnp.concatenate([same] * (bq // same.shape[1]), axis=1) == segq
            for h in range(heads):
                sc[h][u] = jnp.where(same, _dot(kb, qs[h], NT), MASKED)
        out = []
        for h in range(heads):
            m, l, acc = carry[h]
            mn = m
            for u in range(SUB):
                mn = jnp.maximum(mn, jnp.max(sc[h][u], axis=0, keepdims=True))
            a = jnp.exp(m - mn)
            l = l * a
            acc = acc * a
            for u in range(SUB):
                p = jnp.exp(sc[h][u] - mn)
                l = l + jnp.sum(p, axis=0, keepdims=True)
                acc = acc + _dot(vt_ref[sbs[u], h * hd:(h + 1) * hd, :], p.astype(jnp.bfloat16), NN)
            out.append((mn, l, acc))
        return tuple(out)

    init = tuple((jnp.full((1, bq), MASKED, jnp.float32), jnp.zeros((1, bq), jnp.float32), jnp.zeros((hd, bq), jnp.float32)) for _ in range(heads))
    res = lax.fori_loop(0, (hi_ref[gq] - lo_ref[gq] + SUB - 1) // SUB, body, init)
    o_ref[...] = jnp.concatenate([acc / l for (m, l, acc) in res], axis=0).T.astype(o_ref.dtype)
    lse_ref[0] = jnp.concatenate([m + jnp.log(l) for (m, l, acc) in res], axis=0)

def attn_bwd_kernel(lo_ref, hi_ref, shift_ref, q_ref, k_ref, v_ref, o_ref, do_ref, lse_ref, segk_ref, segq_ref, out_ref,
                    qs_ref, dos_ref, kt_ref, delta_ref, dqt_ref, dk_ref, dv_ref, *, bq, bk, hd, scale, nblk):
    w = pl.program_id(0)
    shift = shift_ref[0]
    rows, pair = q_ref.shape
    heads = pair // hd

    @pl.when(w == 0)
    def _():
        lane = lax.broadcasted_iota(jnp.int32, (bk, pair), 1) // hd
        pick = (lax.broadcasted_iota(jnp.int32, (8, pair), 0) == lax.broadcasted_iota(jnp.int32, (8, pair), 1) // hd).astype(jnp.float32)
        sc = jnp.asarray(scale, q_ref.dtype)
        for j in range(nblk):
            r = slice(j * bk, (j + 1) * bk)
            q = q_ref[r, :] * sc
            do = do_ref[r, :]
            for h in range(heads):
                qs_ref[h, r, :] = jnp.where(lane == h, q, jnp.zeros_like(q))
                dos_ref[h, r, :] = jnp.where(lane == h, do, jnp.zeros_like(do))
            kt_ref[j] = (k_ref[r, :] * sc).T
            prod = do.astype(jnp.float32) * o_ref[r, :].astype(jnp.float32)
            delta_ref[:, r] = lax.dot_general(pick, prod, NT, preferred_element_type=jnp.float32, precision=lax.Precision.HIGHEST)


        dqt_ref[...] = jnp.zeros(dqt_ref.shape, jnp.float32)

        def outer(kb, _):
            gk = lax.rem(kb + shift, nblk)
            nq = nblk * bk // bq
            ks = pl.multiple_of(kb * bk, bk)
            kblk = k_ref[pl.ds(ks, bk), :]
            vblk = v_ref[pl.ds(ks, bk), :]
            segk = segk_ref[pl.ds(ks, bk), :]
            segk = jnp.concatenate([segk] * (bq // segk.shape[1]), axis=1)

            def inner(j, carry):
                dk, dv = carry
                sb = lax.rem(j + shift // (bq // bk) if bq >= bk else j + shift * (bk // bq), nq)
                qo = pl.multiple_of(sb * bq, bq)
                same = segk == segq_ref[0:1, pl.ds(qo, bq)]
                qh = [qs_ref[h, pl.ds(qo, bq), :] for h in range(heads)]
                doh = [dos_ref[h, pl.ds(qo, bq), :] for h in range(heads)]
                s = [_dot(kblk, qh[h], NT) for h in range(heads)]
                dp = [_dot(vblk, doh[h], NT) for h in range(heads)]
                p = [jnp.exp(jnp.where(same, s[h] - lse_ref[0, h:h + 1, pl.ds(qo, bq)], MASKED)) for h in range(heads)]
                pb = [p[h].astype(jnp.bfloat16) for h in range(heads)]
                ds = [(p[h] * (dp[h] - delta_ref[h:h + 1, pl.ds(qo, bq)])).astype(jnp.bfloat16) for h in range(heads)]
                for h in range(heads):
                    hs = slice(h * hd, (h + 1) * hd)
                    dv = dv + _dot(pb[h], doh[h], NN)
                    dk = dk + _dot(ds[h], qh[h], NN)
                    dqt_ref[sb, hs, :] += _dot(kt_ref[kb, hs, :], ds[h], NN)
                return dk, dv

            zero = jnp.zeros((bk, pair), jnp.float32)
            dk, dv = lax.fori_loop(lo_ref[gk], hi_ref[gk], inner, (zero, zero))
            dk_ref[pl.ds(ks, bk), :] = dk.astype(jnp.bfloat16)
            dv_ref[pl.ds(ks, bk), :] = dv.astype(jnp.bfloat16)
            return 0

        lax.fori_loop(0, nblk, outer, 0)
        for j in range(nblk * bk // bq):
            out_ref[j * bq:(j + 1) * bq, :] = dqt_ref[j].T.astype(out_ref.dtype)

    @pl.when(w == 1)
    def _():
        out_ref[...] = dk_ref[...]

    @pl.when(w == 2)
    def _():
        out_ref[...] = dv_ref[...]

def pair_block(which, pair, group):
    return (pair // group) * 3 * group + which * group + pair % group


def attn_fwd(qkv, seg_k, seg_q, low, high, shift, pair, pairs, group, head_size, bq, bk):
    rows, wide = qkv.shape[0], 2 * head_size
    blocks = rows // bk
    spec = lambda which: pair_block(which, pair, group)
    return pl.pallas_call(
        functools.partial(attn_fwd_kernel, bq=bq, bk=bk, hd=head_size, scale=float(head_size) ** -0.5, nblk=blocks),
        out_shape=(
            jax.ShapeDtypeStruct((rows, wide), BF),
            jax.ShapeDtypeStruct((1, 2, rows), F32),
        ),
        grid_spec=pltpu.PrefetchScalarGridSpec(
            num_scalar_prefetch=3,
            grid=(rows // bq,),
            in_specs=[
                pl.BlockSpec((bq, wide), lambda i, *_: (i, spec(0))),
                pl.BlockSpec((rows, wide), lambda i, *_: (0, spec(1))),
                pl.BlockSpec((rows, wide), lambda i, *_: (0, spec(2))),
                pl.BlockSpec((rows, 128), lambda i, *_: (0, 0)),
                pl.BlockSpec((8, bq), lambda i, *_: (0, i)),
            ],
            out_specs=(
                pl.BlockSpec((bq, wide), lambda i, *_: (i, 0)),
                pl.BlockSpec((1, 2, bq), lambda i, *_: (0, 0, i)),
            ),
            scratch_shapes=[pltpu.VMEM((blocks, wide, bk), BF)],
        ),
        compiler_params=pltpu.CompilerParams(vmem_limit_bytes=24 << 20),
        cost_estimate=pl.CostEstimate(
            flops=15_000_000_000, bytes_accessed=rows * wide * 8, transcendentals=rows * rows // 2
        ),
        name="attn_fwd",
    )(low, high, shift, qkv, qkv, qkv, seg_k, seg_q)


def attn_bwd(before, qkv, mixed, dctx, lse, seg_k, seg_q, low, high, shift, pair, pairs, group, head_size, bq, bk):
    rows, wide = qkv.shape[0], 2 * head_size
    blocks = rows // bk
    column = lambda which: pl.BlockSpec((rows, wide), lambda w, *_: (0, pair_block(which, pair, group)))
    in_specs = [
        column(0),
        column(1),
        column(2),
        pl.BlockSpec((rows, wide), lambda w, *_: (0, 0)),
        pl.BlockSpec((rows, wide), lambda w, *_: (0, pair)),
        pl.BlockSpec((1, 2, rows), lambda w, *_: (0, 0, 0)),
        pl.BlockSpec((rows, 128), lambda w, *_: (0, 0)),
        pl.BlockSpec((8, rows), lambda w, *_: (0, 0)),
    ]
    operands = [low, high, shift, qkv, qkv, qkv, mixed, dctx, lse, seg_k, seg_q]
    aliases = {}
    kernel = functools.partial(
        attn_bwd_kernel, bq=bq, bk=bk, hd=head_size, scale=float(head_size) ** -0.5, nblk=blocks
    )
    body = kernel
    if before is not None:
        aliases = {len(operands): 0}
        in_specs.append(pl.BlockSpec(memory_space=pl.ANY))
        operands.append(before)

        def body(*refs):
            kernel(*refs[:11], *refs[12:])

    return pl.pallas_call(
        body,
        out_shape=jax.ShapeDtypeStruct(qkv.shape, BF),
        grid_spec=pltpu.PrefetchScalarGridSpec(
            num_scalar_prefetch=3,
            grid=(3,),
            in_specs=in_specs,
            out_specs=pl.BlockSpec((rows, wide), lambda w, *_: (0, (pair // group) * 3 * group + w * group + pair % group)),
            scratch_shapes=[
                pltpu.VMEM((2, rows, wide), BF),
                pltpu.VMEM((2, rows, wide), BF),
                pltpu.VMEM((blocks, wide, bk), BF),
                pltpu.VMEM((8, rows), F32),
                pltpu.VMEM((rows // bq, wide, bq), F32),
                pltpu.VMEM((rows, wide), BF),
                pltpu.VMEM((rows, wide), BF),
            ],
        ),
        input_output_aliases=aliases,
        compiler_params=pltpu.CompilerParams(vmem_limit_bytes=32 << 20),
        cost_estimate=pl.CostEstimate(
            flops=25_000_000_000, bytes_accessed=rows * wide * 16, transcendentals=rows * rows // 2
        ),
        name="attn_bwd",
    )(*operands)


def assemble_kernel(*refs, per, place):
    stacks = len(refs) - 4
    out, buf, in_sem, out_sem = refs[stacks:]
    count = stacks * per
    blocks = [refs[i // per].at[i % per] for i in range(count)]
    for i in range(count):
        pltpu.make_async_copy(blocks[i], buf.at[i], in_sem.at[i]).start()
    outs = []
    for i in range(count):
        pltpu.make_async_copy(blocks[i], buf.at[i], in_sem.at[i]).wait()
        outs.append(pltpu.make_async_copy(buf.at[i], place(out, i), out_sem.at[i]))
        outs[-1].start()
    for one in outs:
        one.wait()


def assemble(stacks, shape, place):
    per = stacks[0].shape[0]
    count = per * len(stacks)
    return pl.pallas_call(
        functools.partial(assemble_kernel, per=per, place=place),
        out_shape=jax.ShapeDtypeStruct(shape, stacks[0].dtype),
        in_specs=[pl.BlockSpec(memory_space=pl.ANY)] * len(stacks),
        out_specs=pl.BlockSpec(memory_space=pl.ANY),
        scratch_shapes=[
            pltpu.VMEM((count,) + stacks[0].shape[1:], stacks[0].dtype),
            pltpu.SemaphoreType.DMA((count,)),
            pltpu.SemaphoreType.DMA((count,)),
        ],
        compiler_params=pltpu.CompilerParams(vmem_limit_bytes=32 << 20),
        cost_estimate=pl.CostEstimate(flops=0, bytes_accessed=2 * 2 * shape[0] * shape[1], transcendentals=0),
        name="assemble",
    )(*stacks)


def segment_bounds(seg_rows, row_block, col_block):
    blocks = seg_rows.reshape(-1, row_block)
    low = jnp.sum(seg_rows[None, :] < blocks[:, :1], axis=1) // col_block
    high = (jnp.sum(seg_rows[None, :] <= blocks[:, -1:], axis=1) + col_block - 1) // col_block
    return low.astype(jnp.int32), high.astype(jnp.int32)


def norm_forward(rows):
    mean = jnp.mean(rows, axis=-1, keepdims=True)
    centred = rows - mean
    inv = lax.rsqrt(jnp.mean(centred * centred, axis=-1, keepdims=True) + NORM_EPS)
    return centred * inv, inv


def norm_backward(grad, normed, inv):
    return inv * (
        grad
        - jnp.mean(grad, axis=-1, keepdims=True)
        - normed * jnp.mean(grad * normed, axis=-1, keepdims=True)
    )


def after(value, *others):
    return lax.optimization_barrier((value,) + others)[0]


def mm(a, b):
    return jnp.dot(a, b, preferred_element_type=F32)


def mm_nt(a, b):
    return lax.dot_general(a, b, (((1,), (1,)), ((), ())), preferred_element_type=F32)


def mm_tn(a, b):
    return lax.dot_general(a, b, (((0,), (0,)), ((), ())), preferred_element_type=F32)


def on_device_rows(
    sizes,
    tokens,
    segment_ids,
    qkv_weight,
    qv_bias,
    proj_weight,
    proj_bias,
    first_gain,
    first_shift,
    up_weight,
    up_bias,
    down_weight,
    down_bias,
    second_gain,
    second_shift,
    out_grad,
):
    nf, nc, nt = sizes
    nz = nf // 2
    zbits = nz.bit_length() - 1
    z, k, c, t = (lax.axis_index(name) for name in AXES)
    f = z * 2 + k

    def send(value, target):
        pairs = []
        for fi in range(nf):
            for ci in range(nc):
                for ti in range(nt):
                    to = target(fi // 2, fi % 2, ci, ti)
                    if to is not None:
                        zo, ko, co, tto = to
                        pairs.append(((fi * nc + ci) * nt + ti, ((zo * 2 + ko) * nc + co) * nt + tto))
        return lax.ppermute(value, AXES, pairs)

    def over_x(v):
        return send(v, lambda zi, ki, ci, ti: (zi, ki, 1 - ci, ti))

    def over_y(v):
        return send(v, lambda zi, ki, ci, ti: (zi, ki, ci, 1 - ti))

    def over_core(v):
        return send(v, lambda zi, ki, ci, ti: (zi, 1 - ki, ci, ti))

    def over_z(v):
        return send(v, lambda zi, ki, ci, ti: ((zi + 1) % nz, ki, ci, ti))

    def over_zbit(v, bit):
        return send(v, lambda zi, ki, ci, ti: (zi ^ (1 << bit), ki, ci, ti))

    def z_all(v):
        return [v] + [
            send(v, lambda zi, ki, ci, ti, d=d: ((zi + d) % nz, ki, ci, ti)) for d in range(1, nz)
        ]

    def z_ring(v):
        out = [v]
        for _ in range(nz - 1):
            out.append(over_z(out[-1]))
        return out

    def ordered(index, own, other, axis=0):
        return jnp.where(index == 0, jnp.concatenate([own, other], axis), jnp.concatenate([other, own], axis))

    seq_count, span, width = tokens.shape
    heads = qv_bias.shape[1]
    head_size = qv_bias.shape[2] * nf
    cols = heads * head_size
    hidden = up_weight.shape[1] * nt
    dblk = width // nf

    pairs = heads // 2
    group = max(1, pairs // 2)
    wide = 2 * head_size

    pieces = [qv_bias, up_bias, proj_bias, first_gain, first_shift, down_bias, second_gain, second_shift]
    small = jnp.concatenate([p.reshape(-1, 128) for p in pieces])
    up_at, vec_at = qv_bias.size // 128, (qv_bias.size + up_bias.size) // 128
    small = jnp.pad(small, ((0, -small.shape[0] % 16), (0, 0)))
    small = lax.all_gather(small, AXES[:2] + AXES[3:])
    small = small.reshape(nf, nt, -1, 128)

    own_rows = jnp.where(t == 0, tokens[0], tokens[1])
    own_seg = jnp.where(t == 0, segment_ids[0], segment_ids[1])
    other_rows = over_x(own_rows)
    other_seg = over_x(own_seg)
    columns = []
    for first in range(0, pairs, group):
        for which in range(3):
            columns.append(qkv_weight[which][:, first * wide : (first + group) * wide])
    qkv_shard = jnp.concatenate(columns, axis=1)
    swapped = send(qkv_shard, lambda zi, ki, ci, ti: (zi, ki, ci, 1 - ti) if ti == ci else None)
    qkv_shard = jnp.where(t == c, qkv_shard, swapped)
    qkv_near = z_all(qkv_shard)
    qkv_blocks = qkv_near + [over_core(b) for b in qkv_near]

    def place_rows(out, i):
        kk, d = i // nz, i % nz
        src = lax.rem(lax.axis_index("z") + nz - d, nz) * 2 + lax.rem(lax.axis_index("core") + kk, 2)
        return out.at[pl.ds(pl.multiple_of(src * dblk, dblk), dblk), :]

    qkv_full = assemble([b[None] for b in qkv_blocks], (width, 3 * cols), place_rows)

    edge = head_size // nf

    def interleave(rows, columns):
        col = lax.broadcasted_iota(jnp.int32, (rows.shape[1], columns), 1)
        source = lax.broadcasted_iota(jnp.int32, (rows.shape[1], columns), 0)
        spread_out = mm(rows, (source == col // head_size * edge + col % edge).astype(BF))
        col = lax.broadcasted_iota(jnp.int32, (nf, columns), 1)
        mine = col % head_size // edge == lax.broadcasted_iota(jnp.int32, (nf, columns), 0)
        return jnp.sum(jnp.where(mine, spread_out, 0.0), axis=0)

    qv_rows = jnp.where(c == 0, small[:, 0, :up_at], small[:, 1, :up_at]).reshape(nf, -1)
    per_kind = qv_rows.shape[1] // 2
    qv_all = [interleave(qv_rows[:, i * per_kind : (i + 1) * per_kind], cols) for i in range(2)]
    up_add = jnp.concatenate(
        [interleave(small[:, i, up_at:vec_at].reshape(nf, -1), hidden // nt) for i in range(nt)]
    )
    proj_add, gain_one, shift_one, down_add, gain_two, shift_two = (
        small[:, 0, vec_at + i].reshape(width).astype(F32) for i in range(6)
    )
    add_parts = [qv_all[0], jnp.zeros_like(qv_all[0]), qv_all[1]]
    qkv_add = jnp.concatenate(
        [add_parts[w][i * wide : (i + group) * wide] for i in range(0, pairs, group) for w in range(3)]
    )

    def place_grid(rows_by_f, rows, columns):
        def place(out, i):
            kk, zi, ti = i // (nz * nt), i // nt % nz, i % nt
            src = zi * 2 + lax.rem(lax.axis_index("core") + kk, 2)
            first, second = (src, ti) if rows_by_f else (ti, src)
            return out.at[
                pl.ds(pl.multiple_of(first * rows, rows), rows),
                pl.ds(pl.multiple_of(second * columns, columns), columns),
            ]

        return place

    def spread(shard):
        mine = lax.all_gather(shard, ("z", "tensor"))
        return mine, over_core(mine)

    def settle(halves, shape, place):
        return assemble(halves, shape, place)

    proj_all = spread(proj_weight)
    up_all = spread(up_weight)
    down_all = spread(down_weight)
    proj_full = settle(proj_all, (width, width), place_grid(False, *proj_weight.shape))
    up_full = settle(up_all, (width, hidden), place_grid(True, *up_weight.shape))
    down_full = settle(down_all, (hidden, width), place_grid(False, *down_weight.shape))

    rows_all = jnp.concatenate([own_rows, other_rows])
    seg_store = jnp.concatenate([own_seg, other_seg])
    seg_global = ordered(c, own_seg, other_seg)
    qkv = (mm(rows_all, qkv_full) + qkv_add).astype(BF)
    total = 2 * span
    blk = 256
    low, high = segment_bounds(seg_global, blk, blk)
    shift = jnp.reshape(c * (total // blk // 2), (1,)).astype(jnp.int32)
    seg_k = jnp.broadcast_to(seg_store[:, None], (total, 128))
    seg_q = jnp.broadcast_to(seg_store[None, :], (8, total))
    attn_args = (seg_k, seg_q, low, high, shift)
    mixed, lse, mixed_other = [], [], []
    for p in range(pairs):
        out, one = attn_fwd(qkv, *attn_args, p, pairs, group, head_size, blk, blk)
        mixed.append(out)
        lse.append(one)
        mixed_other.append(over_x(out[span:]))
    context_rows = ordered(
        c, jnp.concatenate([m[:span] for m in mixed], 1), jnp.concatenate(mixed_other, 1), 1
    )

    token_f32 = own_rows.astype(F32)
    n_one, inv_one = norm_forward(token_f32 + (mm(context_rows, proj_full) + proj_add))
    first = n_one * gain_one + shift_one
    first_low = first.astype(BF)
    hidden_pre = mm(first_low, up_full) + up_add
    act, gelu_pull = jax.vjp(exact_gelu, hidden_pre)
    act_low = act.astype(BF)
    n_two, inv_two = norm_forward(first + (mm(act_low, down_full) + down_add))
    out_low = (n_two * gain_two + shift_two).astype(BF)
    layer_output = ordered(t, out_low[None], over_y(out_low)[None])

    cot = jnp.where(t == 0, out_grad[0], out_grad[1]).astype(F32)
    grad_gain_two = jnp.sum(cot * n_two, axis=0)
    grad_shift_two = jnp.sum(cot, axis=0)
    grad_second = norm_backward(cot * gain_two, n_two, inv_two)
    branch_low = grad_second.astype(BF)
    grad_down_bias = jnp.sum(branch_low.astype(F32), axis=0)
    hidden_low = gelu_pull(mm_nt(branch_low, down_full))[0].astype(BF)
    grad_up_bias = jnp.sum(hidden_low.astype(F32), axis=0)
    grad_first = grad_second + mm_nt(hidden_low, up_full)
    grad_gain_one = jnp.sum(grad_first * n_one, axis=0)
    grad_shift_one = jnp.sum(grad_first, axis=0)
    grad_in = norm_backward(grad_first * gain_one, n_one, inv_one)
    attn_low = grad_in.astype(BF)
    grad_proj_bias = jnp.sum(attn_low.astype(F32), axis=0)
    grad_context = mm_nt(attn_low, proj_full).astype(BF)
    halves = grad_context[:, :cols], grad_context[:, cols:]
    dctx_own = jnp.where(c == 0, halves[0], halves[1])
    dctx_other = over_x(jnp.where(c == 0, halves[1], halves[0]))
    dctx = jnp.concatenate([dctx_own, dctx_other])

    zorder = sorted(range(nz), key=lambda zi: int(format(zi, "0%db" % zbits)[::-1], 2)) if zbits else [0]

    def pick_k(a, kk):
        even = jnp.concatenate([a[:, (2 * zi) * dblk : (2 * zi + 1) * dblk] for zi in zorder], axis=1)
        odd = jnp.concatenate([a[:, (2 * zi + 1) * dblk : (2 * zi + 2) * dblk] for zi in zorder], axis=1)
        return jnp.where(kk == 0, even, odd)

    def pick_plain(a, kk):
        even = jnp.concatenate([a[:, (2 * zi) * dblk : (2 * zi + 1) * dblk] for zi in range(nz)], axis=1)
        odd = jnp.concatenate([a[:, (2 * zi + 1) * dblk : (2 * zi + 2) * dblk] for zi in range(nz)], axis=1)
        return jnp.where(kk == 0, even, odd)

    def half(a, index, axis):
        size = a.shape[axis] // 2
        return lax.dynamic_slice_in_dim(a, index * size, size, axis)

    def halve(a, index, axis, across):
        got = across(half(a, 1 - index, axis))
        return (half(a, index, axis).astype(F32) + got.astype(F32)).astype(BF)

    def z_halve(a, axis):
        for bit in range(zbits):
            a = halve(a, (z >> bit) & 1, axis, functools.partial(over_zbit, bit=bit))
        return a

    def tensor_sum(left, right):
        out = []
        for kk in (1 - k, k):
            mine = pick_plain(left, kk)
            size = right.shape[1] // nt
            out.append([mm_tn(mine, right[:, i * size : (i + 1) * size]) for i in range(nt)])
        got = over_core(jnp.concatenate(out[0]).astype(BF))
        return (jnp.concatenate(out[1]) + got.astype(F32)).astype(BF)

    down_sum = tensor_sum(branch_low, act_low)
    up_sum = tensor_sum(first_low, hidden_low)
    proj_sum = tensor_sum(attn_low, context_rows)
    dctx, down_sum, up_sum, proj_sum = lax.optimization_barrier((dctx, down_sum, up_sum, proj_sum))
    widths = [p.shape[1] for p in (down_sum, up_sum, proj_sum)]
    packed = jnp.concatenate([down_sum, up_sum, proj_sum], axis=1)
    gather = lax.psum_scatter(packed, ("tensor", "z", "context"), scatter_dimension=0, tiled=True)
    gather = ordered(c, gather, over_x(gather), 0).astype(F32)
    grad_down = gather[:, : widths[0]].T
    grad_up = gather[:, widths[0] : widths[0] + widths[1]]
    grad_proj = gather[:, widths[0] + widths[1] :].T

    def total_sum(v):
        v = v + over_core(v)
        for bit in range(zbits):
            v = v + over_zbit(v, bit)
        return v + over_y(v)

    vectors = [grad_proj_bias, grad_gain_one, grad_shift_one, grad_down_bias, grad_gain_two, grad_shift_two]
    sums = jnp.concatenate(vectors + [grad_up_bias]).reshape(-1, 128)
    sums = total_sum(sums)
    sums = (sums + over_x(sums)).reshape(-1)
    vector_out = [
        lax.dynamic_slice_in_dim(sums[i * width : (i + 1) * width], f * dblk, dblk) for i in range(6)
    ]
    up_rows, up_cols = up_bias.shape
    bias_up = sums[6 * width :].reshape(nt * up_rows, nf * up_cols)
    bias_up = lax.dynamic_slice(bias_up, (t * up_rows, f * up_cols), (up_rows, up_cols))

    def reduce_qkv(part):
        sent = mm_tn(pick_k(rows_all, 1 - k), part).astype(BF)
        kept = mm_tn(pick_k(rows_all, k), part)
        g = (kept + over_core(sent).astype(F32)).astype(BF)
        g = z_halve(g, 0)
        g = halve(g, t, 0, over_y)
        near = send(g, lambda zi, ki, ci, ti: (zi, ki, 1 - ci, ci) if ci == ti else (zi, ki, ci, ci))
        far = send(g, lambda zi, ki, ci, ti: (zi, ki, 1 - ci, ci) if ci != ti else None)
        return jnp.where(
            c == t,
            jnp.where(t == 0, jnp.concatenate([g, near]), jnp.concatenate([near, g])),
            jnp.where(t == 0, jnp.concatenate([near, far]), jnp.concatenate([far, near])),
        )

    dqkv, qkv_parts = None, []
    for p in range(pairs):
        dqkv = attn_bwd(dqkv, qkv, mixed[p], dctx, lse[p], *attn_args, p, pairs, group, head_size, blk, blk)
        if (p + 1) % group == 0 and p + 1 < pairs:
            lo_col = (p + 1 - group) * 3 * wide
            part = reduce_qkv(dqkv[:, lo_col : lo_col + 3 * group * wide])
            qkv_parts.append(part)
    chunks = 4
    step = span // chunks
    away = mm_nt(dqkv[span:], qkv_full).astype(BF)
    got = [over_x(away[i * step : (i + 1) * step]) for i in range(chunks)]
    stay = mm_nt(dqkv[:span], qkv_full) + grad_in
    final = [
        (stay[i * step : (i + 1) * step] + got[i].astype(F32)).astype(BF) for i in range(chunks)
    ]
    final_other = [over_y(part) for part in final]
    tokens_grad = ordered(t, jnp.concatenate(final)[None], jnp.concatenate(final_other)[None])
    qkv_parts.append(reduce_qkv(dqkv[:, (pairs - group) * 3 * wide :]))
    qkv_rows = jnp.concatenate(qkv_parts, axis=1)

    def unpack(rows, which):
        return jnp.concatenate(
            [rows[..., (3 * i + which * group) * wide :][..., : group * wide] for i in range(0, pairs, group)],
            axis=-1,
        )

    grad_qkv = jnp.stack([unpack(qkv_rows, which) for which in range(3)]).astype(F32)
    qv_sum = jnp.sum(dqkv.astype(F32), axis=0)
    qv_sum = total_sum(jnp.concatenate([unpack(qv_sum, 0), unpack(qv_sum, 2)]).reshape(-1, 128))
    qv_sum = jnp.where(t == c, qv_sum, over_x(qv_sum)).reshape(2, heads, head_size)
    grad_qv = lax.dynamic_slice_in_dim(qv_sum, f * (head_size // nf), head_size // nf, 2)

    return (
        layer_output,
        tokens_grad,
        grad_qkv,
        grad_qv,
        grad_proj,
        vector_out[0],
        vector_out[1],
        vector_out[2],
        grad_up,
        bias_up,
        grad_down,
        vector_out[3],
        vector_out[4],
        vector_out[5],
    )


def solution(mesh):
    sizes = tuple(mesh.shape[name] for name in ("fsdp", "context", "tensor"))
    nf, nc, nt = sizes
    shards = (
        P("fsdp", "context", None),
        P("fsdp", "context"),
        P(None, "fsdp", "tensor"),
        P(None, "tensor", "fsdp"),
        P("tensor", "fsdp"),
        P("fsdp"),
        P("fsdp"),
        P("fsdp"),
        P("fsdp", "tensor"),
        P("tensor", "fsdp"),
        P("tensor", "fsdp"),
        P("fsdp"),
        P("fsdp"),
        P("fsdp"),
    )
    in_specs = (shards[0],) + shards[1:] + (shards[0],)
    out_specs = (shards[0], shards[0]) + shards[2:]
    nz = nf // 2
    by_rows = nc == nt == 2 and nf % 2 == 0 and nz & (nz - 1) == 0
    rows_mesh = jax.sharding.Mesh(mesh.devices.reshape(nz, 2, nc, nt), AXES) if by_rows else None

    def finer(spec):
        return P(*(("z", "core") if name == "fsdp" else name for name in spec))

    def program(*args):
        if by_rows and args[0].shape[0] // nf == nt:
            return jax.shard_map(
                functools.partial(on_device_rows, sizes),
                mesh=rows_mesh,
                in_specs=tuple(finer(spec) for spec in in_specs),
                out_specs=tuple(finer(spec) for spec in out_specs),
                check_vma=False,
            )(*args)
        return jax.shard_map(
            on_device_general, mesh=mesh, in_specs=in_specs, out_specs=out_specs, check_vma=False
        )(*args)

    return program
```

```python
import functools

import jax
import jax.numpy as jnp
from jax import lax
from jax.experimental import pallas as pl
from jax.experimental.pallas import tpu as pltpu
from jax.sharding import PartitionSpec as P

NORM_EPS = 1e-05


def layer_norm(hidden_rows, norm_gain, norm_shift):
    row_mean = jnp.mean(hidden_rows, axis=-1, keepdims=True)
    centred = hidden_rows - row_mean
    variance = jnp.mean(centred * centred, axis=-1, keepdims=True)
    return centred * lax.rsqrt(variance + NORM_EPS) * norm_gain + norm_shift


def exact_gelu(values):
    return jax.nn.gelu(values, approximate=False)


def masked_logits(query_heads, key_heads, seg_query, seg_key, score_scale):
    logits = (
        jnp.einsum("qhe,khe->hqk", query_heads, key_heads, preferred_element_type=jnp.float32)
        * score_scale
    )
    same_doc = (seg_query[:, None] == seg_key[None, :])[None, :, :]
    return jnp.where(same_doc, logits, -1e30)


def on_device_general(
    tokens,
    segment_ids,
    qkv_weight,
    qv_bias,
    proj_weight,
    proj_bias,
    first_gain,
    first_shift,
    up_weight,
    up_bias,
    down_weight,
    down_bias,
    second_gain,
    second_shift,
    out_grad,
):
    seq_count, span, width = tokens.shape
    total_rows = seq_count * span
    share = total_rows // lax.axis_size("tensor")
    row_start = lax.axis_index("tensor") * share
    token_rows = tokens.reshape(total_rows, width)
    gathered = (
        lax.all_gather(qkv_weight, "fsdp", axis=1, tiled=True),
        lax.all_gather(qv_bias, "fsdp", axis=2, tiled=True),
        lax.all_gather(proj_weight, "fsdp", axis=1, tiled=True),
        lax.all_gather(proj_bias, "fsdp", axis=0, tiled=True),
        lax.all_gather(first_gain, "fsdp", axis=0, tiled=True),
        lax.all_gather(first_shift, "fsdp", axis=0, tiled=True),
        lax.all_gather(up_weight, "fsdp", axis=0, tiled=True),
        lax.all_gather(up_bias, "fsdp", axis=1, tiled=True),
        lax.all_gather(down_weight, "fsdp", axis=1, tiled=True),
        lax.all_gather(down_bias, "fsdp", axis=0, tiled=True),
        lax.all_gather(second_gain, "fsdp", axis=0, tiled=True),
        lax.all_gather(second_shift, "fsdp", axis=0, tiled=True),
    )
    qkv_full, qv_full, proj_full, proj_add, gain_one, shift_one = (
        gathered[0],
        gathered[1],
        gathered[2],
        gathered[3],
        gathered[4],
        gathered[5],
    )
    up_full, up_add, down_full, down_add, gain_two, shift_two = (
        gathered[6],
        gathered[7],
        gathered[8],
        gathered[9],
        gathered[10],
        gathered[11],
    )
    local_width = qkv_full.shape[2]
    head_count = qv_full.shape[1]
    head_size = qv_full.shape[2]
    score_scale = float(head_size) ** (-0.5)
    projected = jnp.einsum("rd,cde->cre", token_rows, qkv_full, preferred_element_type=jnp.float32)
    bias_rows = qv_full.reshape(2, local_width).astype(jnp.float32)
    head_shape = (seq_count, span, head_count, head_size)
    query_heads = (projected[0] + bias_rows[0]).astype(jnp.bfloat16).reshape(head_shape)
    key_heads = projected[1].astype(jnp.bfloat16).reshape(head_shape)
    value_heads = (projected[2] + bias_rows[1]).astype(jnp.bfloat16).reshape(head_shape)
    key_all, value_all, seg_all = (
        lax.all_gather(key_heads, "context", axis=1, tiled=True),
        lax.all_gather(value_heads, "context", axis=1, tiled=True),
        lax.all_gather(segment_ids, "context", axis=1, tiled=True),
    )

    def attend_forward(pieces):
        query_one, key_one, value_one, seg_query, seg_key = pieces
        logits = masked_logits(query_one, key_one, seg_query, seg_key, score_scale)
        row_top = jnp.max(logits, axis=-1, keepdims=True)
        weights = jnp.exp(logits - row_top)
        row_total = jnp.sum(weights, axis=-1, keepdims=True)
        soft_low = (weights / row_total).astype(jnp.bfloat16)
        mixed_one = jnp.einsum(
            "hqk,khe->qhe", soft_low, value_one, preferred_element_type=jnp.float32
        )
        return (mixed_one.astype(jnp.bfloat16), row_top + jnp.log(row_total))

    mixed, log_totals = lax.map(
        attend_forward, (query_heads, key_all, value_all, segment_ids, seg_all)
    )
    context_low = mixed.reshape(total_rows, local_width)
    attn_part = jnp.dot(context_low, proj_full, preferred_element_type=jnp.float32)
    attn_share = lax.psum_scatter(
        attn_part, "tensor", scatter_dimension=0, tiled=True
    ) + proj_add.astype(jnp.float32)
    token_share = lax.dynamic_slice_in_dim(token_rows, row_start, share, 0).astype(jnp.float32)
    first_share, first_pull = jax.vjp(
        layer_norm,
        token_share + attn_share,
        gain_one.astype(jnp.float32),
        shift_one.astype(jnp.float32),
    )
    first_low = lax.all_gather(first_share.astype(jnp.bfloat16), "tensor", axis=0, tiled=True)
    hidden_pre = jnp.dot(first_low, up_full, preferred_element_type=jnp.float32) + up_add.reshape(
        -1
    ).astype(jnp.float32)
    activation, gelu_pull = jax.vjp(exact_gelu, hidden_pre)
    act_low = activation.astype(jnp.bfloat16)
    down_part = jnp.dot(act_low, down_full, preferred_element_type=jnp.float32)
    branch_share = lax.psum_scatter(
        down_part, "tensor", scatter_dimension=0, tiled=True
    ) + down_add.astype(jnp.float32)
    output_share, second_pull = jax.vjp(
        layer_norm,
        first_share + branch_share,
        gain_two.astype(jnp.float32),
        shift_two.astype(jnp.float32),
    )
    qkv_back, proj_back, up_back, down_back = (
        lax.all_gather(qkv_weight, "fsdp", axis=1, tiled=True),
        lax.all_gather(proj_weight, "fsdp", axis=1, tiled=True),
        lax.all_gather(up_weight, "fsdp", axis=0, tiled=True),
        lax.all_gather(down_weight, "fsdp", axis=1, tiled=True),
    )
    cot_share = lax.dynamic_slice_in_dim(
        out_grad.reshape(total_rows, width), row_start, share, 0
    ).astype(jnp.float32)
    grad_second, gain_two_part, shift_two_part = second_pull(cot_share)
    branch_low = lax.all_gather(grad_second.astype(jnp.bfloat16), "tensor", axis=0, tiled=True)
    grad_down_bias = jnp.sum(branch_low.astype(jnp.float32), axis=0)
    grad_down = jnp.einsum("rf,rd->fd", act_low, branch_low, preferred_element_type=jnp.float32)
    grad_act = jnp.einsum("rd,fd->rf", branch_low, down_back, preferred_element_type=jnp.float32)
    hidden_low = gelu_pull(grad_act)[0].astype(jnp.bfloat16)
    grad_up_bias = jnp.sum(hidden_low.astype(jnp.float32), axis=0).reshape(up_add.shape)
    grad_up = jnp.einsum("rd,rf->df", first_low, hidden_low, preferred_element_type=jnp.float32)
    norm_part = jnp.einsum("rf,df->rd", hidden_low, up_back, preferred_element_type=jnp.float32)
    grad_first = grad_second + lax.psum_scatter(
        norm_part, "tensor", scatter_dimension=0, tiled=True
    )
    grad_in_one, gain_one_part, shift_one_part = first_pull(grad_first)
    attn_low = lax.all_gather(grad_in_one.astype(jnp.bfloat16), "tensor", axis=0, tiled=True)
    grad_proj_bias = jnp.sum(attn_low.astype(jnp.float32), axis=0)
    grad_proj = jnp.einsum("rl,rd->ld", context_low, attn_low, preferred_element_type=jnp.float32)
    grad_context = (
        jnp.einsum("rd,ld->rl", attn_low, proj_back, preferred_element_type=jnp.float32)
        .astype(jnp.bfloat16)
        .reshape(head_shape)
    )

    def attend_backward(pieces):
        query_one, key_one, value_one, seg_query, seg_key, log_total, context_grad = pieces
        logits = masked_logits(query_one, key_one, seg_query, seg_key, score_scale)
        soft_again = jnp.exp(logits - log_total)
        grad_soft = jnp.einsum(
            "qhe,khe->hqk", context_grad, value_one, preferred_element_type=jnp.float32
        )
        row_delta = jnp.sum(grad_soft * soft_again, axis=-1, keepdims=True)
        grad_logits = (soft_again * (grad_soft - row_delta)).astype(jnp.bfloat16)
        query_grad = (
            jnp.einsum("hqk,khe->qhe", grad_logits, key_one, preferred_element_type=jnp.float32)
            * score_scale
        ).astype(jnp.bfloat16)
        key_part = (
            jnp.einsum("hqk,qhe->khe", grad_logits, query_one, preferred_element_type=jnp.float32)
            * score_scale
        )
        value_part = jnp.einsum(
            "hqk,qhe->khe",
            soft_again.astype(jnp.bfloat16),
            context_grad,
            preferred_element_type=jnp.float32,
        )
        return (query_grad, key_part, value_part)

    grad_query, key_terms, value_terms = lax.map(
        attend_backward,
        (query_heads, key_all, value_all, segment_ids, seg_all, log_totals, grad_context),
    )
    key_grad, value_grad = (
        lax.psum_scatter(
            key_terms.astype(jnp.bfloat16), "context", scatter_dimension=1, tiled=True
        ).astype(jnp.float32),
        lax.psum_scatter(
            value_terms.astype(jnp.bfloat16), "context", scatter_dimension=1, tiled=True
        ).astype(jnp.float32),
    )
    grad_stack = jnp.stack(
        [
            grad_query.reshape(total_rows, local_width),
            key_grad.astype(jnp.bfloat16).reshape(total_rows, local_width),
            value_grad.astype(jnp.bfloat16).reshape(total_rows, local_width),
        ]
    )
    stack_sums = jnp.sum(grad_stack.astype(jnp.float32), axis=1)
    grad_qv_bias = jnp.stack([stack_sums[0], stack_sums[2]]).reshape(qv_full.shape)
    grad_qkv = jnp.einsum("rd,cre->cde", token_rows, grad_stack, preferred_element_type=jnp.float32)
    input_part = jnp.einsum("cre,cde->rd", grad_stack, qkv_back, preferred_element_type=jnp.float32)
    norm_parts = jnp.tile(
        jnp.stack([gain_one_part, shift_one_part, gain_two_part, shift_two_part]),
        (lax.axis_size("tensor"), 1),
    )
    input_share, norm_sums = (
        lax.psum_scatter(
            input_part.astype(jnp.bfloat16), "tensor", scatter_dimension=0, tiled=True
        ).astype(jnp.float32),
        lax.psum_scatter(
            norm_parts.astype(jnp.bfloat16), "tensor", scatter_dimension=0, tiled=True
        ).astype(jnp.float32),
    )
    grad_share_low = (grad_in_one + input_share).astype(jnp.bfloat16)
    out_rows, grad_rows = (
        lax.all_gather(output_share.astype(jnp.bfloat16), "tensor", axis=0, tiled=True),
        lax.all_gather(grad_share_low, "tensor", axis=0, tiled=True),
    )
    local_grads = (
        grad_qkv,
        grad_qv_bias,
        grad_proj,
        grad_proj_bias,
        norm_sums[0],
        norm_sums[1],
        grad_up,
        grad_up_bias,
        grad_down,
        grad_down_bias,
        norm_sums[2],
        norm_sums[3],
    )
    summed = (
        lax.psum(local_grads[0].astype(jnp.bfloat16), "context").astype(jnp.float32),
        lax.psum(local_grads[1].astype(jnp.bfloat16), "context").astype(jnp.float32),
        lax.psum(local_grads[2].astype(jnp.bfloat16), "context").astype(jnp.float32),
        lax.psum(local_grads[3].astype(jnp.bfloat16), "context").astype(jnp.float32),
        lax.psum(local_grads[4].astype(jnp.bfloat16), "context").astype(jnp.float32),
        lax.psum(local_grads[5].astype(jnp.bfloat16), "context").astype(jnp.float32),
        lax.psum(local_grads[6].astype(jnp.bfloat16), "context").astype(jnp.float32),
        lax.psum(local_grads[7].astype(jnp.bfloat16), "context").astype(jnp.float32),
        lax.psum(local_grads[8].astype(jnp.bfloat16), "context").astype(jnp.float32),
        lax.psum(local_grads[9].astype(jnp.bfloat16), "context").astype(jnp.float32),
        lax.psum(local_grads[10].astype(jnp.bfloat16), "context").astype(jnp.float32),
        lax.psum(local_grads[11].astype(jnp.bfloat16), "context").astype(jnp.float32),
    )
    owned = (
        lax.psum_scatter(
            summed[0].astype(jnp.bfloat16), "fsdp", scatter_dimension=1, tiled=True
        ).astype(jnp.float32),
        lax.psum_scatter(
            summed[1].astype(jnp.bfloat16), "fsdp", scatter_dimension=2, tiled=True
        ).astype(jnp.float32),
        lax.psum_scatter(
            summed[2].astype(jnp.bfloat16), "fsdp", scatter_dimension=1, tiled=True
        ).astype(jnp.float32),
        lax.psum_scatter(
            summed[3].astype(jnp.bfloat16), "fsdp", scatter_dimension=0, tiled=True
        ).astype(jnp.float32),
        lax.psum_scatter(
            summed[4].astype(jnp.bfloat16), "fsdp", scatter_dimension=0, tiled=True
        ).astype(jnp.float32),
        lax.psum_scatter(
            summed[5].astype(jnp.bfloat16), "fsdp", scatter_dimension=0, tiled=True
        ).astype(jnp.float32),
        lax.psum_scatter(
            summed[6].astype(jnp.bfloat16), "fsdp", scatter_dimension=0, tiled=True
        ).astype(jnp.float32),
        lax.psum_scatter(
            summed[7].astype(jnp.bfloat16), "fsdp", scatter_dimension=1, tiled=True
        ).astype(jnp.float32),
        lax.psum_scatter(
            summed[8].astype(jnp.bfloat16), "fsdp", scatter_dimension=1, tiled=True
        ).astype(jnp.float32),
        lax.psum_scatter(
            summed[9].astype(jnp.bfloat16), "fsdp", scatter_dimension=0, tiled=True
        ).astype(jnp.float32),
        lax.psum_scatter(
            summed[10].astype(jnp.bfloat16), "fsdp", scatter_dimension=0, tiled=True
        ).astype(jnp.float32),
        lax.psum_scatter(
            summed[11].astype(jnp.bfloat16), "fsdp", scatter_dimension=0, tiled=True
        ).astype(jnp.float32),
    )
    layer_output = out_rows.reshape(seq_count, span, width)
    tokens_grad = grad_rows.reshape(seq_count, span, width)
    return (
        layer_output,
        tokens_grad,
        owned[0],
        owned[1],
        owned[2],
        owned[3],
        owned[4],
        owned[5],
        owned[6],
        owned[7],
        owned[8],
        owned[9],
        owned[10],
        owned[11],
    )


AXES = ("z", "core", "context", "tensor")
BF = jnp.bfloat16
F32 = jnp.float32
SUB = 2
MASKED = -1e30
NT = (((1,), (1,)), ((), ()))
NN = (((1,), (0,)), ((), ()))

def _dot(a, b, dims):
    return lax.dot_general(a, b, dims, preferred_element_type=jnp.float32)

def attn_fwd_kernel(lo_ref, hi_ref, shift_ref, q_ref, k_ref, v_ref, segk_ref, segq_ref, o_ref, lse_ref, vt_ref, *, bq, bk, hd, scale, nblk):
    qb = pl.program_id(0)
    shift = shift_ref[0]
    pair = q_ref.shape[1]
    heads = pair // hd

    @pl.when(qb == 0)
    def _():
        for j in range(nblk):
            vt_ref[j] = v_ref[j * bk:(j + 1) * bk, :].T

    gq = lax.rem(qb + shift // (bq // bk), nblk * bk // bq)
    lane = lax.broadcasted_iota(jnp.int32, (bq, pair), 1) // hd
    q = q_ref[...] * jnp.asarray(scale, q_ref.dtype)
    qs = [jnp.where(lane == h, q, jnp.zeros_like(q)) for h in range(heads)]
    segq = segq_ref[0:1, :]

    def body(i, carry):
        j = lo_ref[gq] + i * SUB
        sbs = [lax.rem(j + u + shift, nblk) for u in range(SUB)]
        sc = [[None] * SUB for _ in range(heads)]
        for u in range(SUB):
            ks = pl.multiple_of(sbs[u] * bk, bk)
            kb = k_ref[pl.ds(ks, bk), :]
            same = segk_ref[pl.ds(ks, bk), :]
            same = jnp.concatenate([same] * (bq // same.shape[1]), axis=1) == segq
            for h in range(heads):
                sc[h][u] = jnp.where(same, _dot(kb, qs[h], NT), MASKED)
        out = []
        for h in range(heads):
            m, l, acc = carry[h]
            mn = m
            for u in range(SUB):
                mn = jnp.maximum(mn, jnp.max(sc[h][u], axis=0, keepdims=True))
            a = jnp.exp(m - mn)
            l = l * a
            acc = acc * a
            for u in range(SUB):
                p = jnp.exp(sc[h][u] - mn)
                l = l + jnp.sum(p, axis=0, keepdims=True)
                acc = acc + _dot(vt_ref[sbs[u], h * hd:(h + 1) * hd, :], p.astype(jnp.bfloat16), NN)
            out.append((mn, l, acc))
        return tuple(out)

    init = tuple((jnp.full((1, bq), MASKED, jnp.float32), jnp.zeros((1, bq), jnp.float32), jnp.zeros((hd, bq), jnp.float32)) for _ in range(heads))
    res = lax.fori_loop(0, (hi_ref[gq] - lo_ref[gq] + SUB - 1) // SUB, body, init)
    o_ref[...] = jnp.concatenate([acc / l for (m, l, acc) in res], axis=0).T.astype(o_ref.dtype)
    lse_ref[0] = jnp.concatenate([m + jnp.log(l) for (m, l, acc) in res], axis=0)

def attn_bwd_kernel(lo_ref, hi_ref, shift_ref, q_ref, k_ref, v_ref, o_ref, do_ref, lse_ref, segk_ref, segq_ref, out_ref,
                    qs_ref, dos_ref, kt_ref, delta_ref, dqt_ref, dk_ref, dv_ref, *, bq, bk, hd, scale, nblk):
    w = pl.program_id(0)
    shift = shift_ref[0]
    rows, pair = q_ref.shape
    heads = pair // hd

    @pl.when(w == 0)
    def _():
        lane = lax.broadcasted_iota(jnp.int32, (bk, pair), 1) // hd
        pick = (lax.broadcasted_iota(jnp.int32, (8, pair), 0) == lax.broadcasted_iota(jnp.int32, (8, pair), 1) // hd).astype(jnp.float32)
        sc = jnp.asarray(scale, q_ref.dtype)
        for j in range(nblk):
            r = slice(j * bk, (j + 1) * bk)
            q = q_ref[r, :] * sc
            do = do_ref[r, :]
            for h in range(heads):
                qs_ref[h, r, :] = jnp.where(lane == h, q, jnp.zeros_like(q))
                dos_ref[h, r, :] = jnp.where(lane == h, do, jnp.zeros_like(do))
            kt_ref[j] = (k_ref[r, :] * sc).T
            prod = do.astype(jnp.float32) * o_ref[r, :].astype(jnp.float32)
            delta_ref[:, r] = lax.dot_general(pick, prod, NT, preferred_element_type=jnp.float32, precision=lax.Precision.HIGHEST)


        dqt_ref[...] = jnp.zeros(dqt_ref.shape, jnp.float32)

        def outer(kb, _):
            gk = lax.rem(kb + shift, nblk)
            nq = nblk * bk // bq
            ks = pl.multiple_of(kb * bk, bk)
            kblk = k_ref[pl.ds(ks, bk), :]
            vblk = v_ref[pl.ds(ks, bk), :]
            segk = segk_ref[pl.ds(ks, bk), :]
            segk = jnp.concatenate([segk] * (bq // segk.shape[1]), axis=1)

            def inner(j, carry):
                dk, dv = carry
                sb = lax.rem(j + shift // (bq // bk) if bq >= bk else j + shift * (bk // bq), nq)
                qo = pl.multiple_of(sb * bq, bq)
                same = segk == segq_ref[0:1, pl.ds(qo, bq)]
                qh = [qs_ref[h, pl.ds(qo, bq), :] for h in range(heads)]
                doh = [dos_ref[h, pl.ds(qo, bq), :] for h in range(heads)]
                s = [_dot(kblk, qh[h], NT) for h in range(heads)]
                dp = [_dot(vblk, doh[h], NT) for h in range(heads)]
                p = [jnp.exp(jnp.where(same, s[h] - lse_ref[0, h:h + 1, pl.ds(qo, bq)], MASKED)) for h in range(heads)]
                pb = [p[h].astype(jnp.bfloat16) for h in range(heads)]
                ds = [(p[h] * (dp[h] - delta_ref[h:h + 1, pl.ds(qo, bq)])).astype(jnp.bfloat16) for h in range(heads)]
                for h in range(heads):
                    hs = slice(h * hd, (h + 1) * hd)
                    dv = dv + _dot(pb[h], doh[h], NN)
                    dk = dk + _dot(ds[h], qh[h], NN)
                    dqt_ref[sb, hs, :] += _dot(kt_ref[kb, hs, :], ds[h], NN)
                return dk, dv

            zero = jnp.zeros((bk, pair), jnp.float32)
            dk, dv = lax.fori_loop(lo_ref[gk], hi_ref[gk], inner, (zero, zero))
            dk_ref[pl.ds(ks, bk), :] = dk.astype(jnp.bfloat16)
            dv_ref[pl.ds(ks, bk), :] = dv.astype(jnp.bfloat16)
            return 0

        lax.fori_loop(0, nblk, outer, 0)
        for j in range(nblk * bk // bq):
            out_ref[j * bq:(j + 1) * bq, :] = dqt_ref[j].T.astype(out_ref.dtype)

    @pl.when(w == 1)
    def _():
        out_ref[...] = dk_ref[...]

    @pl.when(w == 2)
    def _():
        out_ref[...] = dv_ref[...]

def pair_block(which, pair, group):
    return (pair // group) * 3 * group + which * group + pair % group


def attn_fwd(qkv, seg_k, seg_q, low, high, shift, pair, pairs, group, head_size, bq, bk):
    rows, wide = qkv.shape[0], 2 * head_size
    blocks = rows // bk
    spec = lambda which: pair_block(which, pair, group)
    return pl.pallas_call(
        functools.partial(attn_fwd_kernel, bq=bq, bk=bk, hd=head_size, scale=float(head_size) ** -0.5, nblk=blocks),
        out_shape=(
            jax.ShapeDtypeStruct((rows, wide), BF),
            jax.ShapeDtypeStruct((1, 2, rows), F32),
        ),
        grid_spec=pltpu.PrefetchScalarGridSpec(
            num_scalar_prefetch=3,
            grid=(rows // bq,),
            in_specs=[
                pl.BlockSpec((bq, wide), lambda i, *_: (i, spec(0))),
                pl.BlockSpec((rows, wide), lambda i, *_: (0, spec(1))),
                pl.BlockSpec((rows, wide), lambda i, *_: (0, spec(2))),
                pl.BlockSpec((rows, 128), lambda i, *_: (0, 0)),
                pl.BlockSpec((8, bq), lambda i, *_: (0, i)),
            ],
            out_specs=(
                pl.BlockSpec((bq, wide), lambda i, *_: (i, 0)),
                pl.BlockSpec((1, 2, bq), lambda i, *_: (0, 0, i)),
            ),
            scratch_shapes=[pltpu.VMEM((blocks, wide, bk), BF)],
        ),
        compiler_params=pltpu.CompilerParams(vmem_limit_bytes=24 << 20),
        cost_estimate=pl.CostEstimate(
            flops=15_000_000_000, bytes_accessed=rows * wide * 8, transcendentals=rows * rows // 2
        ),
        name="attn_fwd",
    )(low, high, shift, qkv, qkv, qkv, seg_k, seg_q)


def attn_bwd(before, qkv, mixed, dctx, lse, seg_k, seg_q, low, high, shift, pair, pairs, group, head_size, bq, bk):
    rows, wide = qkv.shape[0], 2 * head_size
    blocks = rows // bk
    column = lambda which: pl.BlockSpec((rows, wide), lambda w, *_: (0, pair_block(which, pair, group)))
    in_specs = [
        column(0),
        column(1),
        column(2),
        pl.BlockSpec((rows, wide), lambda w, *_: (0, 0)),
        pl.BlockSpec((rows, wide), lambda w, *_: (0, pair)),
        pl.BlockSpec((1, 2, rows), lambda w, *_: (0, 0, 0)),
        pl.BlockSpec((rows, 128), lambda w, *_: (0, 0)),
        pl.BlockSpec((8, rows), lambda w, *_: (0, 0)),
    ]
    operands = [low, high, shift, qkv, qkv, qkv, mixed, dctx, lse, seg_k, seg_q]
    aliases = {}
    kernel = functools.partial(
        attn_bwd_kernel, bq=bq, bk=bk, hd=head_size, scale=float(head_size) ** -0.5, nblk=blocks
    )
    body = kernel
    if before is not None:
        aliases = {len(operands): 0}
        in_specs.append(pl.BlockSpec(memory_space=pl.ANY))
        operands.append(before)

        def body(*refs):
            kernel(*refs[:11], *refs[12:])

    return pl.pallas_call(
        body,
        out_shape=jax.ShapeDtypeStruct(qkv.shape, BF),
        grid_spec=pltpu.PrefetchScalarGridSpec(
            num_scalar_prefetch=3,
            grid=(3,),
            in_specs=in_specs,
            out_specs=pl.BlockSpec((rows, wide), lambda w, *_: (0, (pair // group) * 3 * group + w * group + pair % group)),
            scratch_shapes=[
                pltpu.VMEM((2, rows, wide), BF),
                pltpu.VMEM((2, rows, wide), BF),
                pltpu.VMEM((blocks, wide, bk), BF),
                pltpu.VMEM((8, rows), F32),
                pltpu.VMEM((rows // bq, wide, bq), F32),
                pltpu.VMEM((rows, wide), BF),
                pltpu.VMEM((rows, wide), BF),
            ],
        ),
        input_output_aliases=aliases,
        compiler_params=pltpu.CompilerParams(vmem_limit_bytes=32 << 20),
        cost_estimate=pl.CostEstimate(
            flops=25_000_000_000, bytes_accessed=rows * wide * 16, transcendentals=rows * rows // 2
        ),
        name="attn_bwd",
    )(*operands)


def segment_bounds(seg_rows, row_block, col_block):
    blocks = seg_rows.reshape(-1, row_block)
    low = jnp.sum(seg_rows[None, :] < blocks[:, :1], axis=1) // col_block
    high = (jnp.sum(seg_rows[None, :] <= blocks[:, -1:], axis=1) + col_block - 1) // col_block
    return low.astype(jnp.int32), high.astype(jnp.int32)


def norm_forward(rows):
    mean = jnp.mean(rows, axis=-1, keepdims=True)
    centred = rows - mean
    inv = lax.rsqrt(jnp.mean(centred * centred, axis=-1, keepdims=True) + NORM_EPS)
    return centred * inv, inv


def norm_backward(grad, normed, inv):
    return inv * (
        grad
        - jnp.mean(grad, axis=-1, keepdims=True)
        - normed * jnp.mean(grad * normed, axis=-1, keepdims=True)
    )


def after(value, *others):
    return lax.optimization_barrier((value,) + others)[0]


def mm(a, b):
    return jnp.dot(a, b, preferred_element_type=F32)


def mm_nt(a, b):
    return lax.dot_general(a, b, (((1,), (1,)), ((), ())), preferred_element_type=F32)


def mm_tn(a, b):
    return lax.dot_general(a, b, (((0,), (0,)), ((), ())), preferred_element_type=F32)


def remote(src, dst, send_sem, recv_sem, device):
    return pltpu.make_async_remote_copy(
        src_ref=src,
        dst_ref=dst,
        send_sem=send_sem,
        recv_sem=recv_sem,
        device_id=device,
        device_id_type=pl.DeviceIdType.MESH,
    )


def greet(devices):
    barrier = pltpu.get_barrier_semaphore()
    for device in devices:
        pl.semaphore_signal(barrier, inc=1, device_id=device, device_id_type=pl.DeviceIdType.MESH)
    pl.semaphore_wait(barrier, len(devices))


def aligned(start, size):
    return pl.ds(pl.multiple_of(start, size), size)


def open_kernel(
    tokens, weight, small, xt_out, w_out, qkv_out, small_out,
    x, xt, w, qkv, smalls, fill_x, fill_w, x_send, x_recv, s_send, s_recv, y_sems, z_send, z_recv,
    c_send, c_recv, out_sems,
    *, nz, nt, heads, head_size, group, chunk,
):
    z, k, c, t = (lax.axis_index(name) for name in AXES)
    f = z * 2 + k
    nf = nz * 2
    span, width = tokens.shape[1:]
    dblk = weight.shape[1]
    cols = heads * head_size
    gw = group * 2 * head_size
    chunks = span // chunk
    peers = [
        (dz, dk, dt) for dz in range(nz) for dk in range(2) for dt in range(nt) if (dz, dk, dt) != (0, 0, 0)
    ]

    def peer(offset):
        dz, dk, dt = offset
        return {"z": lax.rem(z + dz, nz), "core": lax.rem(k + dk, 2), "tensor": lax.rem(t + dt, nt)}

    def block(index):
        return w.at[aligned(index * dblk, dblk), :]

    for i in range(chunks):
        r = pl.ds(i * chunk, chunk)
        pltpu.make_async_copy(tokens.at[t, r], x.at[r], fill_x.at[i]).start()
    fills = []
    for g in range(cols // gw):
        for which in range(3):
            at = (g * 3 + which) * gw
            fills.append(
                pltpu.make_async_copy(
                    weight.at[which, :, pl.ds(g * gw, gw)],
                    w.at[aligned(f * dblk, dblk), pl.ds(at, gw)],
                    fill_w.at[len(fills)],
                )
            )

    @pl.when(c == t)
    def _():
        for one in fills:
            one.start()

    greet([{"context": 1 - c}] + [peer(offset) for offset in peers])
    x_copies = [
        remote(
            tokens.at[t, pl.ds(i * chunk, chunk)],
            x.at[pl.ds(span + i * chunk, chunk)],
            x_send.at[i],
            x_recv.at[i],
            {"context": 1 - c},
        )
        for i in range(chunks)
    ]
    for one in x_copies:
        one.start()
    y_copy = remote(block(f), block(f), y_sems.at[0], y_sems.at[1], {"tensor": 1 - t})

    @pl.when(c == t)
    def _():
        for one in fills:
            one.wait()
        y_copy.start()

    def small_copy(i, source):
        return remote(small, smalls.at[source], s_send.at[i], s_recv.at[source], peer(peers[i]))

    me = f * nt + t
    for i in range(len(peers)):
        small_copy(i, me).start()
    smalls[me] = small[...]

    @pl.when(c != t)
    def _():
        y_copy.wait_recv()

    def z_copy(d, owner):
        return remote(
            block(owner * 2 + k), block(owner * 2 + k), z_send.at[d - 1], z_recv.at[owner], {"z": lax.rem(z + d, nz)}
        )

    def c_copy(owner, core):
        return remote(
            block(owner * 2 + core), block(owner * 2 + core), c_send.at[owner], c_recv.at[owner], {"core": 1 - k}
        )

    for d in range(1, nz):
        z_copy(d, z).start()
    c_copy(z, k).start()

    for i in range(chunks):
        r = pl.ds(i * chunk, chunk)
        pltpu.make_async_copy(tokens.at[t, r], x.at[r], fill_x.at[i]).wait()
        xt[:, i * chunk : (i + 1) * chunk] = x[i * chunk : (i + 1) * chunk, :].T

    for i in range(len(peers)):
        dz, dk, dt = peers[i]
        source = (lax.rem(z + nz - dz, nz) * 2 + lax.rem(k + dk, 2)) * nt + lax.rem(t + nt - dt, nt)
        small_copy(i, source).wait_recv()

    edge = head_size // nf
    lanes = small.shape[1]
    rows = jnp.concatenate([smalls[fi * nt + c, 0:1, :] for fi in range(nf)], axis=0)
    col = lax.broadcasted_iota(jnp.int32, (lanes, cols), 1)
    source = lax.broadcasted_iota(jnp.int32, (lanes, cols), 0)
    fcol = lax.broadcasted_iota(jnp.int32, (nf, cols), 1)
    mine = lax.rem(fcol, head_size) // edge == lax.broadcasted_iota(jnp.int32, (nf, cols), 0)
    biases = []
    for kind in range(2):
        pick = source == col // head_size * edge + lax.rem(col, edge) + kind * heads * edge
        spread_out = mm(rows, jnp.where(pick, 1.0, 0.0).astype(BF))
        biases.append(jnp.sum(jnp.where(mine, spread_out, 0.0), axis=0, keepdims=True))
    parts = [biases[0], jnp.zeros_like(biases[0]), biases[1]]
    bias = jnp.concatenate(
        [parts[which][:, g * gw : (g + 1) * gw] for g in range(cols // gw) for which in range(3)], axis=1
    )

    for d in range(1, nz):
        owner = lax.rem(z + nz - d, nz)
        z_copy(d, owner).wait_recv()
        c_copy(owner, k).start()
    for owner in range(nz):
        c_copy(owner, 1 - k).wait_recv()

    w_done = pltpu.make_async_copy(w, w_out, out_sems.at[0, 0])
    w_done.start()
    small_done = pltpu.make_async_copy(smalls, small_out, out_sems.at[0, 1])
    small_done.start()

    def project(i):
        r = aligned(i * chunk, chunk)
        acc = mm(x[r, :], w[...]) + bias
        qkv[r, :] = acc.astype(BF)
        pltpu.make_async_copy(qkv.at[r], qkv_out.at[r], out_sems.at[1, i]).start()

    @pl.loop(0, chunks)
    def _(i):
        project(i)

    @pl.loop(0, chunks)
    def _(i):
        remote(
            tokens.at[t, aligned(i * chunk, chunk)],
            x.at[aligned(span + i * chunk, chunk)],
            x_send.at[i],
            x_recv.at[i],
            {"context": 1 - c},
        ).wait_recv()
        r = aligned(span + i * chunk, chunk)
        xt[:, r] = x[r, :].T
        project(chunks + i)

    xt_done = pltpu.make_async_copy(xt, xt_out, out_sems.at[0, 2])
    xt_done.start()
    for i in range(2 * chunks):
        r = pl.ds(i * chunk, chunk)
        pltpu.make_async_copy(qkv.at[r], qkv_out.at[r], out_sems.at[1, i]).wait()
    for one in (w_done, small_done, xt_done):
        one.wait()
    for one in x_copies:
        one.wait_send()
    for i in range(len(peers)):
        small_copy(i, me).wait_send()
    for d in range(1, nz):
        z_copy(d, z).wait_send()
    for owner in range(nz):
        c_copy(owner, k).wait_send()

    @pl.when(c == t)
    def _():
        y_copy.wait_send()


def open_layer(tokens, weight, small, nz, nt, heads, head_size, group):
    span, width = tokens.shape[1:]
    cols = heads * head_size
    chunk = 256
    chunks = span // chunk
    nf = nz * 2
    dma = pltpu.SemaphoreType.DMA
    hbm = pl.BlockSpec(memory_space=pl.ANY)
    moved = 2 * (span * width * 2 + 4 * width * cols * 3)
    return pl.pallas_call(
        functools.partial(
            open_kernel, nz=nz, nt=nt, heads=heads, head_size=head_size, group=group, chunk=chunk
        ),
        out_shape=(
            jax.ShapeDtypeStruct((width, 2 * span), BF),
            jax.ShapeDtypeStruct((width, 3 * cols), BF),
            jax.ShapeDtypeStruct((2 * span, 3 * cols), BF),
            jax.ShapeDtypeStruct((nf * nt,) + small.shape, BF),
        ),
        in_specs=[hbm, hbm, pl.BlockSpec(memory_space=pltpu.VMEM)],
        out_specs=(hbm,) * 4,
        scratch_shapes=[
            pltpu.VMEM((2 * span, width), BF),
            pltpu.VMEM((width, 2 * span), BF),
            pltpu.VMEM((width, 3 * cols), BF),
            pltpu.VMEM((2 * span, 3 * cols), BF),
            pltpu.VMEM((nf * nt,) + small.shape, BF),
            dma((chunks,)),
            dma((heads // 2 // group * 3,)),
            dma((chunks,)),
            dma((chunks,)),
            dma((nf * nt,)),
            dma((nf * nt,)),
            dma((2,)),
            dma((nz,)),
            dma((nz,)),
            dma((nz,)),
            dma((nz,)),
            dma((2, max(3, 2 * chunks))),
        ],
        compiler_params=pltpu.CompilerParams(
            collective_id=0, has_side_effects=True, vmem_limit_bytes=40 << 20
        ),
        cost_estimate=pl.CostEstimate(
            flops=2 * 2 * span * width * 3 * cols, bytes_accessed=moved, transcendentals=0
        ),
        name="open_layer",
    )(tokens, weight, small)


def close_kernel(
    dqkv_in, w_in, xt_in, grad_in, vec_in, tokens_out, grad_out, sums_out,
    dqkv, w, xt, dres, own, xs, xr, fin, away, near, zs, zr, piece, last, sums, sums_near, sums_z, sums_last,
    fill, x_send, x_recv, y_send, y_recv, c_sems, z_send, z_recv, p_send, p_recv, o_sems,
    *, nz, chunk, tile,
):
    z, k, c, t = (lax.axis_index(name) for name in AXES)
    rows, wide = dqkv.shape
    span = rows // 2
    dblk = xt.shape[2]
    chunks = span // chunk
    steps = wide // tile
    x_dev, y_dev, core_dev = {"context": 1 - c}, {"tensor": 1 - t}, {"core": 1 - k}
    diag = {"context": 1 - c, "tensor": 1 - t}

    loads = [
        pltpu.make_async_copy(w_in, w, fill.at[0]),
        pltpu.make_async_copy(dqkv_in.at[pl.ds(span, span)], dqkv.at[pl.ds(span, span)], fill.at[1]),
        pltpu.make_async_copy(dqkv_in.at[pl.ds(0, span)], dqkv.at[pl.ds(0, span)], fill.at[2]),
        pltpu.make_async_copy(grad_in, dres, fill.at[3]),
        pltpu.make_async_copy(vec_in, sums.at[pl.ds(sums.shape[0] - vec_in.shape[0], vec_in.shape[0])], fill.at[4]),
    ]
    for kk in range(2):
        for zi in range(nz):
            source = zi * 2 + lax.rem(1 - k + kk, 2)
            loads.append(
                pltpu.make_async_copy(
                    xt_in.at[aligned(source * dblk, dblk)], xt.at[kk, zi], fill.at[len(loads)]
                )
            )
    for one in loads:
        one.start()
    greet([x_dev, y_dev, diag, core_dev] + [{"z": lax.rem(z + d, nz)} for d in range(1, nz)])

    def x_copy(i):
        return remote(xs.at[i], xr.at[i], x_send.at[i], x_recv.at[i], x_dev)

    def y_copy(i):
        return remote(fin.at[i], tokens_out.at[t, aligned(i * chunk, chunk)], y_send.at[i], y_recv.at[i], y_dev)

    loads[0].wait()
    loads[1].wait()

    @pl.loop(0, chunks)
    def _(i):
        xs[i] = mm_nt(dqkv[aligned(span + i * chunk, chunk), :], w[...]).astype(BF)
        x_copy(i).start()

    for one in loads[2:]:
        one.wait()
    ones = jnp.ones((8, rows), BF)
    vec_at = sums.shape[0] - vec_in.shape[0]
    sums[0:vec_at, :] = jnp.zeros((vec_at, 128), F32)

    @pl.loop(0, steps)
    def _(j):
        part = dqkv[:, aligned(j * tile, tile)]
        for zi in range(nz):
            away[zi, :, aligned(j * tile, tile)] = mm(xt[0, zi], part).astype(BF)
        total = mm(ones, part)
        for u in range(tile // 128):
            sums[pl.ds(j * (tile // 128) + u, 1), :] = total[0:1, u * 128 : (u + 1) * 128]

    core_copy = remote(away, near, c_sems.at[0], c_sems.at[1], core_dev)
    core_copy.start()
    core_sum = remote(sums, sums_near, c_sems.at[2], c_sems.at[3], core_dev)
    core_sum.start()

    @pl.loop(0, chunks)
    def _(i):
        r = aligned(i * chunk, chunk)
        own[r, :] = mm_nt(dqkv[r, :], w[...]) + dres[r, :]

    def finish(i):
        x_copy(i).wait_recv()
        r = aligned(i * chunk, chunk)
        fin[i] = (own[r, :] + xr[i].astype(F32)).astype(BF)
        pltpu.make_async_copy(fin.at[i], tokens_out.at[t, r], o_sems.at[i]).start()
        y_copy(i).start()

    core_copy.wait_recv()
    core_sum.wait_recv()
    sums_z[z] = sums[...] + sums_near[...]

    @pl.loop(0, steps)
    def _(j):
        cut = aligned(j * tile, tile)
        part = dqkv[:, cut]
        for zi in range(nz):
            zs[zi, :, cut] = (mm(xt[1, zi], part) + near[zi, :, cut].astype(F32)).astype(BF)

    def z_copy(d, owner, target):
        return remote(zs.at[target], zr.at[owner], z_send.at[0, d - 1], z_recv.at[0, owner], {"z": lax.rem(z + d, nz)})

    def z_sum(d, owner):
        return remote(
            sums_z.at[owner], sums_z.at[owner], z_send.at[1, d - 1], z_recv.at[1, owner], {"z": lax.rem(z + d, nz)}
        )

    for d in range(1, nz):
        z_copy(d, z, lax.rem(z + d, nz)).start()
        z_sum(d, z).start()

    half = chunks // 2

    @pl.loop(0, half)
    def _(i):
        finish(i)

    for d in range(1, nz):
        owner = lax.rem(z + nz - d, nz)
        z_copy(d, owner, z).wait_recv()
        z_sum(d, owner).wait_recv()
    total = zs[z].astype(F32)
    for d in range(1, nz):
        total = total + zr[lax.rem(z + nz - d, nz)].astype(F32)
    piece[...] = total.astype(BF)
    sums_last[0] = jnp.sum(sums_z[...], axis=0)

    p_x = remote(piece, last.at[0], p_send.at[0], p_recv.at[0], x_dev)
    p_y = remote(piece, last.at[1], p_send.at[1], p_recv.at[1], y_dev)
    p_d = remote(piece, last.at[2], p_send.at[2], p_recv.at[2], diag)
    s_x = remote(sums_last.at[0], sums_last.at[1], p_send.at[3], p_recv.at[3], x_dev)
    s_y = remote(sums_last.at[0], sums_last.at[2], p_send.at[4], p_recv.at[4], y_dev)
    s_d = remote(sums_last.at[0], sums_last.at[3], p_send.at[5], p_recv.at[5], diag)

    for one in (s_x, s_y, s_d):
        one.start()

    @pl.when(c == t)
    def _():
        p_x.start()

    @pl.when(c != t)
    def _():
        p_y.start()
        p_d.start()

    @pl.loop(half, chunks)
    def _(i):
        finish(i)

    for one in (s_x, s_y, s_d):
        one.wait()
    near_pair = sums_last[0] + sums_last[2]
    far_pair = sums_last[1] + sums_last[3]
    sums_out[0:vec_at, :] = jnp.where(c == t, near_pair, far_pair)[0:vec_at]
    sums_out[vec_at:, :] = (near_pair + far_pair)[vec_at:]

    @pl.when(c == t)
    def _():
        p_y.wait_recv()
        grad_out[...] = piece[...].astype(F32) + last[1].astype(F32)
        p_x.wait_send()

    @pl.when(c != t)
    def _():
        p_x.wait_recv()
        p_d.wait_recv()
        grad_out[...] = last[0].astype(F32) + last[2].astype(F32)
        p_y.wait_send()
        p_d.wait_send()

    core_copy.wait_send()
    core_sum.wait_send()
    for d in range(1, nz):
        z_copy(d, z, lax.rem(z + d, nz)).wait_send()
        z_sum(d, z).wait_send()

    @pl.loop(0, chunks)
    def _(i):
        r = aligned(i * chunk, chunk)
        x_copy(i).wait_send()
        pltpu.make_async_copy(fin.at[i], tokens_out.at[t, r], o_sems.at[i]).wait()
        y_copy(i).wait_send()
        remote(fin.at[i], tokens_out.at[1 - t, r], y_send.at[i], y_recv.at[i], y_dev).wait_recv()


def close_layer(dqkv, w, xt, grad_in, vectors, nz):
    rows, wide = dqkv.shape
    width = w.shape[0]
    span = rows // 2
    dblk = width // (2 * nz)
    chunk, tile = 128, 256
    chunks = span // chunk
    dma = pltpu.SemaphoreType.DMA
    hbm = pl.BlockSpec(memory_space=pl.ANY)
    sum_rows = wide // 128 + -(wide // 128) % 8 + vectors.shape[0]
    return pl.pallas_call(
        functools.partial(close_kernel, nz=nz, chunk=chunk, tile=tile),
        out_shape=(
            jax.ShapeDtypeStruct((2, span, width), BF),
            jax.ShapeDtypeStruct((dblk, wide), F32),
            jax.ShapeDtypeStruct((sum_rows, 128), F32),
        ),
        in_specs=[hbm] * 5,
        out_specs=(hbm, pl.BlockSpec(memory_space=pltpu.VMEM), pl.BlockSpec(memory_space=pltpu.VMEM)),
        scratch_shapes=[
            pltpu.VMEM((rows, wide), BF),
            pltpu.VMEM((width, wide), BF),
            pltpu.VMEM((2, nz, dblk, rows), BF),
            pltpu.VMEM((span, width), F32),
            pltpu.VMEM((span, width), F32),
            pltpu.VMEM((chunks, chunk, width), BF),
            pltpu.VMEM((chunks, chunk, width), BF),
            pltpu.VMEM((chunks, chunk, width), BF),
            pltpu.VMEM((nz, dblk, wide), BF),
            pltpu.VMEM((nz, dblk, wide), BF),
            pltpu.VMEM((nz, dblk, wide), BF),
            pltpu.VMEM((nz, dblk, wide), BF),
            pltpu.VMEM((dblk, wide), BF),
            pltpu.VMEM((3, dblk, wide), BF),
            pltpu.VMEM((sum_rows, 128), F32),
            pltpu.VMEM((sum_rows, 128), F32),
            pltpu.VMEM((nz, sum_rows, 128), F32),
            pltpu.VMEM((4, sum_rows, 128), F32),
            dma((5 + 2 * nz,)),
            dma((chunks,)),
            dma((chunks,)),
            dma((chunks,)),
            dma((chunks,)),
            dma((4,)),
            dma((2, nz)),
            dma((2, nz)),
            dma((6,)),
            dma((6,)),
            dma((chunks,)),
        ],
        compiler_params=pltpu.CompilerParams(
            collective_id=1, has_side_effects=True, vmem_limit_bytes=56 << 20
        ),
        cost_estimate=pl.CostEstimate(
            flops=4 * rows * width * wide, bytes_accessed=30 << 20, transcendentals=0
        ),
        name="close_layer",
    )(dqkv, w, xt, grad_in, vectors)


def mean_of(rows):
    return jnp.mean(rows, axis=-1, keepdims=True)


def load_blocks(stack, start, dest, sems, nt, rows_by_f):
    count, rows = stack.shape[:2]
    columns = dest.shape[1] // nt if rows_by_f else stack.shape[2]
    copies = []
    for b in range(count):
        first, second = (b // nt, b % nt) if rows_by_f else (b % nt, b // nt)
        spot = dest.at[pl.ds(first * rows, rows), pl.ds(second * columns, columns)]
        copies.append(pltpu.make_async_copy(stack.at[b, :, pl.ds(start, columns)], spot, sems.at[b]))
    return copies


def up_kernel(
    t_ref, ctx, tok, vecs, up_add, up_in, first, norm_one, inv_one, first_t, act, slope,
    up, proj, low, u, fill,
    *, nt, tile,
):
    i = pl.program_id(0)
    width, hidden = up.shape
    tiles = hidden // tile
    up_fill = load_blocks(up_in, 0, up, fill.at[0], nt, True)
    proj_fill = load_blocks(up_in, hidden // nt, proj, fill.at[1], nt, True)

    @pl.when(i == 0)
    def _():
        for one in proj_fill + up_fill:
            one.start()
        for one in proj_fill:
            one.wait()

    def vec(row):
        return vecs[row : row + 1, :]

    h = tok[0].astype(F32) + (mm_nt(ctx[...], proj[...]) + vec(0))
    centred = h - mean_of(h)
    inv = lax.rsqrt(mean_of(centred * centred) + NORM_EPS)
    normed = centred * inv
    norm_one[...] = normed
    inv_one[...] = jnp.broadcast_to(inv, inv_one.shape)
    normed = normed * vec(1) + vec(2)
    first[...] = normed
    low[...] = normed.astype(BF)
    first_t[...] = low[...].T

    @pl.when(i == 0)
    def _():
        for one in up_fill:
            one.wait()

    u[0] = mm(low[...], up[:, :tile])

    def activate(j, slot):
        cut = aligned(j * tile, tile)
        value = u[slot] + up_add[0:1, cut]
        phi = 0.5 + 0.5 * lax.erf(value * (0.5**0.5))
        act[:, cut] = (value * phi).astype(BF)
        slope[:, cut] = (phi + value * (jnp.exp(-0.5 * value * value) * ((2.0 * jnp.pi) ** -0.5))).astype(BF)

    @pl.loop(0, tiles - 1)
    def _(j):
        slot = lax.rem(j, 2)
        following = mm(low[...], up[:, aligned((j + 1) * tile, tile)])
        activate(j, slot)
        u[1 - slot] = following

    activate(tiles - 1, (tiles - 1) % 2)


def up_layer(t, ctx, tokens, vecs, up_add, up_all, nt):
    span, width = ctx.shape
    hidden = up_add.shape[1]
    block, tile = 256, 512
    hbm = pl.BlockSpec(memory_space=pl.ANY)
    rows = pl.BlockSpec((block, width), lambda i, _: (i, 0))
    wide = pl.BlockSpec((block, hidden), lambda i, _: (i, 0))
    whole = lambda shape: pl.BlockSpec(shape, lambda i, _: (0,) * len(shape))
    picked = pl.BlockSpec((1, block, width), lambda i, t_ref: (t_ref[0], i, 0))
    sds = jax.ShapeDtypeStruct
    return pl.pallas_call(
        functools.partial(up_kernel, nt=nt, tile=tile),
        out_shape=(
            sds((span, width), F32),
            sds((span, width), F32),
            sds((span, 128), F32),
            sds((width, span), BF),
            sds((span, hidden), BF),
            sds((span, hidden), BF),
        ),
        grid_spec=pltpu.PrefetchScalarGridSpec(
            num_scalar_prefetch=1,
            grid=(span // block,),
            in_specs=[rows, picked, whole(vecs.shape), whole(up_add.shape), hbm],
            out_specs=(
                rows,
                rows,
                pl.BlockSpec((block, 128), lambda i, _: (i, 0)),
                pl.BlockSpec((width, block), lambda i, _: (0, i)),
                wide,
                wide,
            ),
            scratch_shapes=[
                pltpu.VMEM((width, hidden), BF),
                pltpu.VMEM((width, width), BF),
                pltpu.VMEM((block, width), BF),
                pltpu.VMEM((2, block, tile), F32),
                pltpu.SemaphoreType.DMA((2, up_all.shape[0])),
            ],
        ),
        compiler_params=pltpu.CompilerParams(vmem_limit_bytes=60 << 20),
        cost_estimate=pl.CostEstimate(
            flops=2 * span * width * (width + hidden), bytes_accessed=40 << 20, transcendentals=2 * span * hidden
        ),
        name="up_layer",
    )(t, ctx, tokens, vecs, up_add, up_all)


def add_rows(sums, row, value):
    sums[row] += jnp.sum(value.reshape(-1, 8, value.shape[1]), axis=0)


def down_kernel(
    t_ref, cot, vecs, first, act, down_in, out, branch, branch_t, grad_second, vec_sums,
    down, acc, sums, fill,
    *, nt,
):
    i = pl.program_id(0)
    hidden, width = down.shape
    down_fill = load_blocks(down_in, 0, down, fill, nt, False)

    @pl.when(i == 0)
    def _():
        for one in down_fill:
            one.start()
        sums[...] = jnp.zeros(sums.shape, F32)
        for one in down_fill:
            one.wait()

    def vec(row):
        return vecs[row : row + 1, :]

    tile = 256

    @pl.loop(0, width // tile)
    def _(j):
        cut = aligned(j * tile, tile)
        acc[:, cut] = mm(act[...], down[:, cut])

    h = first[...] + (acc[...] + vec(3))
    centred = h - mean_of(h)
    inv = lax.rsqrt(mean_of(centred * centred) + NORM_EPS)
    normed = centred * inv
    out[...] = (normed * vec(4) + vec(5)).astype(BF)
    grad = cot[0].astype(F32)
    add_rows(sums, 1, grad * normed)
    add_rows(sums, 2, grad)
    grad = grad * vec(4)
    grad = inv * (grad - mean_of(grad) - normed * mean_of(grad * normed))
    grad_second[...] = grad
    low = grad.astype(BF)
    branch[...] = low
    add_rows(sums, 0, low.astype(F32))
    branch_t[...] = low.T

    @pl.when(i == pl.num_programs(0) - 1)
    def _():
        for row in range(3):
            vec_sums[row : row + 1, :] = jnp.sum(sums[row], axis=0, keepdims=True)
        vec_sums[3:8, :] = jnp.zeros((5, width), F32)


def down_layer(t, out_grad, vecs, first, act, down_all, nt):
    span, width = first.shape
    hidden = act.shape[1]
    block = 256
    rows = pl.BlockSpec((block, width), lambda i, _: (i, 0))
    whole = lambda shape: pl.BlockSpec(shape, lambda i, _: (0,) * len(shape))
    sds = jax.ShapeDtypeStruct
    return pl.pallas_call(
        functools.partial(down_kernel, nt=nt),
        out_shape=(
            sds((span, width), BF),
            sds((span, width), BF),
            sds((width, span), BF),
            sds((span, width), F32),
            sds((8, width), F32),
        ),
        grid_spec=pltpu.PrefetchScalarGridSpec(
            num_scalar_prefetch=1,
            grid=(span // block,),
            in_specs=[
                pl.BlockSpec((1, block, width), lambda i, t_ref: (t_ref[0], i, 0)),
                whole(vecs.shape),
                rows,
                pl.BlockSpec((block, hidden), lambda i, _: (i, 0)),
                pl.BlockSpec(memory_space=pl.ANY),
            ],
            out_specs=(rows, rows, pl.BlockSpec((width, block), lambda i, _: (0, i)), rows, whole((8, width))),
            scratch_shapes=[
                pltpu.VMEM((hidden, width), BF),
                pltpu.VMEM((block, width), F32),
                pltpu.VMEM((3, 8, width), F32),
                pltpu.SemaphoreType.DMA((down_all.shape[0],)),
            ],
        ),
        compiler_params=pltpu.CompilerParams(vmem_limit_bytes=60 << 20),
        cost_estimate=pl.CostEstimate(
            flops=2 * span * width * hidden, bytes_accessed=30 << 20, transcendentals=0
        ),
        name="down_layer",
    )(t, out_grad, vecs, first, act, down_all)


def back_kernel(
    vecs, branch, grad_second, slope, norm_one, inv_one, up_in, down_in,
    hid, attn_t, grad_in, grad_ctx, vec_sums, up_sums,
    up, down, proj, acc, sums, sums_u, fill,
    *, nt, tile,
):
    i = pl.program_id(0)
    width, hidden = up.shape
    down_fill = load_blocks(down_in, 0, down, fill.at[0], nt, False)
    up_fill = load_blocks(up_in, 0, up, fill.at[1], nt, True)
    proj_fill = load_blocks(up_in, hidden // nt, proj, fill.at[2], nt, True)

    @pl.when(i == 0)
    def _():
        for one in down_fill + up_fill + proj_fill:
            one.start()
        sums[...] = jnp.zeros(sums.shape, F32)
        sums_u[...] = jnp.zeros(sums_u.shape, F32)
        for one in down_fill + up_fill + proj_fill:
            one.wait()

    ones = jnp.ones((8, branch.shape[0]), BF)
    acc[...] = grad_second[...]

    @pl.loop(0, hidden // tile)
    def _(j):
        cut = aligned(j * tile, tile)
        low_hid = (mm_nt(branch[...], down[cut, :]) * slope[:, cut].astype(F32)).astype(BF)
        hid[:, cut] = low_hid
        sums_u[:, cut] += mm(ones, low_hid)
        acc[...] += mm_nt(low_hid, up[:, cut])

    grad = acc[...]
    normed = norm_one[...]
    add_rows(sums, 1, grad * normed)
    add_rows(sums, 2, grad)
    grad = grad * vecs[1:2, :]
    grad = inv_one[:, 0:1] * (grad - mean_of(grad) - normed * mean_of(grad * normed))
    grad_in[...] = grad
    low = grad.astype(BF)
    add_rows(sums, 0, low.astype(F32))
    attn_t[...] = low.T
    grad_ctx[...] = mm(low, proj[...]).astype(BF)

    @pl.when(i == pl.num_programs(0) - 1)
    def _():
        for row in range(3):
            vec_sums[row : row + 1, :] = jnp.sum(sums[row], axis=0, keepdims=True)
        vec_sums[3:8, :] = jnp.zeros((5, width), F32)
        up_sums[...] = sums_u[...]


def back_layer(vecs, branch, grad_second, slope, norm_one, inv_one, up_all, down_all, nt):
    span, width = branch.shape
    hidden = slope.shape[1]
    block, tile = 256, 512
    hbm = pl.BlockSpec(memory_space=pl.ANY)
    rows = pl.BlockSpec((block, width), lambda i: (i, 0))
    wide = pl.BlockSpec((block, hidden), lambda i: (i, 0))
    whole = lambda shape: pl.BlockSpec(shape, lambda i: (0,) * len(shape))
    sds = jax.ShapeDtypeStruct
    return pl.pallas_call(
        functools.partial(back_kernel, nt=nt, tile=tile),
        out_shape=(
            sds((span, hidden), BF),
            sds((width, span), BF),
            sds((span, width), F32),
            sds((span, width), BF),
            sds((8, width), F32),
            sds((8, hidden), F32),
        ),
        grid=(span // block,),
        in_specs=[
            whole(vecs.shape),
            rows,
            rows,
            wide,
            rows,
            pl.BlockSpec((block, 128), lambda i: (i, 0)),
            hbm,
            hbm,
        ],
        out_specs=(
            wide, pl.BlockSpec((width, block), lambda i: (0, i)), rows, rows, whole((8, width)), whole((8, hidden)),
        ),
        scratch_shapes=[
            pltpu.VMEM((width, hidden), BF),
            pltpu.VMEM((hidden, width), BF),
            pltpu.VMEM((width, width), BF),
            pltpu.VMEM((block, width), F32),
            pltpu.VMEM((3, 8, width), F32),
            pltpu.VMEM((8, hidden), F32),
            pltpu.SemaphoreType.DMA((3, up_all.shape[0])),
        ],
        compiler_params=pltpu.CompilerParams(vmem_limit_bytes=60 << 20),
        cost_estimate=pl.CostEstimate(
            flops=2 * span * width * (width + 2 * hidden), bytes_accessed=60 << 20, transcendentals=0
        ),
        name="back_layer",
    )(vecs, branch, grad_second, slope, norm_one, inv_one, up_all, down_all)


def grads_kernel(*refs, pairs, nz, nt, chunk):
    lefts, rights = refs[0 : 2 * pairs : 2], refs[1 : 2 * pairs : 2]
    packed, left, right, away, near, stage, l_fill, r_fill, send, recv, out_sems = refs[2 * pairs :]
    k = lax.axis_index("core")
    core_dev = {"core": 1 - k}
    dblk = left.shape[3]
    span = right.shape[1]
    plan = []
    base = 0
    for which in range(pairs):
        size = rights[which].shape[1] // nt
        for ti in range(nt):
            for at in range(0, size, min(chunk, size)):
                step = min(chunk, size)
                plan.append((which, ti * size + at, ti, base + at, step))
        base += size

    l_copies = [
        [
            pltpu.make_async_copy(
                lefts[which].at[aligned((zi * 2 + lax.rem(k + 1 + kk, 2)) * dblk, dblk)],
                left.at[which, kk, zi],
                l_fill.at[which, kk, zi],
            )
            for kk in range(2)
            for zi in range(nz)
        ]
        for which in range(pairs)
    ]
    r_copies = [
        pltpu.make_async_copy(
            rights[which].at[:, pl.ds(col, step)], right.at[n, :, pl.ds(0, step)], r_fill.at[n]
        )
        for n, (which, col, _ti, _out, step) in enumerate(plan)
    ]
    for n, (which, _col, _ti, _out, _step) in enumerate(plan):
        if n == 0 or plan[n - 1][0] != which:
            for one in l_copies[which]:
                one.start()
        r_copies[n].start()
    greet([core_dev])

    def exchange(n):
        step = plan[n][4]
        cut = pl.ds(0, step)
        return remote(away.at[n, :, :, cut], near.at[n, :, :, cut], send.at[n], recv.at[n], core_dev)

    sub = 256
    for n, (which, _col, _ti, _out, step) in enumerate(plan):
        if n == 0 or plan[n - 1][0] != which:
            for one in l_copies[which]:
                one.wait()
        r_copies[n].wait()

        @pl.loop(0, step // sub)
        def _(j, n=n, which=which):
            cut = aligned(j * sub, sub)
            for zi in range(nz):
                away[n, zi, :, cut] = mm(left[which, 0, zi], right[n, :, cut]).astype(BF)

        exchange(n).start()

    outs = []
    for n, (which, _col, ti, out, step) in enumerate(plan):
        exchange(n).wait_recv()
        slot = n % 2
        if n >= 2:
            for one in outs[n - 2]:
                one.wait()

        @pl.loop(0, step // sub)
        def _(j, n=n, which=which, slot=slot):
            cut = aligned(j * sub, sub)
            for zi in range(nz):
                stage[slot, zi, :, cut] = (
                    mm(left[which, 1, zi], right[n, :, cut]) + near[n, zi, :, cut].astype(F32)
                ).astype(BF)

        outs.append(
            [
                pltpu.make_async_copy(
                    stage.at[slot, zi, :, pl.ds(0, step)],
                    packed.at[pl.ds((ti * nz + zi) * dblk, dblk), pl.ds(out, step)],
                    out_sems.at[slot, zi],
                )
                for zi in range(nz)
            ]
        )
        for one in outs[n]:
            one.start()
    for group in outs[-2:]:
        for one in group:
            one.wait()
    for n in range(len(plan)):
        exchange(n).wait_send()


def grads_layer(operands, nz, nt, collective_id):
    pairs = len(operands) // 2
    width, span = operands[0].shape
    chunk = 1024
    dblk = width // (2 * nz)
    sizes = [one.shape[1] // nt for one in operands[1::2]]
    count = sum(nt * max(1, size // chunk) for size in sizes)
    dma = pltpu.SemaphoreType.DMA
    hbm = pl.BlockSpec(memory_space=pl.ANY)
    return pl.pallas_call(
        functools.partial(grads_kernel, pairs=pairs, nz=nz, nt=nt, chunk=chunk),
        out_shape=jax.ShapeDtypeStruct((nt * nz * dblk, sum(sizes)), BF),
        in_specs=[hbm] * len(operands),
        out_specs=hbm,
        scratch_shapes=[
            pltpu.VMEM((pairs, 2, nz, dblk, span), BF),
            pltpu.VMEM((count, span, chunk), BF),
            pltpu.VMEM((count, nz, dblk, chunk), BF),
            pltpu.VMEM((count, nz, dblk, chunk), BF),
            pltpu.VMEM((2, nz, dblk, chunk), BF),
            dma((pairs, 2, nz)),
            dma((count,)),
            dma((count,)),
            dma((count,)),
            dma((2, nz)),
        ],
        compiler_params=pltpu.CompilerParams(
            collective_id=collective_id, has_side_effects=True, vmem_limit_bytes=60 << 20
        ),
        cost_estimate=pl.CostEstimate(
            flops=2 * span * width * nt * sum(sizes), bytes_accessed=40 << 20, transcendentals=0
        ),
        name="grads_layer",
    )(*operands)


def on_device_rows(
    sizes,
    tokens,
    segment_ids,
    qkv_weight,
    qv_bias,
    proj_weight,
    proj_bias,
    first_gain,
    first_shift,
    up_weight,
    up_bias,
    down_weight,
    down_bias,
    second_gain,
    second_shift,
    out_grad,
):
    nf, nc, nt = sizes
    nz = nf // 2
    zbits = nz.bit_length() - 1
    z, k, c, t = (lax.axis_index(name) for name in AXES)
    f = z * 2 + k

    def send(value, target):
        pairs = []
        for fi in range(nf):
            for ci in range(nc):
                for ti in range(nt):
                    to = target(fi // 2, fi % 2, ci, ti)
                    if to is not None:
                        zo, ko, co, tto = to
                        pairs.append(((fi * nc + ci) * nt + ti, ((zo * 2 + ko) * nc + co) * nt + tto))
        return lax.ppermute(value, AXES, pairs)

    def over_x(v):
        return send(v, lambda zi, ki, ci, ti: (zi, ki, 1 - ci, ti))

    def over_y(v):
        return send(v, lambda zi, ki, ci, ti: (zi, ki, ci, 1 - ti))

    def over_core(v):
        return send(v, lambda zi, ki, ci, ti: (zi, 1 - ki, ci, ti))

    def over_z(v):
        return send(v, lambda zi, ki, ci, ti: ((zi + 1) % nz, ki, ci, ti))

    def over_zbit(v, bit):
        return send(v, lambda zi, ki, ci, ti: (zi ^ (1 << bit), ki, ci, ti))

    def z_all(v):
        return [v] + [
            send(v, lambda zi, ki, ci, ti, d=d: ((zi + d) % nz, ki, ci, ti)) for d in range(1, nz)
        ]

    def z_ring(v):
        out = [v]
        for _ in range(nz - 1):
            out.append(over_z(out[-1]))
        return out

    def ordered(index, own, other, axis=0):
        return jnp.where(index == 0, jnp.concatenate([own, other], axis), jnp.concatenate([other, own], axis))

    seq_count, span, width = tokens.shape
    heads = qv_bias.shape[1]
    head_size = qv_bias.shape[2] * nf
    cols = heads * head_size
    hidden = up_weight.shape[1] * nt
    dblk = width // nf

    pairs = heads // 2
    group = max(1, pairs // 2)
    wide = 2 * head_size

    pieces = [qv_bias, up_bias, proj_bias, first_gain, first_shift, down_bias, second_gain, second_shift]
    small = jnp.concatenate([p.reshape(-1, 128) for p in pieces])
    up_at, vec_at = qv_bias.size // 128, (qv_bias.size + up_bias.size) // 128
    small = jnp.pad(small, ((0, -(small.shape[0] + 2) % 16 + 2), (0, 0)))
    own_seg = jnp.where(t == 0, segment_ids[0], segment_ids[1])
    other_seg = over_x(own_seg)
    rows_t, qkv_full, qkv, small = open_layer(tokens, qkv_weight, small, nz, nt, heads, head_size, group)
    small = small.reshape(nf, nt, -1, 128)
    edge = head_size // nf

    def interleave(rows, columns):
        col = lax.broadcasted_iota(jnp.int32, (rows.shape[1], columns), 1)
        source = lax.broadcasted_iota(jnp.int32, (rows.shape[1], columns), 0)
        spread_out = mm(rows, (source == col // head_size * edge + col % edge).astype(BF))
        col = lax.broadcasted_iota(jnp.int32, (nf, columns), 1)
        mine = col % head_size // edge == lax.broadcasted_iota(jnp.int32, (nf, columns), 0)
        return jnp.sum(jnp.where(mine, spread_out, 0.0), axis=0)

    up_add = jnp.concatenate(
        [interleave(small[:, i, up_at:vec_at].reshape(nf, -1), hidden // nt) for i in range(nt)]
    ).reshape(1, hidden)
    vecs = small[:, 0, vec_at : vec_at + 8].transpose(1, 0, 2).reshape(8, width).astype(F32)

    every = AXES[:2] + AXES[3:]
    up_shard = jnp.concatenate([up_weight, proj_weight.T], axis=1)
    up_all = lax.all_gather(up_shard, every).reshape((-1,) + up_shard.shape)
    down_all = lax.all_gather(after(down_weight, up_shard), every).reshape((-1,) + down_weight.shape)

    seg_store = jnp.concatenate([own_seg, other_seg])
    seg_global = ordered(c, own_seg, other_seg)
    total = 2 * span
    blk = 256
    low, high = segment_bounds(seg_global, blk, blk)
    shift = jnp.reshape(c * (total // blk // 2), (1,)).astype(jnp.int32)
    seg_k = jnp.broadcast_to(seg_store[:, None], (total, 128))
    seg_q = jnp.broadcast_to(seg_store[None, :], (8, total))
    attn_args = (seg_k, seg_q, low, high, shift)
    mixed, lse, mixed_other = [], [], []
    for p in range(pairs):
        out, one = attn_fwd(qkv, *attn_args, p, pairs, group, head_size, blk, blk)
        mixed.append(out)
        lse.append(one)
        mixed_other.append(over_x(out[span:]))
    up_all, _last = lax.optimization_barrier((up_all, mixed[-1]))
    context_rows = ordered(
        c, jnp.concatenate([m[:span] for m in mixed], 1), jnp.concatenate(mixed_other, 1), 1
    )

    which = t.reshape(1)
    first, norm_one, inv_one, first_t, act_low, slope = up_layer(
        which, context_rows, tokens, vecs, up_add, up_all, nt
    )
    down_all, first = lax.optimization_barrier((down_all, first))
    out_low, branch, branch_t, grad_second, vec_two = down_layer(
        which, out_grad, vecs, first, act_low, down_all, nt
    )
    down_sum = grads_layer([branch_t, act_low], nz, nt, 2)
    branch, down_sum = lax.optimization_barrier((branch, down_sum))
    hidden_low, attn_t, grad_in, grad_context, vec_one, up_sums = back_layer(
        vecs, branch, grad_second, slope, norm_one, inv_one, up_all, down_all, nt
    )
    layer_output = ordered(t, out_low[None], over_y(out_low)[None])
    halves = grad_context[:, :cols], grad_context[:, cols:]
    dctx_own = jnp.where(c == 0, halves[0], halves[1])
    dctx_other = over_x(jnp.where(c == 0, halves[1], halves[0]))
    dctx = jnp.concatenate([dctx_own, dctx_other])

    other_sum = grads_layer([first_t, hidden_low, attn_t, context_rows], nz, nt, 3)
    dctx, other_sum = lax.optimization_barrier((dctx, other_sum))
    part = lax.psum_scatter(down_sum, ("tensor", "z"), scatter_dimension=0, tiled=True)
    grad_down = (part.astype(F32) + over_x(part).astype(F32)).T
    part = lax.psum_scatter(other_sum, ("tensor", "z", "context"), scatter_dimension=0, tiled=True)
    part = ordered(c, part, over_x(part), 0).astype(F32)
    grad_up = part[:, : hidden // nt]
    grad_proj = part[:, hidden // nt :].T

    sums = jnp.concatenate([vec_one[:3].reshape(-1, 128), vec_two[:3].reshape(-1, 128), up_sums[0].reshape(-1, 128)])
    dqkv = None
    for p in range(pairs):
        dqkv = attn_bwd(dqkv, qkv, mixed[p], dctx, lse[p], *attn_args, p, pairs, group, head_size, blk, blk)
    tokens_grad, qkv_rows, qv_sum = close_layer(dqkv, qkv_full, rows_t, grad_in, sums, nz)
    sums = qv_sum[-sums.shape[0] :].reshape(-1)
    qv_sum = qv_sum[: 3 * cols // 128].reshape(-1)
    vector_out = [
        lax.dynamic_slice_in_dim(sums[i * width : (i + 1) * width], f * dblk, dblk) for i in range(6)
    ]
    up_rows, up_cols = up_bias.shape
    bias_up = sums[6 * width :].reshape(nt * up_rows, nf * up_cols)
    bias_up = lax.dynamic_slice(bias_up, (t * up_rows, f * up_cols), (up_rows, up_cols))


    def unpack(rows, which):
        return jnp.concatenate(
            [rows[..., (3 * i + which * group) * wide :][..., : group * wide] for i in range(0, pairs, group)],
            axis=-1,
        )

    grad_qkv = jnp.stack([unpack(qkv_rows, which) for which in range(3)])
    qv_sum = jnp.concatenate([unpack(qv_sum, 0), unpack(qv_sum, 2)]).reshape(2, heads, head_size)
    grad_qv = lax.dynamic_slice_in_dim(qv_sum, f * (head_size // nf), head_size // nf, 2)

    return (
        layer_output,
        tokens_grad,
        grad_qkv,
        grad_qv,
        grad_proj,
        vector_out[0],
        vector_out[1],
        vector_out[2],
        grad_up,
        bias_up,
        grad_down,
        vector_out[3],
        vector_out[4],
        vector_out[5],
    )


def solution(mesh):
    sizes = tuple(mesh.shape[name] for name in ("fsdp", "context", "tensor"))
    nf, nc, nt = sizes
    shards = (
        P("fsdp", "context", None),
        P("fsdp", "context"),
        P(None, "fsdp", "tensor"),
        P(None, "tensor", "fsdp"),
        P("tensor", "fsdp"),
        P("fsdp"),
        P("fsdp"),
        P("fsdp"),
        P("fsdp", "tensor"),
        P("tensor", "fsdp"),
        P("tensor", "fsdp"),
        P("fsdp"),
        P("fsdp"),
        P("fsdp"),
    )
    in_specs = (shards[0],) + shards[1:] + (shards[0],)
    out_specs = (shards[0], shards[0]) + shards[2:]
    nz = nf // 2
    by_rows = nc == nt == 2 and nf % 2 == 0 and nz & (nz - 1) == 0
    rows_mesh = jax.sharding.Mesh(mesh.devices.reshape(nz, 2, nc, nt), AXES) if by_rows else None

    def finer(spec):
        return P(*(("z", "core") if name == "fsdp" else name for name in spec))

    def program(*args):
        if by_rows and args[0].shape[0] // nf == nt:
            return jax.shard_map(
                functools.partial(on_device_rows, sizes),
                mesh=rows_mesh,
                in_specs=tuple(finer(spec) for spec in in_specs),
                out_specs=tuple(finer(spec) for spec in out_specs),
                check_vma=False,
            )(*args)
        return jax.shard_map(
            on_device_general, mesh=mesh, in_specs=in_specs, out_specs=out_specs, check_vma=False
        )(*args)

    return program
```

```python
import functools

import jax
import jax.numpy as jnp
from jax import lax
from jax.experimental import pallas as pl
from jax.experimental.pallas import tpu as pltpu
from jax.sharding import PartitionSpec as P

NORM_EPS = 1e-05


def layer_norm(hidden_rows, norm_gain, norm_shift):
    row_mean = jnp.mean(hidden_rows, axis=-1, keepdims=True)
    centred = hidden_rows - row_mean
    variance = jnp.mean(centred * centred, axis=-1, keepdims=True)
    return centred * lax.rsqrt(variance + NORM_EPS) * norm_gain + norm_shift


def exact_gelu(values):
    return jax.nn.gelu(values, approximate=False)


def masked_logits(query_heads, key_heads, seg_query, seg_key, score_scale):
    logits = (
        jnp.einsum("qhe,khe->hqk", query_heads, key_heads, preferred_element_type=jnp.float32)
        * score_scale
    )
    same_doc = (seg_query[:, None] == seg_key[None, :])[None, :, :]
    return jnp.where(same_doc, logits, -1e30)


def on_device_general(
    tokens,
    segment_ids,
    qkv_weight,
    qv_bias,
    proj_weight,
    proj_bias,
    first_gain,
    first_shift,
    up_weight,
    up_bias,
    down_weight,
    down_bias,
    second_gain,
    second_shift,
    out_grad,
):
    seq_count, span, width = tokens.shape
    total_rows = seq_count * span
    share = total_rows // lax.axis_size("tensor")
    row_start = lax.axis_index("tensor") * share
    token_rows = tokens.reshape(total_rows, width)
    gathered = (
        lax.all_gather(qkv_weight, "fsdp", axis=1, tiled=True),
        lax.all_gather(qv_bias, "fsdp", axis=2, tiled=True),
        lax.all_gather(proj_weight, "fsdp", axis=1, tiled=True),
        lax.all_gather(proj_bias, "fsdp", axis=0, tiled=True),
        lax.all_gather(first_gain, "fsdp", axis=0, tiled=True),
        lax.all_gather(first_shift, "fsdp", axis=0, tiled=True),
        lax.all_gather(up_weight, "fsdp", axis=0, tiled=True),
        lax.all_gather(up_bias, "fsdp", axis=1, tiled=True),
        lax.all_gather(down_weight, "fsdp", axis=1, tiled=True),
        lax.all_gather(down_bias, "fsdp", axis=0, tiled=True),
        lax.all_gather(second_gain, "fsdp", axis=0, tiled=True),
        lax.all_gather(second_shift, "fsdp", axis=0, tiled=True),
    )
    qkv_full, qv_full, proj_full, proj_add, gain_one, shift_one = (
        gathered[0],
        gathered[1],
        gathered[2],
        gathered[3],
        gathered[4],
        gathered[5],
    )
    up_full, up_add, down_full, down_add, gain_two, shift_two = (
        gathered[6],
        gathered[7],
        gathered[8],
        gathered[9],
        gathered[10],
        gathered[11],
    )
    local_width = qkv_full.shape[2]
    head_count = qv_full.shape[1]
    head_size = qv_full.shape[2]
    score_scale = float(head_size) ** (-0.5)
    projected = jnp.einsum("rd,cde->cre", token_rows, qkv_full, preferred_element_type=jnp.float32)
    bias_rows = qv_full.reshape(2, local_width).astype(jnp.float32)
    head_shape = (seq_count, span, head_count, head_size)
    query_heads = (projected[0] + bias_rows[0]).astype(jnp.bfloat16).reshape(head_shape)
    key_heads = projected[1].astype(jnp.bfloat16).reshape(head_shape)
    value_heads = (projected[2] + bias_rows[1]).astype(jnp.bfloat16).reshape(head_shape)
    key_all, value_all, seg_all = (
        lax.all_gather(key_heads, "context", axis=1, tiled=True),
        lax.all_gather(value_heads, "context", axis=1, tiled=True),
        lax.all_gather(segment_ids, "context", axis=1, tiled=True),
    )

    def attend_forward(pieces):
        query_one, key_one, value_one, seg_query, seg_key = pieces
        logits = masked_logits(query_one, key_one, seg_query, seg_key, score_scale)
        row_top = jnp.max(logits, axis=-1, keepdims=True)
        weights = jnp.exp(logits - row_top)
        row_total = jnp.sum(weights, axis=-1, keepdims=True)
        soft_low = (weights / row_total).astype(jnp.bfloat16)
        mixed_one = jnp.einsum(
            "hqk,khe->qhe", soft_low, value_one, preferred_element_type=jnp.float32
        )
        return (mixed_one.astype(jnp.bfloat16), row_top + jnp.log(row_total))

    mixed, log_totals = lax.map(
        attend_forward, (query_heads, key_all, value_all, segment_ids, seg_all)
    )
    context_low = mixed.reshape(total_rows, local_width)
    attn_part = jnp.dot(context_low, proj_full, preferred_element_type=jnp.float32)
    attn_share = lax.psum_scatter(
        attn_part, "tensor", scatter_dimension=0, tiled=True
    ) + proj_add.astype(jnp.float32)
    token_share = lax.dynamic_slice_in_dim(token_rows, row_start, share, 0).astype(jnp.float32)
    first_share, first_pull = jax.vjp(
        layer_norm,
        token_share + attn_share,
        gain_one.astype(jnp.float32),
        shift_one.astype(jnp.float32),
    )
    first_low = lax.all_gather(first_share.astype(jnp.bfloat16), "tensor", axis=0, tiled=True)
    hidden_pre = jnp.dot(first_low, up_full, preferred_element_type=jnp.float32) + up_add.reshape(
        -1
    ).astype(jnp.float32)
    activation, gelu_pull = jax.vjp(exact_gelu, hidden_pre)
    act_low = activation.astype(jnp.bfloat16)
    down_part = jnp.dot(act_low, down_full, preferred_element_type=jnp.float32)
    branch_share = lax.psum_scatter(
        down_part, "tensor", scatter_dimension=0, tiled=True
    ) + down_add.astype(jnp.float32)
    output_share, second_pull = jax.vjp(
        layer_norm,
        first_share + branch_share,
        gain_two.astype(jnp.float32),
        shift_two.astype(jnp.float32),
    )
    qkv_back, proj_back, up_back, down_back = (
        lax.all_gather(qkv_weight, "fsdp", axis=1, tiled=True),
        lax.all_gather(proj_weight, "fsdp", axis=1, tiled=True),
        lax.all_gather(up_weight, "fsdp", axis=0, tiled=True),
        lax.all_gather(down_weight, "fsdp", axis=1, tiled=True),
    )
    cot_share = lax.dynamic_slice_in_dim(
        out_grad.reshape(total_rows, width), row_start, share, 0
    ).astype(jnp.float32)
    grad_second, gain_two_part, shift_two_part = second_pull(cot_share)
    branch_low = lax.all_gather(grad_second.astype(jnp.bfloat16), "tensor", axis=0, tiled=True)
    grad_down_bias = jnp.sum(branch_low.astype(jnp.float32), axis=0)
    grad_down = jnp.einsum("rf,rd->fd", act_low, branch_low, preferred_element_type=jnp.float32)
    grad_act = jnp.einsum("rd,fd->rf", branch_low, down_back, preferred_element_type=jnp.float32)
    hidden_low = gelu_pull(grad_act)[0].astype(jnp.bfloat16)
    grad_up_bias = jnp.sum(hidden_low.astype(jnp.float32), axis=0).reshape(up_add.shape)
    grad_up = jnp.einsum("rd,rf->df", first_low, hidden_low, preferred_element_type=jnp.float32)
    norm_part = jnp.einsum("rf,df->rd", hidden_low, up_back, preferred_element_type=jnp.float32)
    grad_first = grad_second + lax.psum_scatter(
        norm_part, "tensor", scatter_dimension=0, tiled=True
    )
    grad_in_one, gain_one_part, shift_one_part = first_pull(grad_first)
    attn_low = lax.all_gather(grad_in_one.astype(jnp.bfloat16), "tensor", axis=0, tiled=True)
    grad_proj_bias = jnp.sum(attn_low.astype(jnp.float32), axis=0)
    grad_proj = jnp.einsum("rl,rd->ld", context_low, attn_low, preferred_element_type=jnp.float32)
    grad_context = (
        jnp.einsum("rd,ld->rl", attn_low, proj_back, preferred_element_type=jnp.float32)
        .astype(jnp.bfloat16)
        .reshape(head_shape)
    )

    def attend_backward(pieces):
        query_one, key_one, value_one, seg_query, seg_key, log_total, context_grad = pieces
        logits = masked_logits(query_one, key_one, seg_query, seg_key, score_scale)
        soft_again = jnp.exp(logits - log_total)
        grad_soft = jnp.einsum(
            "qhe,khe->hqk", context_grad, value_one, preferred_element_type=jnp.float32
        )
        row_delta = jnp.sum(grad_soft * soft_again, axis=-1, keepdims=True)
        grad_logits = (soft_again * (grad_soft - row_delta)).astype(jnp.bfloat16)
        query_grad = (
            jnp.einsum("hqk,khe->qhe", grad_logits, key_one, preferred_element_type=jnp.float32)
            * score_scale
        ).astype(jnp.bfloat16)
        key_part = (
            jnp.einsum("hqk,qhe->khe", grad_logits, query_one, preferred_element_type=jnp.float32)
            * score_scale
        )
        value_part = jnp.einsum(
            "hqk,qhe->khe",
            soft_again.astype(jnp.bfloat16),
            context_grad,
            preferred_element_type=jnp.float32,
        )
        return (query_grad, key_part, value_part)

    grad_query, key_terms, value_terms = lax.map(
        attend_backward,
        (query_heads, key_all, value_all, segment_ids, seg_all, log_totals, grad_context),
    )
    key_grad, value_grad = (
        lax.psum_scatter(
            key_terms.astype(jnp.bfloat16), "context", scatter_dimension=1, tiled=True
        ).astype(jnp.float32),
        lax.psum_scatter(
            value_terms.astype(jnp.bfloat16), "context", scatter_dimension=1, tiled=True
        ).astype(jnp.float32),
    )
    grad_stack = jnp.stack(
        [
            grad_query.reshape(total_rows, local_width),
            key_grad.astype(jnp.bfloat16).reshape(total_rows, local_width),
            value_grad.astype(jnp.bfloat16).reshape(total_rows, local_width),
        ]
    )
    stack_sums = jnp.sum(grad_stack.astype(jnp.float32), axis=1)
    grad_qv_bias = jnp.stack([stack_sums[0], stack_sums[2]]).reshape(qv_full.shape)
    grad_qkv = jnp.einsum("rd,cre->cde", token_rows, grad_stack, preferred_element_type=jnp.float32)
    input_part = jnp.einsum("cre,cde->rd", grad_stack, qkv_back, preferred_element_type=jnp.float32)
    norm_parts = jnp.tile(
        jnp.stack([gain_one_part, shift_one_part, gain_two_part, shift_two_part]),
        (lax.axis_size("tensor"), 1),
    )
    input_share, norm_sums = (
        lax.psum_scatter(
            input_part.astype(jnp.bfloat16), "tensor", scatter_dimension=0, tiled=True
        ).astype(jnp.float32),
        lax.psum_scatter(
            norm_parts.astype(jnp.bfloat16), "tensor", scatter_dimension=0, tiled=True
        ).astype(jnp.float32),
    )
    grad_share_low = (grad_in_one + input_share).astype(jnp.bfloat16)
    out_rows, grad_rows = (
        lax.all_gather(output_share.astype(jnp.bfloat16), "tensor", axis=0, tiled=True),
        lax.all_gather(grad_share_low, "tensor", axis=0, tiled=True),
    )
    local_grads = (
        grad_qkv,
        grad_qv_bias,
        grad_proj,
        grad_proj_bias,
        norm_sums[0],
        norm_sums[1],
        grad_up,
        grad_up_bias,
        grad_down,
        grad_down_bias,
        norm_sums[2],
        norm_sums[3],
    )
    summed = (
        lax.psum(local_grads[0].astype(jnp.bfloat16), "context").astype(jnp.float32),
        lax.psum(local_grads[1].astype(jnp.bfloat16), "context").astype(jnp.float32),
        lax.psum(local_grads[2].astype(jnp.bfloat16), "context").astype(jnp.float32),
        lax.psum(local_grads[3].astype(jnp.bfloat16), "context").astype(jnp.float32),
        lax.psum(local_grads[4].astype(jnp.bfloat16), "context").astype(jnp.float32),
        lax.psum(local_grads[5].astype(jnp.bfloat16), "context").astype(jnp.float32),
        lax.psum(local_grads[6].astype(jnp.bfloat16), "context").astype(jnp.float32),
        lax.psum(local_grads[7].astype(jnp.bfloat16), "context").astype(jnp.float32),
        lax.psum(local_grads[8].astype(jnp.bfloat16), "context").astype(jnp.float32),
        lax.psum(local_grads[9].astype(jnp.bfloat16), "context").astype(jnp.float32),
        lax.psum(local_grads[10].astype(jnp.bfloat16), "context").astype(jnp.float32),
        lax.psum(local_grads[11].astype(jnp.bfloat16), "context").astype(jnp.float32),
    )
    owned = (
        lax.psum_scatter(
            summed[0].astype(jnp.bfloat16), "fsdp", scatter_dimension=1, tiled=True
        ).astype(jnp.float32),
        lax.psum_scatter(
            summed[1].astype(jnp.bfloat16), "fsdp", scatter_dimension=2, tiled=True
        ).astype(jnp.float32),
        lax.psum_scatter(
            summed[2].astype(jnp.bfloat16), "fsdp", scatter_dimension=1, tiled=True
        ).astype(jnp.float32),
        lax.psum_scatter(
            summed[3].astype(jnp.bfloat16), "fsdp", scatter_dimension=0, tiled=True
        ).astype(jnp.float32),
        lax.psum_scatter(
            summed[4].astype(jnp.bfloat16), "fsdp", scatter_dimension=0, tiled=True
        ).astype(jnp.float32),
        lax.psum_scatter(
            summed[5].astype(jnp.bfloat16), "fsdp", scatter_dimension=0, tiled=True
        ).astype(jnp.float32),
        lax.psum_scatter(
            summed[6].astype(jnp.bfloat16), "fsdp", scatter_dimension=0, tiled=True
        ).astype(jnp.float32),
        lax.psum_scatter(
            summed[7].astype(jnp.bfloat16), "fsdp", scatter_dimension=1, tiled=True
        ).astype(jnp.float32),
        lax.psum_scatter(
            summed[8].astype(jnp.bfloat16), "fsdp", scatter_dimension=1, tiled=True
        ).astype(jnp.float32),
        lax.psum_scatter(
            summed[9].astype(jnp.bfloat16), "fsdp", scatter_dimension=0, tiled=True
        ).astype(jnp.float32),
        lax.psum_scatter(
            summed[10].astype(jnp.bfloat16), "fsdp", scatter_dimension=0, tiled=True
        ).astype(jnp.float32),
        lax.psum_scatter(
            summed[11].astype(jnp.bfloat16), "fsdp", scatter_dimension=0, tiled=True
        ).astype(jnp.float32),
    )
    layer_output = out_rows.reshape(seq_count, span, width)
    tokens_grad = grad_rows.reshape(seq_count, span, width)
    return (
        layer_output,
        tokens_grad,
        owned[0],
        owned[1],
        owned[2],
        owned[3],
        owned[4],
        owned[5],
        owned[6],
        owned[7],
        owned[8],
        owned[9],
        owned[10],
        owned[11],
    )


AXES = ("z", "core", "context", "tensor")
BF = jnp.bfloat16
F32 = jnp.float32
FINE = 128
MASKED = -1e30
NT = (((1,), (1,)), ((), ()))

def attn_fwd_kernel(
    lo_ref, hi_ref, shift_ref, q_ref, k_ref, v_ref, segk_ref, segq_ref, o_ref, lse_ref, vt_ref,
    *, fine, many, hd, scale,
):
    block = pl.program_id(0)
    shift = shift_ref[0]
    bq, pair = q_ref.shape
    pieces = k_ref.shape[0] // fine
    heads = pair // hd

    @pl.when(block == 0)
    def _():
        for j in range(pieces):
            vt_ref[j] = v_ref[j * fine : (j + 1) * fine, :].T

    at = lax.rem(block + shift // (bq // fine), pieces * fine // bq)
    low, high = lo_ref[at], hi_ref[at]
    lane = lax.broadcasted_iota(jnp.int32, (bq, pair), 1) // hd
    q = q_ref[...] * jnp.asarray(scale, BF)
    qs = [jnp.where(lane == h, q, jnp.zeros_like(q)) for h in range(heads)]
    seg_q = segq_ref[0:1, :]

    def body(i, carry):
        j = low + i * many
        spots = [lax.rem(j + u + shift, pieces) for u in range(many)]
        keys = jnp.concatenate([k_ref[aligned(spot * fine, fine), :] for spot in spots])
        values_t = jnp.concatenate([vt_ref[spot] for spot in spots], axis=1)
        seg_k = jnp.concatenate(
            [
                jnp.where(j + u < high, segk_ref[aligned(spot * fine, fine), :], -1)
                for u, spot in enumerate(spots)
            ]
        )
        same = jnp.concatenate([seg_k] * (bq // seg_k.shape[1]), axis=1) == seg_q
        scores = [jnp.where(same, mm_nt(keys, qs[h]), MASKED) for h in range(heads)]
        out = []
        for h in range(heads):
            top, total, acc = carry[h]
            new_top = jnp.maximum(top, jnp.max(scores[h], axis=0, keepdims=True))
            weights = jnp.exp(scores[h] - new_top)
            fade = jnp.exp(top - new_top)
            total = total * fade + jnp.sum(weights, axis=0, keepdims=True)
            acc = acc * fade + mm(values_t[h * hd : (h + 1) * hd, :], weights.astype(BF))
            out.append((new_top, total, acc))
        return tuple(out)

    init = (jnp.full((1, bq), MASKED, F32), jnp.zeros((1, bq), F32), jnp.zeros((hd, bq), F32))
    done = lax.fori_loop(0, (high - low + many - 1) // many, body, (init,) * heads)
    o_ref[...] = jnp.concatenate([acc / total for _, total, acc in done], axis=0).T.astype(BF)
    lse_ref[0] = jnp.concatenate([top + jnp.log(total) for top, total, _ in done], axis=0)


def attn_bwd_kernel(
    lo_ref, hi_ref, shift_ref, q_ref, k_ref, v_ref, o_ref, do_ref, lse_ref, segk_ref, segq_ref, out_ref,
    qs_ref, dos_ref, kt_ref, delta_ref, dqt_ref, dk_ref, dv_ref,
    *, bk, fine, many, hd, scale,
):
    w = pl.program_id(1)
    shift = shift_ref[0]
    rows, pair = q_ref.shape
    pieces = rows // fine
    blocks = rows // bk
    heads = pair // hd

    @pl.when(w == 0)
    def _():
        lane = lax.broadcasted_iota(jnp.int32, (bk, pair), 1) // hd
        head = lax.broadcasted_iota(jnp.int32, (8, pair), 0)
        pick = (head == lax.broadcasted_iota(jnp.int32, (8, pair), 1) // hd).astype(F32)
        factor = jnp.asarray(scale, BF)
        for j in range(blocks):
            r = slice(j * bk, (j + 1) * bk)
            q = q_ref[r, :] * factor
            do = do_ref[r, :]
            for h in range(heads):
                qs_ref[h, r, :] = jnp.where(lane == h, q, jnp.zeros_like(q))
                dos_ref[h, r, :] = jnp.where(lane == h, do, jnp.zeros_like(do))
            kt_ref[j] = (k_ref[r, :] * factor).T
            prod = do.astype(F32) * o_ref[r, :].astype(F32)
            delta_ref[:, r] = lax.dot_general(
                pick, prod, NT, preferred_element_type=F32, precision=lax.Precision.HIGHEST
            )
        dqt_ref[...] = jnp.zeros(dqt_ref.shape, F32)

        def outer(block, _):
            at = lax.rem(block + shift // (bk // fine), blocks)
            low, high = lo_ref[at], hi_ref[at]
            r = aligned(block * bk, bk)
            keys, values = k_ref[r, :], v_ref[r, :]
            seg_k = jnp.concatenate([segk_ref[r, :]] * (many * fine // segk_ref.shape[1]), axis=1)

            def inner(i, carry):
                dk, dv = carry
                j = low + i * many
                spots = [lax.rem(j + u + shift, pieces) for u in range(many)]
                cuts = [aligned(spot * fine, fine) for spot in spots]
                seg_q = jnp.concatenate(
                    [jnp.where(j + u < high, segq_ref[0:1, cut], -1) for u, cut in enumerate(cuts)], axis=1
                )
                same = seg_k == seg_q
                q = [jnp.concatenate([qs_ref[h, cut, :] for cut in cuts]) for h in range(heads)]
                do = [jnp.concatenate([dos_ref[h, cut, :] for cut in cuts]) for h in range(heads)]
                lse = jnp.concatenate([lse_ref[0, :, cut] for cut in cuts], axis=1)
                delta = jnp.concatenate([delta_ref[:, cut] for cut in cuts], axis=1)
                scores = [mm_nt(keys, q[h]) for h in range(heads)]
                dp = [mm_nt(values, do[h]) for h in range(heads)]
                p = [jnp.exp(jnp.where(same, scores[h] - lse[h : h + 1, :], MASKED)) for h in range(heads)]
                p_low = [p[h].astype(BF) for h in range(heads)]
                ds = [(p[h] * (dp[h] - delta[h : h + 1, :])).astype(BF) for h in range(heads)]
                for h in range(heads):
                    hs = slice(h * hd, (h + 1) * hd)
                    dv = dv + mm(p_low[h], do[h])
                    dk = dk + mm(ds[h], q[h])
                    dq = mm(kt_ref[block, hs, :], ds[h])
                    for u in range(many):
                        dqt_ref[spots[u], hs, :] += dq[:, u * fine : (u + 1) * fine]
                return dk, dv

            zero = jnp.zeros((bk, pair), F32)
            dk, dv = lax.fori_loop(0, (high - low + many - 1) // many, inner, (zero, zero))
            dk_ref[r, :] = dk.astype(BF)
            dv_ref[r, :] = dv.astype(BF)
            return 0

        lax.fori_loop(0, blocks, outer, 0)
        for j in range(pieces):
            out_ref[j * fine : (j + 1) * fine, :] = dqt_ref[j].T.astype(BF)

    @pl.when(w == 1)
    def _():
        out_ref[...] = dk_ref[...]

    @pl.when(w == 2)
    def _():
        out_ref[...] = dv_ref[...]


def pair_block(which, pair, group):
    return (pair // group) * 3 * group + which * group + pair % group


def attn_fwd(qkv, seg_k, seg_q, low, high, shift, pair, pairs, group, head_size, bq, many):
    rows, wide = qkv.shape[0], 2 * head_size
    spec = lambda which: pair_block(which, pair, group)
    return pl.pallas_call(
        functools.partial(
            attn_fwd_kernel, fine=FINE, many=many, hd=head_size, scale=float(head_size) ** -0.5
        ),
        out_shape=(
            jax.ShapeDtypeStruct((rows, wide), BF),
            jax.ShapeDtypeStruct((1, 2, rows), F32),
        ),
        grid_spec=pltpu.PrefetchScalarGridSpec(
            num_scalar_prefetch=3,
            grid=(rows // bq,),
            in_specs=[
                pl.BlockSpec((bq, wide), lambda i, *_: (i, spec(0))),
                pl.BlockSpec((rows, wide), lambda i, *_: (0, spec(1))),
                pl.BlockSpec((rows, wide), lambda i, *_: (0, spec(2))),
                pl.BlockSpec((rows, 128), lambda i, *_: (0, 0)),
                pl.BlockSpec((8, bq), lambda i, *_: (0, i)),
            ],
            out_specs=(
                pl.BlockSpec((bq, wide), lambda i, *_: (i, 0)),
                pl.BlockSpec((1, 2, bq), lambda i, *_: (0, 0, i)),
            ),
            scratch_shapes=[pltpu.VMEM((rows // FINE, wide, FINE), BF)],
        ),
        compiler_params=pltpu.CompilerParams(vmem_limit_bytes=24 << 20),
        cost_estimate=pl.CostEstimate(
            flops=15_000_000_000, bytes_accessed=rows * wide * 8, transcendentals=rows * rows // 2
        ),
        name="attn_fwd",
    )(low, high, shift, qkv, qkv, qkv, seg_k, seg_q)


def attn_bwd(qkv, mixed, dctx, lse, seg_k, seg_q, low, high, shift, pairs, group, head_size, bk, many):
    rows, wide = qkv.shape[0], 2 * head_size
    blocks = rows // bk
    column = lambda which: pl.BlockSpec((rows, wide), lambda p, w, *_: (0, pair_block(which, p, group)))
    own = pl.BlockSpec((rows, wide), lambda p, w, *_: (0, p))
    return pl.pallas_call(
        functools.partial(
            attn_bwd_kernel, bk=bk, fine=FINE, many=many, hd=head_size, scale=float(head_size) ** -0.5
        ),
        out_shape=jax.ShapeDtypeStruct(qkv.shape, BF),
        grid_spec=pltpu.PrefetchScalarGridSpec(
            num_scalar_prefetch=3,
            grid=(pairs, 3),
            in_specs=[
                column(0),
                column(1),
                column(2),
                own,
                own,
                pl.BlockSpec((1, 2, rows), lambda p, w, *_: (p, 0, 0)),
                pl.BlockSpec((rows, 128), lambda p, w, *_: (0, 0)),
                pl.BlockSpec((8, rows), lambda p, w, *_: (0, 0)),
            ],
            out_specs=pl.BlockSpec((rows, wide), lambda p, w, *_: (0, pair_block(w, p, group))),
            scratch_shapes=[
                pltpu.VMEM((2, rows, wide), BF),
                pltpu.VMEM((2, rows, wide), BF),
                pltpu.VMEM((blocks, wide, bk), BF),
                pltpu.VMEM((8, rows), F32),
                pltpu.VMEM((rows // FINE, wide, FINE), F32),
                pltpu.VMEM((rows, wide), BF),
                pltpu.VMEM((rows, wide), BF),
            ],
        ),
        compiler_params=pltpu.CompilerParams(vmem_limit_bytes=58 << 20),
        cost_estimate=pl.CostEstimate(
            flops=100_000_000_000, bytes_accessed=rows * wide * 64, transcendentals=2 * rows * rows
        ),
        name="attn_bwd",
    )(low, high, shift, qkv, qkv, qkv, mixed, dctx, lse, seg_k, seg_q)


def segment_bounds(seg_rows, row_block, col_block):
    blocks = seg_rows.reshape(-1, row_block)
    low = jnp.sum(seg_rows[None, :] < blocks[:, :1], axis=1) // col_block
    high = (jnp.sum(seg_rows[None, :] <= blocks[:, -1:], axis=1) + col_block - 1) // col_block
    return low.astype(jnp.int32), high.astype(jnp.int32)


def norm_forward(rows):
    mean = jnp.mean(rows, axis=-1, keepdims=True)
    centred = rows - mean
    inv = lax.rsqrt(jnp.mean(centred * centred, axis=-1, keepdims=True) + NORM_EPS)
    return centred * inv, inv


def norm_backward(grad, normed, inv):
    return inv * (
        grad
        - jnp.mean(grad, axis=-1, keepdims=True)
        - normed * jnp.mean(grad * normed, axis=-1, keepdims=True)
    )


def after(value, *others):
    return lax.optimization_barrier((value,) + others)[0]


def mm(a, b):
    return jnp.dot(a, b, preferred_element_type=F32)


def mm_nt(a, b):
    return lax.dot_general(a, b, (((1,), (1,)), ((), ())), preferred_element_type=F32)


def mm_tn(a, b):
    return lax.dot_general(a, b, (((0,), (0,)), ((), ())), preferred_element_type=F32)


def remote(src, dst, send_sem, recv_sem, device):
    return pltpu.make_async_remote_copy(
        src_ref=src,
        dst_ref=dst,
        send_sem=send_sem,
        recv_sem=recv_sem,
        device_id=device,
        device_id_type=pl.DeviceIdType.MESH,
    )


def greet(devices):
    barrier = pltpu.get_barrier_semaphore()
    for device in devices:
        pl.semaphore_signal(barrier, inc=1, device_id=device, device_id_type=pl.DeviceIdType.MESH)
    pl.semaphore_wait(barrier, len(devices))


def aligned(start, size):
    return pl.ds(pl.multiple_of(start, size), size)


def open_kernel(
    tokens, weight, small, xt_out, w_out, qkv_out, small_out,
    x, xt, w, qkv, smalls, fill_x, fill_w, x_send, x_recv, s_send, s_recv, y_sems, z_send, z_recv,
    c_send, c_recv, out_sems,
    *, nz, nt, heads, head_size, group, chunk,
):
    z, k, c, t = (lax.axis_index(name) for name in AXES)
    f = z * 2 + k
    nf = nz * 2
    span, width = tokens.shape[1:]
    dblk = weight.shape[1]
    cols = heads * head_size
    gw = group * 2 * head_size
    chunks = span // chunk
    peers = [
        (dz, dk, dt) for dz in range(nz) for dk in range(2) for dt in range(nt) if (dz, dk, dt) != (0, 0, 0)
    ]

    def peer(offset):
        dz, dk, dt = offset
        return {"z": lax.rem(z + dz, nz), "core": lax.rem(k + dk, 2), "tensor": lax.rem(t + dt, nt)}

    def block(index):
        return w.at[aligned(index * dblk, dblk), :]

    for i in range(chunks):
        r = pl.ds(i * chunk, chunk)
        pltpu.make_async_copy(tokens.at[t, r], x.at[r], fill_x.at[i]).start()
    fills = []
    for g in range(cols // gw):
        for which in range(3):
            at = (g * 3 + which) * gw
            fills.append(
                pltpu.make_async_copy(
                    weight.at[which, :, pl.ds(g * gw, gw)],
                    w.at[aligned(f * dblk, dblk), pl.ds(at, gw)],
                    fill_w.at[len(fills)],
                )
            )

    @pl.when(c == t)
    def _():
        for one in fills:
            one.start()

    greet([{"context": 1 - c}] + [peer(offset) for offset in peers])
    x_copies = [
        remote(
            tokens.at[t, pl.ds(i * chunk, chunk)],
            x.at[pl.ds(span + i * chunk, chunk)],
            x_send.at[i],
            x_recv.at[i],
            {"context": 1 - c},
        )
        for i in range(chunks)
    ]
    for one in x_copies:
        one.start()
    y_copy = remote(block(f), block(f), y_sems.at[0], y_sems.at[1], {"tensor": 1 - t})

    @pl.when(c == t)
    def _():
        for one in fills:
            one.wait()
        y_copy.start()

    def small_copy(i, source):
        return remote(small, smalls.at[source], s_send.at[i], s_recv.at[source], peer(peers[i]))

    me = f * nt + t
    for i in range(len(peers)):
        small_copy(i, me).start()
    smalls[me] = small[...]

    @pl.when(c != t)
    def _():
        y_copy.wait_recv()

    def z_copy(d, owner):
        return remote(
            block(owner * 2 + k), block(owner * 2 + k), z_send.at[d - 1], z_recv.at[owner], {"z": lax.rem(z + d, nz)}
        )

    def c_copy(owner, core):
        return remote(
            block(owner * 2 + core), block(owner * 2 + core), c_send.at[owner], c_recv.at[owner], {"core": 1 - k}
        )

    for d in range(1, nz):
        z_copy(d, z).start()
    c_copy(z, k).start()

    for i in range(chunks):
        r = pl.ds(i * chunk, chunk)
        pltpu.make_async_copy(tokens.at[t, r], x.at[r], fill_x.at[i]).wait()
        xt[:, i * chunk : (i + 1) * chunk] = x[i * chunk : (i + 1) * chunk, :].T

    for i in range(len(peers)):
        dz, dk, dt = peers[i]
        source = (lax.rem(z + nz - dz, nz) * 2 + lax.rem(k + dk, 2)) * nt + lax.rem(t + nt - dt, nt)
        small_copy(i, source).wait_recv()

    edge = head_size // nf
    lanes = small.shape[1]
    rows = jnp.concatenate([smalls[fi * nt + c, 0:1, :] for fi in range(nf)], axis=0)
    col = lax.broadcasted_iota(jnp.int32, (lanes, cols), 1)
    source = lax.broadcasted_iota(jnp.int32, (lanes, cols), 0)
    fcol = lax.broadcasted_iota(jnp.int32, (nf, cols), 1)
    mine = lax.rem(fcol, head_size) // edge == lax.broadcasted_iota(jnp.int32, (nf, cols), 0)
    biases = []
    for kind in range(2):
        pick = source == col // head_size * edge + lax.rem(col, edge) + kind * heads * edge
        spread_out = mm(rows, jnp.where(pick, 1.0, 0.0).astype(BF))
        biases.append(jnp.sum(jnp.where(mine, spread_out, 0.0), axis=0, keepdims=True))
    parts = [biases[0], jnp.zeros_like(biases[0]), biases[1]]
    bias = jnp.concatenate(
        [parts[which][:, g * gw : (g + 1) * gw] for g in range(cols // gw) for which in range(3)], axis=1
    )

    for d in range(1, nz):
        owner = lax.rem(z + nz - d, nz)
        z_copy(d, owner).wait_recv()
        c_copy(owner, k).start()
    for owner in range(nz):
        c_copy(owner, 1 - k).wait_recv()

    w_done = pltpu.make_async_copy(w, w_out, out_sems.at[0, 0])
    w_done.start()
    small_done = pltpu.make_async_copy(smalls, small_out, out_sems.at[0, 1])
    small_done.start()

    def project(i):
        r = aligned(i * chunk, chunk)
        acc = mm(x[r, :], w[...]) + bias
        qkv[r, :] = acc.astype(BF)
        pltpu.make_async_copy(qkv.at[r], qkv_out.at[r], out_sems.at[1, i]).start()

    @pl.loop(0, chunks)
    def _(i):
        project(i)

    @pl.loop(0, chunks)
    def _(i):
        remote(
            tokens.at[t, aligned(i * chunk, chunk)],
            x.at[aligned(span + i * chunk, chunk)],
            x_send.at[i],
            x_recv.at[i],
            {"context": 1 - c},
        ).wait_recv()
        r = aligned(span + i * chunk, chunk)
        xt[:, r] = x[r, :].T
        project(chunks + i)

    xt_done = pltpu.make_async_copy(xt, xt_out, out_sems.at[0, 2])
    xt_done.start()
    for i in range(2 * chunks):
        r = pl.ds(i * chunk, chunk)
        pltpu.make_async_copy(qkv.at[r], qkv_out.at[r], out_sems.at[1, i]).wait()
    for one in (w_done, small_done, xt_done):
        one.wait()
    for one in x_copies:
        one.wait_send()
    for i in range(len(peers)):
        small_copy(i, me).wait_send()
    for d in range(1, nz):
        z_copy(d, z).wait_send()
    for owner in range(nz):
        c_copy(owner, k).wait_send()

    @pl.when(c == t)
    def _():
        y_copy.wait_send()


def open_layer(tokens, weight, small, nz, nt, heads, head_size, group):
    span, width = tokens.shape[1:]
    cols = heads * head_size
    chunk = 256
    chunks = span // chunk
    nf = nz * 2
    dma = pltpu.SemaphoreType.DMA
    hbm = pl.BlockSpec(memory_space=pl.ANY)
    fixed = pl.BlockSpec(memory_space=pltpu.HBM)
    moved = 2 * (span * width * 2 + 4 * width * cols * 3)
    return pl.pallas_call(
        functools.partial(
            open_kernel, nz=nz, nt=nt, heads=heads, head_size=head_size, group=group, chunk=chunk
        ),
        out_shape=(
            jax.ShapeDtypeStruct((width, 2 * span), BF),
            jax.ShapeDtypeStruct((width, 3 * cols), BF),
            jax.ShapeDtypeStruct((2 * span, 3 * cols), BF),
            jax.ShapeDtypeStruct((nf * nt,) + small.shape, BF),
        ),
        in_specs=[fixed, fixed, pl.BlockSpec(memory_space=pltpu.VMEM)],
        out_specs=(hbm,) * 4,
        scratch_shapes=[
            pltpu.VMEM((2 * span, width), BF),
            pltpu.VMEM((width, 2 * span), BF),
            pltpu.VMEM((width, 3 * cols), BF),
            pltpu.VMEM((2 * span, 3 * cols), BF),
            pltpu.VMEM((nf * nt,) + small.shape, BF),
            dma((chunks,)),
            dma((heads // 2 // group * 3,)),
            dma((chunks,)),
            dma((chunks,)),
            dma((nf * nt,)),
            dma((nf * nt,)),
            dma((2,)),
            dma((nz,)),
            dma((nz,)),
            dma((nz,)),
            dma((nz,)),
            dma((2, max(3, 2 * chunks))),
        ],
        compiler_params=pltpu.CompilerParams(
            collective_id=0, has_side_effects=True, vmem_limit_bytes=58 << 20
        ),
        cost_estimate=pl.CostEstimate(
            flops=2 * 2 * span * width * 3 * cols, bytes_accessed=moved, transcendentals=0
        ),
        name="open_layer",
    )(tokens, weight, small)


def close_kernel(
    dqkv_in, w_in, xt_in, grad_in, vec_one, vec_two, tokens_out, grad_out, sums_out, vec_out,
    dqkv, w, xt, dres, own, xs, xr, fin, away, near, zs, zr, piece, last,
    sums, sums_near, sums_z, sums_last, vecs, vecs_near, vecs_z, vecs_last,
    fill, x_send, x_recv, y_send, y_recv, c_send, c_recv, z_send, z_recv, p_send, p_recv, o_sems,
    *, nz, chunk, tile, part,
):
    z, k, c, t = (lax.axis_index(name) for name in AXES)
    rows, wide = dqkv.shape
    span = rows // 2
    dblk = piece.shape[0]
    chunks = span // chunk
    steps = wide // tile
    x_dev, y_dev, core_dev = {"context": 1 - c}, {"tensor": 1 - t}, {"core": 1 - k}
    diag = {"context": 1 - c, "tensor": 1 - t}

    loads = [
        pltpu.make_async_copy(w_in, w, fill.at[0]),
        pltpu.make_async_copy(dqkv_in.at[pl.ds(span, span)], dqkv.at[pl.ds(span, span)], fill.at[1]),
        pltpu.make_async_copy(dqkv_in.at[pl.ds(0, span)], dqkv.at[pl.ds(0, span)], fill.at[2]),
    ]
    for kk in range(2):
        for zi in range(nz):
            source = zi * 2 + lax.rem(1 - k + kk, 2)
            loads.append(
                pltpu.make_async_copy(
                    xt_in.at[aligned(source * dblk, dblk)], xt.at[kk, pl.ds(zi * dblk, dblk)], fill.at[len(loads)]
                )
            )
    for source, dest in (
        (grad_in, dres),
        (vec_one, vecs.at[pl.ds(0, 8)]),
        (vec_two, vecs.at[pl.ds(8, 8)]),
    ):
        loads.append(pltpu.make_async_copy(source, dest, fill.at[len(loads)]))
    for one in loads:
        one.start()
    greet([x_dev, y_dev, diag, core_dev] + [{"z": lax.rem(z + d, nz)} for d in range(1, nz)])

    def x_copy(i):
        return remote(xs.at[i], xr.at[i], x_send.at[i], x_recv.at[i], x_dev)

    def y_copy(i):
        return remote(fin.at[i], tokens_out.at[t, aligned(i * chunk, chunk)], y_send.at[i], y_recv.at[i], y_dev)

    def leave(i):
        value = mm_nt(dqkv[aligned(span + i * 2 * chunk, 2 * chunk), :], w[...]).astype(BF)
        xs[2 * i] = value[:chunk]
        xs[2 * i + 1] = value[chunk:]
        x_copy(2 * i).start()
        x_copy(2 * i + 1).start()

    loads[0].wait()
    loads[1].wait()

    @pl.loop(0, 1)
    def _(i):
        leave(i)

    for one in loads[2:]:
        one.wait()
    ones = jnp.ones((8, rows), BF)
    sums[...] = jnp.zeros(sums.shape, F32)

    @pl.loop(0, steps)
    def _(j):
        value = dqkv[:, aligned(j * tile, tile)]
        away[:, aligned(j * tile, tile)] = mm(xt[0], value).astype(BF)
        total = mm(ones, value)
        for u in range(tile // 128):
            sums[pl.ds(j * (tile // 128) + u, 1), :] = total[0:1, u * 128 : (u + 1) * 128]

    core_copies = [
        remote(mine, theirs, c_send.at[i], c_recv.at[i], core_dev)
        for i, (mine, theirs) in enumerate(((away, near), (sums, sums_near), (vecs, vecs_near)))
    ]
    for one in core_copies:
        one.start()

    @pl.loop(1, chunks // 2)
    def _(i):
        leave(i)

    for one in core_copies:
        one.wait_recv()
    sums_z[z] = sums[...] + sums_near[...]
    vecs_z[z] = vecs[...] + vecs_near[...]

    @pl.loop(0, steps)
    def _(j):
        cut = aligned(j * tile, tile)
        zs[:, cut] = (mm(xt[1], dqkv[:, cut]) + near[:, cut].astype(F32)).astype(BF)

    def z_copies(d, owner):
        dev = {"z": lax.rem(z + d, nz)}
        return [
            remote(buf.at[owner], buf.at[owner], z_send.at[i, d - 1], z_recv.at[i, owner], dev)
            for i, buf in enumerate((sums_z, vecs_z))
        ]

    def ring(step):
        source = zs.at[aligned(lax.rem(z + nz - step, nz) * dblk, dblk)]
        return remote(source, zr.at[step - 1], z_send.at[2, step - 1], z_recv.at[2, step - 1], {"z": lax.rem(z + 1, nz)})

    def arrived(step):
        ring(step).wait_recv()
        spot = aligned(lax.rem(z + 2 * nz - step - 1, nz) * dblk, dblk)
        zs[spot, :] = (zs[spot, :].astype(F32) + zr[step - 1].astype(F32)).astype(BF)
        if step + 1 < nz:
            ring(step + 1).start()

    ring(1).start()
    for d in range(1, nz):
        for one in z_copies(d, z):
            one.start()

    @pl.loop(0, chunks // 2)
    def _(i):
        r = aligned(i * 2 * chunk, 2 * chunk)
        own[r, :] = mm_nt(dqkv[r, :], w[...]) + dres[r, :]

    def finish(i):
        x_copy(i).wait_recv()
        r = aligned(i * chunk, chunk)
        fin[i] = (own[r, :] + xr[i].astype(F32)).astype(BF)
        pltpu.make_async_copy(fin.at[i], tokens_out.at[t, r], o_sems.at[i]).start()
        y_copy(i).start()

    cuts = [chunks * step // nz for step in range(nz + 1)]
    for step in range(1, nz):
        pl.loop(cuts[step - 1], cuts[step])(finish)
        arrived(step)
    for d in range(1, nz):
        for one in z_copies(d, lax.rem(z + nz - d, nz)):
            one.wait_recv()
    piece[...] = zs[aligned(z * dblk, dblk), :]
    sums_last[0] = jnp.sum(sums_z[...], axis=0)
    vecs_last[0] = jnp.sum(vecs_z[...], axis=0)

    trio = ((x_dev, 0), (y_dev, 1), (diag, 2))
    p_x, p_y, p_d = (remote(piece, last.at[i], p_send.at[i], p_recv.at[i], dev) for dev, i in trio)
    everywhere = [
        remote(buf.at[0], buf.at[1 + i], p_send.at[at + i], p_recv.at[at + i], dev)
        for dev, i in trio
        for buf, at in ((sums_last, 3), (vecs_last, 6))
    ]
    for one in everywhere:
        one.start()

    @pl.when(c == t)
    def _():
        p_x.start()

    @pl.when(c != t)
    def _():
        p_y.start()
        p_d.start()

    pl.loop(cuts[nz - 1], chunks)(finish)

    def give(value):
        width = part
        for g in range(wide // (3 * width)):
            for which in range(3):
                at = (g * 3 + which) * width
                grad_out[which, :, g * width : (g + 1) * width] = value[:, at : at + width]

    for one in everywhere:
        one.wait()
    near_pair = sums_last[0] + sums_last[2]
    sums_out[...] = jnp.where(c == t, near_pair, sums_last[1] + sums_last[3])
    vec_out[...] = (vecs_last[0] + vecs_last[2]) + (vecs_last[1] + vecs_last[3])

    @pl.when(c == t)
    def _():
        p_y.wait_recv()
        give(piece[...].astype(F32) + last[1].astype(F32))
        p_x.wait_send()

    @pl.when(c != t)
    def _():
        p_x.wait_recv()
        p_d.wait_recv()
        give(last[0].astype(F32) + last[2].astype(F32))
        p_y.wait_send()
        p_d.wait_send()

    for one in core_copies:
        one.wait_send()
    for d in range(1, nz):
        ring(d).wait_send()
        for one in z_copies(d, z):
            one.wait_send()

    @pl.loop(0, chunks)
    def _(i):
        r = aligned(i * chunk, chunk)
        x_copy(i).wait_send()
        pltpu.make_async_copy(fin.at[i], tokens_out.at[t, r], o_sems.at[i]).wait()
        y_copy(i).wait_send()
        remote(fin.at[i], tokens_out.at[1 - t, r], y_send.at[i], y_recv.at[i], y_dev).wait_recv()


def close_layer(dqkv, w, xt, grad_in, vec_one, vec_two, nz, part):
    rows, wide = dqkv.shape
    width = w.shape[0]
    span = rows // 2
    dblk = width // (2 * nz)
    chunk, tile = 128, 256
    chunks = span // chunk
    dma = pltpu.SemaphoreType.DMA
    hbm = pl.BlockSpec(memory_space=pl.ANY)
    vmem = pl.BlockSpec(memory_space=pltpu.VMEM)
    sum_shape = (wide // 128 + -(wide // 128) % 8, 128)
    vec_shape = (16, width)
    return pl.pallas_call(
        functools.partial(close_kernel, nz=nz, chunk=chunk, tile=tile, part=part),
        out_shape=(
            jax.ShapeDtypeStruct((2, span, width), BF),
            jax.ShapeDtypeStruct((3, dblk, wide // 3), F32),
            jax.ShapeDtypeStruct(sum_shape, F32),
            jax.ShapeDtypeStruct(vec_shape, F32),
        ),
        in_specs=[hbm] * 6,
        out_specs=(hbm, vmem, vmem, vmem),
        scratch_shapes=[
            pltpu.VMEM((rows, wide), BF),
            pltpu.VMEM((width, wide), BF),
            pltpu.VMEM((2, nz * dblk, rows), BF),
            pltpu.VMEM((span, width), F32),
            pltpu.VMEM((span, width), F32),
            pltpu.VMEM((chunks, chunk, width), BF),
            pltpu.VMEM((chunks, chunk, width), BF),
            pltpu.VMEM((chunks, chunk, width), BF),
            pltpu.VMEM((nz * dblk, wide), BF),
            pltpu.VMEM((nz * dblk, wide), BF),
            pltpu.VMEM((nz * dblk, wide), BF),
            pltpu.VMEM((nz, dblk, wide), BF),
            pltpu.VMEM((dblk, wide), BF),
            pltpu.VMEM((3, dblk, wide), BF),
            pltpu.VMEM(sum_shape, F32),
            pltpu.VMEM(sum_shape, F32),
            pltpu.VMEM((nz,) + sum_shape, F32),
            pltpu.VMEM((4,) + sum_shape, F32),
            pltpu.VMEM(vec_shape, F32),
            pltpu.VMEM(vec_shape, F32),
            pltpu.VMEM((nz,) + vec_shape, F32),
            pltpu.VMEM((4,) + vec_shape, F32),
            dma((6 + 2 * nz,)),
            dma((chunks,)),
            dma((chunks,)),
            dma((chunks,)),
            dma((chunks,)),
            dma((3,)),
            dma((3,)),
            dma((3, nz)),
            dma((3, nz)),
            dma((9,)),
            dma((9,)),
            dma((chunks,)),
        ],
        compiler_params=pltpu.CompilerParams(
            collective_id=1, has_side_effects=True, vmem_limit_bytes=46 << 20
        ),
        cost_estimate=pl.CostEstimate(
            flops=4 * rows * width * wide, bytes_accessed=30 << 20, transcendentals=0
        ),
        name="close_layer",
    )(dqkv, w, xt, grad_in, vec_one, vec_two)


def mean_of(rows):
    return jnp.mean(rows, axis=-1, keepdims=True)


def load_blocks(stack, start, dest, sems, nt, rows_by_f):
    count, rows = stack.shape[:2]
    columns = dest.shape[1] // nt if rows_by_f else stack.shape[2]
    copies = []
    for b in range(count):
        first, second = (b // nt, b % nt) if rows_by_f else (b % nt, b // nt)
        spot = dest.at[pl.ds(first * rows, rows), pl.ds(second * columns, columns)]
        copies.append(pltpu.make_async_copy(stack.at[b, :, pl.ds(start, columns)], spot, sems.at[b]))
    return copies


def up_kernel(
    t_ref, ctx, tok, vecs, up_add, up_in, first, norm_one, inv_one, first_t, act, slope,
    up, proj, low, u, fill,
    *, nt, tile,
):
    i = pl.program_id(0)
    width, hidden = up.shape
    tiles = hidden // tile
    up_fill = load_blocks(up_in, 0, up, fill.at[0], nt, True)
    proj_fill = load_blocks(up_in, hidden // nt, proj, fill.at[1], nt, True)

    @pl.when(i == 0)
    def _():
        for one in proj_fill + up_fill:
            one.start()
        for one in proj_fill:
            one.wait()

    def vec(row):
        return vecs[row : row + 1, :]

    h = tok[0].astype(F32) + (mm_nt(ctx[...], proj[...]) + vec(0))
    centred = h - mean_of(h)
    inv = lax.rsqrt(mean_of(centred * centred) + NORM_EPS)
    normed = centred * inv
    norm_one[...] = normed
    inv_one[...] = jnp.broadcast_to(inv, inv_one.shape)
    normed = normed * vec(1) + vec(2)
    first[...] = normed
    low[...] = normed.astype(BF)
    first_t[...] = low[...].T

    @pl.when(i == 0)
    def _():
        for one in up_fill:
            one.wait()

    u[0] = mm(low[...], up[:, :tile])

    def activate(j, slot):
        cut = aligned(j * tile, tile)
        value = u[slot] + up_add[0:1, cut]
        phi = 0.5 + 0.5 * lax.erf(value * (0.5**0.5))
        act[:, cut] = (value * phi).astype(BF)
        slope[:, cut] = (phi + value * (jnp.exp(-0.5 * value * value) * ((2.0 * jnp.pi) ** -0.5))).astype(BF)

    @pl.loop(0, tiles - 1)
    def _(j):
        slot = lax.rem(j, 2)
        following = mm(low[...], up[:, aligned((j + 1) * tile, tile)])
        activate(j, slot)
        u[1 - slot] = following

    activate(tiles - 1, (tiles - 1) % 2)


def up_layer(t, ctx, tokens, vecs, up_add, up_all, nt):
    span, width = ctx.shape
    hidden = up_add.shape[1]
    block, tile = 512, 512
    hbm = pl.BlockSpec(memory_space=pl.ANY)
    rows = pl.BlockSpec((block, width), lambda i, _: (i, 0))
    wide = pl.BlockSpec((block, hidden), lambda i, _: (i, 0))
    whole = lambda shape: pl.BlockSpec(shape, lambda i, _: (0,) * len(shape))
    picked = pl.BlockSpec((1, block, width), lambda i, t_ref: (t_ref[0], i, 0))
    sds = jax.ShapeDtypeStruct
    return pl.pallas_call(
        functools.partial(up_kernel, nt=nt, tile=tile),
        out_shape=(
            sds((span, width), F32),
            sds((span, width), F32),
            sds((span, 128), F32),
            sds((width, span), BF),
            sds((span, hidden), BF),
            sds((span, hidden), BF),
        ),
        grid_spec=pltpu.PrefetchScalarGridSpec(
            num_scalar_prefetch=1,
            grid=(span // block,),
            in_specs=[rows, picked, whole(vecs.shape), whole(up_add.shape), hbm],
            out_specs=(
                rows,
                rows,
                pl.BlockSpec((block, 128), lambda i, _: (i, 0)),
                pl.BlockSpec((width, block), lambda i, _: (0, i)),
                wide,
                wide,
            ),
            scratch_shapes=[
                pltpu.VMEM((width, hidden), BF),
                pltpu.VMEM((width, width), BF),
                pltpu.VMEM((block, width), BF),
                pltpu.VMEM((2, block, tile), F32),
                pltpu.SemaphoreType.DMA((2, up_all.shape[0])),
            ],
        ),
        compiler_params=pltpu.CompilerParams(vmem_limit_bytes=60 << 20),
        cost_estimate=pl.CostEstimate(
            flops=2 * span * width * (width + hidden), bytes_accessed=40 << 20, transcendentals=2 * span * hidden
        ),
        name="up_layer",
    )(t, ctx, tokens, vecs, up_add, up_all)


def add_rows(sums, row, value):
    sums[row] += jnp.sum(value.reshape(-1, 8, value.shape[1]), axis=0)


def down_kernel(
    t_ref, cot, vecs, first, act, down_in, out, branch, branch_t, grad_second, vec_sums,
    down, acc, sums, fill,
    *, nt,
):
    i = pl.program_id(0)
    hidden, width = down.shape
    down_fill = load_blocks(down_in, 0, down, fill, nt, False)

    @pl.when(i == 0)
    def _():
        for one in down_fill:
            one.start()
        sums[...] = jnp.zeros(sums.shape, F32)
        for one in down_fill:
            one.wait()

    def vec(row):
        return vecs[row : row + 1, :]

    tile = 256

    @pl.loop(0, width // tile)
    def _(j):
        cut = aligned(j * tile, tile)
        acc[:, cut] = mm(act[...], down[:, cut])

    h = first[...] + (acc[...] + vec(3))
    centred = h - mean_of(h)
    inv = lax.rsqrt(mean_of(centred * centred) + NORM_EPS)
    normed = centred * inv
    out[...] = (normed * vec(4) + vec(5)).astype(BF)
    grad = cot[0].astype(F32)
    add_rows(sums, 1, grad * normed)
    add_rows(sums, 2, grad)
    grad = grad * vec(4)
    grad = inv * (grad - mean_of(grad) - normed * mean_of(grad * normed))
    grad_second[...] = grad
    low = grad.astype(BF)
    branch[...] = low
    add_rows(sums, 0, low.astype(F32))
    branch_t[...] = low.T

    @pl.when(i == pl.num_programs(0) - 1)
    def _():
        for row in range(3):
            vec_sums[row : row + 1, :] = jnp.sum(sums[row], axis=0, keepdims=True)
        vec_sums[3:8, :] = jnp.zeros((5, width), F32)


def down_layer(t, out_grad, vecs, first, act, down_all, nt):
    span, width = first.shape
    hidden = act.shape[1]
    block = 512
    rows = pl.BlockSpec((block, width), lambda i, _: (i, 0))
    whole = lambda shape: pl.BlockSpec(shape, lambda i, _: (0,) * len(shape))
    sds = jax.ShapeDtypeStruct
    return pl.pallas_call(
        functools.partial(down_kernel, nt=nt),
        out_shape=(
            sds((span, width), BF),
            sds((span, width), BF),
            sds((width, span), BF),
            sds((span, width), F32),
            sds((8, width), F32),
        ),
        grid_spec=pltpu.PrefetchScalarGridSpec(
            num_scalar_prefetch=1,
            grid=(span // block,),
            in_specs=[
                pl.BlockSpec((1, block, width), lambda i, t_ref: (t_ref[0], i, 0)),
                whole(vecs.shape),
                rows,
                pl.BlockSpec((block, hidden), lambda i, _: (i, 0)),
                pl.BlockSpec(memory_space=pl.ANY),
            ],
            out_specs=(rows, rows, pl.BlockSpec((width, block), lambda i, _: (0, i)), rows, whole((8, width))),
            scratch_shapes=[
                pltpu.VMEM((hidden, width), BF),
                pltpu.VMEM((block, width), F32),
                pltpu.VMEM((3, 8, width), F32),
                pltpu.SemaphoreType.DMA((down_all.shape[0],)),
            ],
        ),
        compiler_params=pltpu.CompilerParams(vmem_limit_bytes=60 << 20),
        cost_estimate=pl.CostEstimate(
            flops=2 * span * width * hidden, bytes_accessed=30 << 20, transcendentals=0
        ),
        name="down_layer",
    )(t, out_grad, vecs, first, act, down_all)


def back_kernel(
    vecs, branch, grad_second, slope, norm_one, inv_one, up_in, down_in, partial,
    hid, attn_t, grad_in, grad_ctx, vec_sums, quarter,
    up, down, proj, acc, sums, sums_u, by_y, near_y, by_x, near_x, last_x, last_y,
    fill, own_fill, one_send, one_recv, two_send, two_recv,
    *, nz, nt, tile,
):
    i = pl.program_id(0)
    c, t = lax.axis_index("context"), lax.axis_index("tensor")
    x_dev, y_dev = {"context": 1 - c}, {"tensor": 1 - t}
    width, hidden = up.shape
    rest = last_x.shape[0] // nz
    half = last_x.shape[1]
    tall = nz * 2 * rest
    left, right = pl.ds(0, half), pl.ds(half, half)
    own_copies = [pltpu.make_async_copy(partial.at[aligned(t * tall, tall), left], by_y, own_fill.at[0])]
    first_copies = [
        remote(partial.at[aligned((1 - t) * tall, tall), left], near_y, one_send.at[0], one_recv.at[0], y_dev)
    ]
    for b in range(nt * nz):
        spot = pl.ds(b * rest, rest)
        own_copies.append(
            pltpu.make_async_copy(
                partial.at[aligned((b * 2 + c) * rest, rest), right], by_x.at[spot], own_fill.at[1 + b]
            )
        )
        first_copies.append(
            remote(
                partial.at[aligned((b * 2 + 1 - c) * rest, rest), right],
                near_x.at[spot],
                one_send.at[1 + b],
                one_recv.at[1 + b],
                x_dev,
            )
        )
    second_copies = [
        remote(by_x.at[aligned((1 - t) * nz * rest, nz * rest)], last_y, two_send.at[0], two_recv.at[0], y_dev)
    ]
    for zi in range(nz):
        second_copies.append(
            remote(
                by_y.at[aligned((zi * 2 + 1 - c) * rest, rest)],
                last_x.at[pl.ds(zi * rest, rest)],
                two_send.at[1 + zi],
                two_recv.at[1 + zi],
                x_dev,
            )
        )

    @pl.when(i == 0)
    def _():
        greet([x_dev, y_dev])
        for one in first_copies + own_copies:
            one.start()

    @pl.when(i == 2)
    def _():
        for one in own_copies:
            one.wait()
        for one in first_copies:
            one.wait_recv()
        by_y[...] = (by_y[...].astype(F32) + near_y[...].astype(F32)).astype(BF)
        by_x[...] = (by_x[...].astype(F32) + near_x[...].astype(F32)).astype(BF)
        for one in second_copies:
            one.start()

    down_fill = load_blocks(down_in, 0, down, fill.at[0], nt, False)
    up_fill = load_blocks(up_in, 0, up, fill.at[1], nt, True)
    proj_fill = load_blocks(up_in, hidden // nt, proj, fill.at[2], nt, True)

    @pl.when(i == 0)
    def _():
        for one in down_fill + up_fill + proj_fill:
            one.start()
        sums[...] = jnp.zeros(sums.shape, F32)
        sums_u[...] = jnp.zeros(sums_u.shape, F32)
        for one in down_fill + up_fill + proj_fill:
            one.wait()

    ones = jnp.ones((8, branch.shape[0]), BF)
    acc[...] = grad_second[...]

    @pl.loop(0, hidden // tile)
    def _(j):
        cut = aligned(j * tile, tile)
        low_hid = (mm_nt(branch[...], down[cut, :]) * slope[:, cut].astype(F32)).astype(BF)
        hid[:, cut] = low_hid
        sums_u[:, cut] += mm(ones, low_hid)
        acc[...] += mm_nt(low_hid, up[:, cut])

    grad = acc[...]
    normed = norm_one[...]
    add_rows(sums, 1, grad * normed)
    add_rows(sums, 2, grad)
    grad = grad * vecs[1:2, :]
    grad = inv_one[:, 0:1] * (grad - mean_of(grad) - normed * mean_of(grad * normed))
    grad_in[...] = grad
    low = grad.astype(BF)
    add_rows(sums, 0, low.astype(F32))
    attn_t[...] = low.T
    grad_ctx[...] = mm(low, proj[...]).astype(BF)

    @pl.when(i == pl.num_programs(0) - 1)
    def _():
        for row in range(3):
            vec_sums[row : row + 1, :] = jnp.sum(sums[row], axis=0, keepdims=True)
        vec_sums[3:8, :] = jnp.zeros((5, width), F32)
        for row in range(hidden // width):
            vec_sums[3 + row : 4 + row, :] = sums_u[0:1, row * width : (row + 1) * width]
        for one in second_copies:
            one.wait_recv()
        for zi in range(nz):
            spot = slice(zi * rest, (zi + 1) * rest)
            mine = by_y[aligned((zi * 2 + c) * rest, rest), :]
            quarter[spot, :half] = (mine.astype(F32) + last_x[spot, :].astype(F32)).astype(BF)
        mine = by_x[aligned(t * nz * rest, nz * rest), :]
        quarter[:, half:] = (mine.astype(F32) + last_y[...].astype(F32)).astype(BF)
        for one in first_copies + second_copies:
            one.wait_send()


def back_layer(vecs, branch, grad_second, slope, norm_one, inv_one, up_all, down_all, partial, nz, nt):
    span, width = branch.shape
    hidden = slope.shape[1]
    block, tile = span // 4, 512
    rest, half = partial.shape[0] // (nt * nz * 2), partial.shape[1] // 2
    quarter = (nz * rest, 2 * half)
    hbm = pl.BlockSpec(memory_space=pl.ANY)
    rows = pl.BlockSpec((block, width), lambda i: (i, 0))
    wide = pl.BlockSpec((block, hidden), lambda i: (i, 0))
    whole = lambda shape: pl.BlockSpec(shape, lambda i: (0,) * len(shape))
    sds = jax.ShapeDtypeStruct
    return pl.pallas_call(
        functools.partial(back_kernel, nz=nz, nt=nt, tile=tile),
        out_shape=(
            sds((span, hidden), BF),
            sds((width, span), BF),
            sds((span, width), F32),
            sds((span, width), BF),
            sds((8, width), F32),
            sds(quarter, BF),
        ),
        grid=(span // block,),
        in_specs=[
            whole(vecs.shape),
            rows,
            rows,
            wide,
            rows,
            pl.BlockSpec((block, 128), lambda i: (i, 0)),
            hbm,
            hbm,
            hbm,
        ],
        out_specs=(
            wide, pl.BlockSpec((width, block), lambda i: (0, i)), rows, rows, whole((8, width)), whole(quarter),
        ),
        scratch_shapes=[
            pltpu.VMEM((width, hidden), BF),
            pltpu.VMEM((hidden, width), BF),
            pltpu.VMEM((width, width), BF),
            pltpu.VMEM((block, width), F32),
            pltpu.VMEM((3, 8, width), F32),
            pltpu.VMEM((8, hidden), F32),
            pltpu.VMEM((nz * 2 * rest, half), BF),
            pltpu.VMEM((nz * 2 * rest, half), BF),
            pltpu.VMEM((nt * nz * rest, half), BF),
            pltpu.VMEM((nt * nz * rest, half), BF),
            pltpu.VMEM((nz * rest, half), BF),
            pltpu.VMEM((nz * rest, half), BF),
            pltpu.SemaphoreType.DMA((3, up_all.shape[0])),
            pltpu.SemaphoreType.DMA((1 + nt * nz,)),
            pltpu.SemaphoreType.DMA((1 + nt * nz,)),
            pltpu.SemaphoreType.DMA((1 + nt * nz,)),
            pltpu.SemaphoreType.DMA((1 + nz,)),
            pltpu.SemaphoreType.DMA((1 + nz,)),
        ],
        compiler_params=pltpu.CompilerParams(
            collective_id=4, has_side_effects=True, vmem_limit_bytes=60 << 20
        ),
        cost_estimate=pl.CostEstimate(
            flops=2 * span * width * (width + 2 * hidden), bytes_accessed=60 << 20, transcendentals=0
        ),
        name="back_layer",
    )(vecs, branch, grad_second, slope, norm_one, inv_one, up_all, down_all, partial)


def grads_kernel(*refs, pairs, nz, nt, chunk):
    lefts, rights = refs[0 : 2 * pairs : 2], refs[1 : 2 * pairs : 2]
    refs = refs[2 * pairs :]
    quarter = None
    if len(refs) > 11:
        quarter, dctx_in, packed, shard, dctx = refs[:5]
        mine, others, dctx_own, mine_fill, dctx_sems, q_send, q_recv = refs[-7:]
        refs = (packed,) + refs[5:-7]
    packed, left, right, away, near, stage, l_fill, r_fill, send, recv, out_sems = refs
    z = lax.axis_index("z")
    k = lax.axis_index("core")
    core_dev = {"core": 1 - k}
    dblk = left.shape[2] // nz
    span = right.shape[1]
    plan = []
    base = 0
    for which in range(pairs):
        size = rights[which].shape[1] // nt
        for ti in range(nt):
            for at in range(0, size, min(chunk, size)):
                step = min(chunk, size)
                plan.append((which, ti * size + at, ti, base + at, step))
        base += size

    l_copies = [
        [
            pltpu.make_async_copy(
                lefts[which].at[aligned((zi * 2 + lax.rem(k + 1 + kk, 2)) * dblk, dblk)],
                left.at[which, kk, pl.ds(zi * dblk, dblk)],
                l_fill.at[which, kk, zi],
            )
            for kk in range(2)
            for zi in range(nz)
        ]
        for which in range(pairs)
    ]
    r_copies = [
        pltpu.make_async_copy(
            rights[which].at[:, pl.ds(col, step)], right.at[n, :, pl.ds(0, step)], r_fill.at[n]
        )
        for n, (which, col, _ti, _out, step) in enumerate(plan)
    ]
    for n, (which, _col, _ti, _out, _step) in enumerate(plan):
        if n == 0 or plan[n - 1][0] != which:
            for one in l_copies[which]:
                one.start()
        r_copies[n].start()
    friends = [core_dev]
    if quarter is not None:
        c = lax.axis_index("context")
        friends += [{"context": 1 - c}]
        friends += [{"z": lax.rem(z + d, nz)} for d in range(1, nz)]
    greet(friends)
    if quarter is not None:
        rest = mine.shape[0]

        def q_copy(d, owner, target):
            return remote(
                quarter.at[aligned(target * rest, rest)],
                others.at[owner],
                q_send.at[d - 1],
                q_recv.at[owner],
                {"z": lax.rem(z + d, nz)},
            )

        cols = dctx.shape[1]
        own_in = pltpu.make_async_copy(dctx_in.at[:, aligned(c * cols, cols)], dctx_own, dctx_sems.at[0])
        own_out = pltpu.make_async_copy(dctx_own, dctx.at[pl.ds(0, span)], dctx_sems.at[1])
        dctx_copy = remote(
            dctx_in.at[:, aligned((1 - c) * cols, cols)],
            dctx.at[pl.ds(span, span)],
            dctx_sems.at[2],
            dctx_sems.at[3],
            {"context": 1 - c},
        )
        own_in.start()
        dctx_copy.start()
        own = pltpu.make_async_copy(quarter.at[aligned(z * rest, rest)], mine, mine_fill)
        own.start()

    def exchange(n):
        step = plan[n][4]
        cut = pl.ds(0, step)
        return remote(away.at[n, :, cut], near.at[n, :, cut], send.at[n], recv.at[n], core_dev)

    sub = 256
    for n, (which, _col, _ti, _out, step) in enumerate(plan):
        if n == 0 or plan[n - 1][0] != which:
            for one in l_copies[which]:
                one.wait()
        r_copies[n].wait()

        @pl.loop(0, step // sub)
        def _(j, n=n, which=which):
            cut = aligned(j * sub, sub)
            away[n, :, cut] = mm(left[which, 0], right[n, :, cut]).astype(BF)

        exchange(n).start()

    if quarter is not None:
        own_in.wait()
        own_out.start()
        for d in range(1, nz):
            q_copy(d, z, lax.rem(z + d, nz)).start()
    outs = []
    for n, (which, _col, ti, out, step) in enumerate(plan):
        exchange(n).wait_recv()
        slot = n % 2
        if n >= 2:
            outs[n - 2].wait()

        @pl.loop(0, step // sub)
        def _(j, n=n, which=which, slot=slot):
            cut = aligned(j * sub, sub)
            stage[slot, :, cut] = (
                mm(left[which, 1], right[n, :, cut]) + near[n, :, cut].astype(F32)
            ).astype(BF)

        outs.append(
            pltpu.make_async_copy(
                stage.at[slot, :, pl.ds(0, step)],
                packed.at[pl.ds(ti * nz * dblk, nz * dblk), pl.ds(out, step)],
                out_sems.at[slot],
            )
        )
        outs[n].start()
    for one in outs[-2:]:
        one.wait()
    for n in range(len(plan)):
        exchange(n).wait_send()
    if quarter is not None:
        own.wait()
        total = mine[...].astype(F32)
        for d in range(1, nz):
            owner = lax.rem(z + nz - d, nz)
            q_copy(d, owner, z).wait_recv()
            total = total + others[owner].astype(F32)
        shard[...] = total.astype(BF)
        own_out.wait()
        dctx_copy.wait()
        for d in range(1, nz):
            q_copy(d, z, lax.rem(z + d, nz)).wait_send()


def grads_layer(operands, nz, nt, collective_id, quarter=None, grad_context=None):
    pairs = len(operands) // 2
    width, span = operands[0].shape
    chunk = 1024
    dblk = width // (2 * nz)
    sizes = [one.shape[1] // nt for one in operands[1::2]]
    count = sum(nt * max(1, size // chunk) for size in sizes)
    dma = pltpu.SemaphoreType.DMA
    hbm = pl.BlockSpec(memory_space=pl.ANY)
    out_shape = [jax.ShapeDtypeStruct((nt * nz * dblk, sum(sizes)), BF)]
    out_specs, extra = [hbm], []
    if quarter is not None:
        rest = (quarter.shape[0] // nz, quarter.shape[1])
        operands = operands + [quarter, grad_context]
        dctx = (2 * span, grad_context.shape[1] // 2)
        out_shape += [jax.ShapeDtypeStruct(rest, BF), jax.ShapeDtypeStruct(dctx, BF)]
        out_specs += [pl.BlockSpec(memory_space=pltpu.VMEM), hbm]
        extra = [
            pltpu.VMEM(rest, BF),
            pltpu.VMEM((nz,) + rest, BF),
            pltpu.VMEM((span, dctx[1]), BF),
            dma(()),
            dma((4,)),
            dma((nz,)),
            dma((nz,)),
        ]
    return pl.pallas_call(
        functools.partial(grads_kernel, pairs=pairs, nz=nz, nt=nt, chunk=chunk),
        out_shape=out_shape,
        in_specs=[hbm] * len(operands),
        out_specs=out_specs,
        scratch_shapes=[
            pltpu.VMEM((pairs, 2, nz * dblk, span), BF),
            pltpu.VMEM((count, span, chunk), BF),
            pltpu.VMEM((count, nz * dblk, chunk), BF),
            pltpu.VMEM((count, nz * dblk, chunk), BF),
            pltpu.VMEM((2, nz * dblk, chunk), BF),
            dma((pairs, 2, nz)),
            dma((count,)),
            dma((count,)),
            dma((count,)),
            dma((2,)),
        ]
        + extra,
        compiler_params=pltpu.CompilerParams(
            collective_id=collective_id, has_side_effects=True, vmem_limit_bytes=60 << 20
        ),
        cost_estimate=pl.CostEstimate(
            flops=2 * span * width * nt * sum(sizes), bytes_accessed=40 << 20, transcendentals=0
        ),
        name="grads_layer",
    )(*operands)


def on_device_rows(
    sizes,
    tokens,
    segment_ids,
    qkv_weight,
    qv_bias,
    proj_weight,
    proj_bias,
    first_gain,
    first_shift,
    up_weight,
    up_bias,
    down_weight,
    down_bias,
    second_gain,
    second_shift,
    out_grad,
):
    nf, nc, nt = sizes
    nz = nf // 2
    zbits = nz.bit_length() - 1
    z, k, c, t = (lax.axis_index(name) for name in AXES)
    f = z * 2 + k

    def send(value, target):
        pairs = []
        for fi in range(nf):
            for ci in range(nc):
                for ti in range(nt):
                    to = target(fi // 2, fi % 2, ci, ti)
                    if to is not None:
                        zo, ko, co, tto = to
                        pairs.append(((fi * nc + ci) * nt + ti, ((zo * 2 + ko) * nc + co) * nt + tto))
        return lax.ppermute(value, AXES, pairs)

    def over_x(v):
        return send(v, lambda zi, ki, ci, ti: (zi, ki, 1 - ci, ti))

    def over_y(v):
        return send(v, lambda zi, ki, ci, ti: (zi, ki, ci, 1 - ti))

    def over_core(v):
        return send(v, lambda zi, ki, ci, ti: (zi, 1 - ki, ci, ti))

    def over_z(v):
        return send(v, lambda zi, ki, ci, ti: ((zi + 1) % nz, ki, ci, ti))

    def over_zbit(v, bit):
        return send(v, lambda zi, ki, ci, ti: (zi ^ (1 << bit), ki, ci, ti))

    def z_all(v):
        return [v] + [
            send(v, lambda zi, ki, ci, ti, d=d: ((zi + d) % nz, ki, ci, ti)) for d in range(1, nz)
        ]

    def z_ring(v):
        out = [v]
        for _ in range(nz - 1):
            out.append(over_z(out[-1]))
        return out

    def ordered(index, own, other, axis=0):
        return jnp.where(index == 0, jnp.concatenate([own, other], axis), jnp.concatenate([other, own], axis))

    seq_count, span, width = tokens.shape
    heads = qv_bias.shape[1]
    head_size = qv_bias.shape[2] * nf
    cols = heads * head_size
    hidden = up_weight.shape[1] * nt
    dblk = width // nf

    pairs = heads // 2
    group = max(1, pairs // 2)
    wide = 2 * head_size

    pieces = [qv_bias, up_bias, proj_bias, first_gain, first_shift, down_bias, second_gain, second_shift]
    small = jnp.concatenate([p.reshape(-1, 128) for p in pieces])
    up_at, vec_at = qv_bias.size // 128, (qv_bias.size + up_bias.size) // 128
    small = jnp.pad(small, ((0, -(small.shape[0] + 2) % 16 + 2), (0, 0)))
    own_seg = jnp.where(t == 0, segment_ids[0], segment_ids[1])
    other_seg = over_x(own_seg)
    rows_t, qkv_full, qkv, small = open_layer(tokens, qkv_weight, small, nz, nt, heads, head_size, group)
    small = small.reshape(nf, nt, -1, 128)
    edge = head_size // nf

    def interleave(rows, columns):
        col = lax.broadcasted_iota(jnp.int32, (rows.shape[1], columns), 1)
        source = lax.broadcasted_iota(jnp.int32, (rows.shape[1], columns), 0)
        spread_out = mm(rows, (source == col // head_size * edge + col % edge).astype(BF))
        col = lax.broadcasted_iota(jnp.int32, (nf, columns), 1)
        mine = col % head_size // edge == lax.broadcasted_iota(jnp.int32, (nf, columns), 0)
        return jnp.sum(jnp.where(mine, spread_out, 0.0), axis=0)

    up_add = jnp.concatenate(
        [interleave(small[:, i, up_at:vec_at].reshape(nf, -1), hidden // nt) for i in range(nt)]
    ).reshape(1, hidden)
    vecs = small[:, 0, vec_at : vec_at + 8].transpose(1, 0, 2).reshape(8, width).astype(F32)

    every = AXES[:2] + AXES[3:]
    up_shard = jnp.concatenate([up_weight, proj_weight.T], axis=1)
    up_all = lax.all_gather(up_shard, every).reshape((-1,) + up_shard.shape)
    down_all = lax.all_gather(after(down_weight, up_shard), every).reshape((-1,) + down_weight.shape)

    seg_store = jnp.concatenate([own_seg, other_seg])
    seg_global = ordered(c, own_seg, other_seg)
    total = 2 * span
    blk = 256
    low, high = segment_bounds(seg_global, blk, FINE)
    shift = jnp.reshape(c * (total // FINE // 2), (1,)).astype(jnp.int32)
    seg_k = jnp.broadcast_to(seg_store[:, None], (total, 128))
    seg_q = jnp.broadcast_to(seg_store[None, :], (8, total))
    attn_args = (seg_k, seg_q, low, high, shift)
    mixed, lse, mixed_other = [], [], []
    for p in range(pairs):
        source = after(qkv, mixed_other[p - 2]) if p >= 2 else qkv
        out, one = attn_fwd(source, *attn_args, p, pairs, group, head_size, blk, 3)
        mixed.append(out)
        lse.append(one)
        mixed_other.append(over_x(out[span:]))
    up_all, _last = lax.optimization_barrier((up_all, mixed[-1]))
    context_rows = ordered(
        c, jnp.concatenate([m[:span] for m in mixed], 1), jnp.concatenate(mixed_other, 1), 1
    )

    which = t.reshape(1)
    first, norm_one, inv_one, first_t, act_low, slope = up_layer(
        which, context_rows, tokens, vecs, up_add, up_all, nt
    )
    down_all, first = lax.optimization_barrier((down_all, first))
    out_low, branch, branch_t, grad_second, vec_two = down_layer(
        which, out_grad, vecs, first, act_low, down_all, nt
    )
    (down_sum,) = grads_layer([branch_t, act_low], nz, nt, 2)
    hidden_low, attn_t, grad_in, grad_context, vec_one, quarter = back_layer(
        vecs, branch, grad_second, slope, norm_one, inv_one, up_all, down_all, down_sum, nz, nt
    )
    out_low = after(out_low, quarter)
    out_other = over_y(out_low)
    other_sum, down_part, dctx = grads_layer([first_t, hidden_low, attn_t, context_rows], nz, nt, 3, quarter, grad_context)
    grad_down = ordered(c, down_part, over_x(down_part), 0).astype(F32).T
    part = lax.psum_scatter(other_sum, ("tensor", "z", "context"), scatter_dimension=0, tiled=True)
    part = ordered(c, part, over_x(part), 0).astype(F32)
    grad_up = part[:, : hidden // nt]
    grad_proj = part[:, hidden // nt :].T

    mixed = lax.optimization_barrier(tuple(mixed) + (quarter,))[:pairs]
    dqkv = attn_bwd(
        qkv, jnp.concatenate(mixed, axis=1), dctx, jnp.concatenate(lse), *attn_args, pairs, group, head_size, blk, 3
    )
    layer_output = ordered(t, out_low[None], out_other[None])
    dqkv, grad_down, layer_output = lax.optimization_barrier((dqkv, grad_down, layer_output))
    tokens_grad, grad_qkv, qv_sum, vec_sums = close_layer(
        dqkv, qkv_full, rows_t, grad_in, vec_one, vec_two, nz, group * wide
    )
    own_vecs = lax.dynamic_slice_in_dim(vec_sums, f * dblk, dblk, 1)
    vector_out = [own_vecs[row] for row in (0, 1, 2, 8, 9, 10)]
    up_rows, up_cols = up_bias.shape
    bias_up = vec_sums[3 : 3 + hidden // width].reshape(nt * up_rows, nf * up_cols)
    bias_up = lax.dynamic_slice(bias_up, (t * up_rows, f * up_cols), (up_rows, up_cols))
    per = wide // 128 * group
    kinds = [
        jnp.concatenate([qv_sum[(3 * g + which) * per :][:per] for g in range(pairs // group)])
        for which in (0, 2)
    ]
    grad_qv = jnp.stack(kinds).reshape(2, heads, head_size)
    grad_qv = lax.dynamic_slice_in_dim(grad_qv, f * (head_size // nf), head_size // nf, 2)

    return (
        layer_output,
        tokens_grad,
        grad_qkv,
        grad_qv,
        grad_proj,
        vector_out[0],
        vector_out[1],
        vector_out[2],
        grad_up,
        bias_up,
        grad_down,
        vector_out[3],
        vector_out[4],
        vector_out[5],
    )


def solution(mesh):
    sizes = tuple(mesh.shape[name] for name in ("fsdp", "context", "tensor"))
    nf, nc, nt = sizes
    shards = (
        P("fsdp", "context", None),
        P("fsdp", "context"),
        P(None, "fsdp", "tensor"),
        P(None, "tensor", "fsdp"),
        P("tensor", "fsdp"),
        P("fsdp"),
        P("fsdp"),
        P("fsdp"),
        P("fsdp", "tensor"),
        P("tensor", "fsdp"),
        P("tensor", "fsdp"),
        P("fsdp"),
        P("fsdp"),
        P("fsdp"),
    )
    in_specs = (shards[0],) + shards[1:] + (shards[0],)
    out_specs = (shards[0], shards[0]) + shards[2:]
    nz = nf // 2
    by_rows = nc == nt == 2 and nf % 2 == 0 and nz & (nz - 1) == 0
    rows_mesh = jax.sharding.Mesh(mesh.devices.reshape(nz, 2, nc, nt), AXES) if by_rows else None

    def finer(spec):
        return P(*(("z", "core") if name == "fsdp" else name for name in spec))

    def program(*args):
        if by_rows and args[0].shape[0] // nf == nt:
            return jax.shard_map(
                functools.partial(on_device_rows, sizes),
                mesh=rows_mesh,
                in_specs=tuple(finer(spec) for spec in in_specs),
                out_specs=tuple(finer(spec) for spec in out_specs),
                check_vma=False,
            )(*args)
        return jax.shard_map(
            on_device_general, mesh=mesh, in_specs=in_specs, out_specs=out_specs, check_vma=False
        )(*args)

    return program
```

```python
import functools

import jax
import jax.numpy as jnp
from jax import lax
from jax.experimental import pallas as pl
from jax.experimental.pallas import tpu as pltpu
from jax.sharding import PartitionSpec as P

NORM_EPS = 1e-05


def layer_norm(hidden_rows, norm_gain, norm_shift):
    row_mean = jnp.mean(hidden_rows, axis=-1, keepdims=True)
    centred = hidden_rows - row_mean
    variance = jnp.mean(centred * centred, axis=-1, keepdims=True)
    return centred * lax.rsqrt(variance + NORM_EPS) * norm_gain + norm_shift


def exact_gelu(values):
    return jax.nn.gelu(values, approximate=False)


def masked_logits(query_heads, key_heads, seg_query, seg_key, score_scale):
    logits = (
        jnp.einsum("qhe,khe->hqk", query_heads, key_heads, preferred_element_type=jnp.float32)
        * score_scale
    )
    same_doc = (seg_query[:, None] == seg_key[None, :])[None, :, :]
    return jnp.where(same_doc, logits, -1e30)


def on_device_general(
    tokens,
    segment_ids,
    qkv_weight,
    qv_bias,
    proj_weight,
    proj_bias,
    first_gain,
    first_shift,
    up_weight,
    up_bias,
    down_weight,
    down_bias,
    second_gain,
    second_shift,
    out_grad,
):
    seq_count, span, width = tokens.shape
    total_rows = seq_count * span
    share = total_rows // lax.axis_size("tensor")
    row_start = lax.axis_index("tensor") * share
    token_rows = tokens.reshape(total_rows, width)
    gathered = (
        lax.all_gather(qkv_weight, "fsdp", axis=1, tiled=True),
        lax.all_gather(qv_bias, "fsdp", axis=2, tiled=True),
        lax.all_gather(proj_weight, "fsdp", axis=1, tiled=True),
        lax.all_gather(proj_bias, "fsdp", axis=0, tiled=True),
        lax.all_gather(first_gain, "fsdp", axis=0, tiled=True),
        lax.all_gather(first_shift, "fsdp", axis=0, tiled=True),
        lax.all_gather(up_weight, "fsdp", axis=0, tiled=True),
        lax.all_gather(up_bias, "fsdp", axis=1, tiled=True),
        lax.all_gather(down_weight, "fsdp", axis=1, tiled=True),
        lax.all_gather(down_bias, "fsdp", axis=0, tiled=True),
        lax.all_gather(second_gain, "fsdp", axis=0, tiled=True),
        lax.all_gather(second_shift, "fsdp", axis=0, tiled=True),
    )
    qkv_full, qv_full, proj_full, proj_add, gain_one, shift_one = (
        gathered[0],
        gathered[1],
        gathered[2],
        gathered[3],
        gathered[4],
        gathered[5],
    )
    up_full, up_add, down_full, down_add, gain_two, shift_two = (
        gathered[6],
        gathered[7],
        gathered[8],
        gathered[9],
        gathered[10],
        gathered[11],
    )
    local_width = qkv_full.shape[2]
    head_count = qv_full.shape[1]
    head_size = qv_full.shape[2]
    score_scale = float(head_size) ** (-0.5)
    projected = jnp.einsum("rd,cde->cre", token_rows, qkv_full, preferred_element_type=jnp.float32)
    bias_rows = qv_full.reshape(2, local_width).astype(jnp.float32)
    head_shape = (seq_count, span, head_count, head_size)
    query_heads = (projected[0] + bias_rows[0]).astype(jnp.bfloat16).reshape(head_shape)
    key_heads = projected[1].astype(jnp.bfloat16).reshape(head_shape)
    value_heads = (projected[2] + bias_rows[1]).astype(jnp.bfloat16).reshape(head_shape)
    key_all, value_all, seg_all = (
        lax.all_gather(key_heads, "context", axis=1, tiled=True),
        lax.all_gather(value_heads, "context", axis=1, tiled=True),
        lax.all_gather(segment_ids, "context", axis=1, tiled=True),
    )

    def attend_forward(pieces):
        query_one, key_one, value_one, seg_query, seg_key = pieces
        logits = masked_logits(query_one, key_one, seg_query, seg_key, score_scale)
        row_top = jnp.max(logits, axis=-1, keepdims=True)
        weights = jnp.exp(logits - row_top)
        row_total = jnp.sum(weights, axis=-1, keepdims=True)
        soft_low = (weights / row_total).astype(jnp.bfloat16)
        mixed_one = jnp.einsum(
            "hqk,khe->qhe", soft_low, value_one, preferred_element_type=jnp.float32
        )
        return (mixed_one.astype(jnp.bfloat16), row_top + jnp.log(row_total))

    mixed, log_totals = lax.map(
        attend_forward, (query_heads, key_all, value_all, segment_ids, seg_all)
    )
    context_low = mixed.reshape(total_rows, local_width)
    attn_part = jnp.dot(context_low, proj_full, preferred_element_type=jnp.float32)
    attn_share = lax.psum_scatter(
        attn_part, "tensor", scatter_dimension=0, tiled=True
    ) + proj_add.astype(jnp.float32)
    token_share = lax.dynamic_slice_in_dim(token_rows, row_start, share, 0).astype(jnp.float32)
    first_share, first_pull = jax.vjp(
        layer_norm,
        token_share + attn_share,
        gain_one.astype(jnp.float32),
        shift_one.astype(jnp.float32),
    )
    first_low = lax.all_gather(first_share.astype(jnp.bfloat16), "tensor", axis=0, tiled=True)
    hidden_pre = jnp.dot(first_low, up_full, preferred_element_type=jnp.float32) + up_add.reshape(
        -1
    ).astype(jnp.float32)
    activation, gelu_pull = jax.vjp(exact_gelu, hidden_pre)
    act_low = activation.astype(jnp.bfloat16)
    down_part = jnp.dot(act_low, down_full, preferred_element_type=jnp.float32)
    branch_share = lax.psum_scatter(
        down_part, "tensor", scatter_dimension=0, tiled=True
    ) + down_add.astype(jnp.float32)
    output_share, second_pull = jax.vjp(
        layer_norm,
        first_share + branch_share,
        gain_two.astype(jnp.float32),
        shift_two.astype(jnp.float32),
    )
    qkv_back, proj_back, up_back, down_back = (
        lax.all_gather(qkv_weight, "fsdp", axis=1, tiled=True),
        lax.all_gather(proj_weight, "fsdp", axis=1, tiled=True),
        lax.all_gather(up_weight, "fsdp", axis=0, tiled=True),
        lax.all_gather(down_weight, "fsdp", axis=1, tiled=True),
    )
    cot_share = lax.dynamic_slice_in_dim(
        out_grad.reshape(total_rows, width), row_start, share, 0
    ).astype(jnp.float32)
    grad_second, gain_two_part, shift_two_part = second_pull(cot_share)
    branch_low = lax.all_gather(grad_second.astype(jnp.bfloat16), "tensor", axis=0, tiled=True)
    grad_down_bias = jnp.sum(branch_low.astype(jnp.float32), axis=0)
    grad_down = jnp.einsum("rf,rd->fd", act_low, branch_low, preferred_element_type=jnp.float32)
    grad_act = jnp.einsum("rd,fd->rf", branch_low, down_back, preferred_element_type=jnp.float32)
    hidden_low = gelu_pull(grad_act)[0].astype(jnp.bfloat16)
    grad_up_bias = jnp.sum(hidden_low.astype(jnp.float32), axis=0).reshape(up_add.shape)
    grad_up = jnp.einsum("rd,rf->df", first_low, hidden_low, preferred_element_type=jnp.float32)
    norm_part = jnp.einsum("rf,df->rd", hidden_low, up_back, preferred_element_type=jnp.float32)
    grad_first = grad_second + lax.psum_scatter(
        norm_part, "tensor", scatter_dimension=0, tiled=True
    )
    grad_in_one, gain_one_part, shift_one_part = first_pull(grad_first)
    attn_low = lax.all_gather(grad_in_one.astype(jnp.bfloat16), "tensor", axis=0, tiled=True)
    grad_proj_bias = jnp.sum(attn_low.astype(jnp.float32), axis=0)
    grad_proj = jnp.einsum("rl,rd->ld", context_low, attn_low, preferred_element_type=jnp.float32)
    grad_context = (
        jnp.einsum("rd,ld->rl", attn_low, proj_back, preferred_element_type=jnp.float32)
        .astype(jnp.bfloat16)
        .reshape(head_shape)
    )

    def attend_backward(pieces):
        query_one, key_one, value_one, seg_query, seg_key, log_total, context_grad = pieces
        logits = masked_logits(query_one, key_one, seg_query, seg_key, score_scale)
        soft_again = jnp.exp(logits - log_total)
        grad_soft = jnp.einsum(
            "qhe,khe->hqk", context_grad, value_one, preferred_element_type=jnp.float32
        )
        row_delta = jnp.sum(grad_soft * soft_again, axis=-1, keepdims=True)
        grad_logits = (soft_again * (grad_soft - row_delta)).astype(jnp.bfloat16)
        query_grad = (
            jnp.einsum("hqk,khe->qhe", grad_logits, key_one, preferred_element_type=jnp.float32)
            * score_scale
        ).astype(jnp.bfloat16)
        key_part = (
            jnp.einsum("hqk,qhe->khe", grad_logits, query_one, preferred_element_type=jnp.float32)
            * score_scale
        )
        value_part = jnp.einsum(
            "hqk,qhe->khe",
            soft_again.astype(jnp.bfloat16),
            context_grad,
            preferred_element_type=jnp.float32,
        )
        return (query_grad, key_part, value_part)

    grad_query, key_terms, value_terms = lax.map(
        attend_backward,
        (query_heads, key_all, value_all, segment_ids, seg_all, log_totals, grad_context),
    )
    key_grad, value_grad = (
        lax.psum_scatter(
            key_terms.astype(jnp.bfloat16), "context", scatter_dimension=1, tiled=True
        ).astype(jnp.float32),
        lax.psum_scatter(
            value_terms.astype(jnp.bfloat16), "context", scatter_dimension=1, tiled=True
        ).astype(jnp.float32),
    )
    grad_stack = jnp.stack(
        [
            grad_query.reshape(total_rows, local_width),
            key_grad.astype(jnp.bfloat16).reshape(total_rows, local_width),
            value_grad.astype(jnp.bfloat16).reshape(total_rows, local_width),
        ]
    )
    stack_sums = jnp.sum(grad_stack.astype(jnp.float32), axis=1)
    grad_qv_bias = jnp.stack([stack_sums[0], stack_sums[2]]).reshape(qv_full.shape)
    grad_qkv = jnp.einsum("rd,cre->cde", token_rows, grad_stack, preferred_element_type=jnp.float32)
    input_part = jnp.einsum("cre,cde->rd", grad_stack, qkv_back, preferred_element_type=jnp.float32)
    norm_parts = jnp.tile(
        jnp.stack([gain_one_part, shift_one_part, gain_two_part, shift_two_part]),
        (lax.axis_size("tensor"), 1),
    )
    input_share, norm_sums = (
        lax.psum_scatter(
            input_part.astype(jnp.bfloat16), "tensor", scatter_dimension=0, tiled=True
        ).astype(jnp.float32),
        lax.psum_scatter(
            norm_parts.astype(jnp.bfloat16), "tensor", scatter_dimension=0, tiled=True
        ).astype(jnp.float32),
    )
    grad_share_low = (grad_in_one + input_share).astype(jnp.bfloat16)
    out_rows, grad_rows = (
        lax.all_gather(output_share.astype(jnp.bfloat16), "tensor", axis=0, tiled=True),
        lax.all_gather(grad_share_low, "tensor", axis=0, tiled=True),
    )
    local_grads = (
        grad_qkv,
        grad_qv_bias,
        grad_proj,
        grad_proj_bias,
        norm_sums[0],
        norm_sums[1],
        grad_up,
        grad_up_bias,
        grad_down,
        grad_down_bias,
        norm_sums[2],
        norm_sums[3],
    )
    summed = (
        lax.psum(local_grads[0].astype(jnp.bfloat16), "context").astype(jnp.float32),
        lax.psum(local_grads[1].astype(jnp.bfloat16), "context").astype(jnp.float32),
        lax.psum(local_grads[2].astype(jnp.bfloat16), "context").astype(jnp.float32),
        lax.psum(local_grads[3].astype(jnp.bfloat16), "context").astype(jnp.float32),
        lax.psum(local_grads[4].astype(jnp.bfloat16), "context").astype(jnp.float32),
        lax.psum(local_grads[5].astype(jnp.bfloat16), "context").astype(jnp.float32),
        lax.psum(local_grads[6].astype(jnp.bfloat16), "context").astype(jnp.float32),
        lax.psum(local_grads[7].astype(jnp.bfloat16), "context").astype(jnp.float32),
        lax.psum(local_grads[8].astype(jnp.bfloat16), "context").astype(jnp.float32),
        lax.psum(local_grads[9].astype(jnp.bfloat16), "context").astype(jnp.float32),
        lax.psum(local_grads[10].astype(jnp.bfloat16), "context").astype(jnp.float32),
        lax.psum(local_grads[11].astype(jnp.bfloat16), "context").astype(jnp.float32),
    )
    owned = (
        lax.psum_scatter(
            summed[0].astype(jnp.bfloat16), "fsdp", scatter_dimension=1, tiled=True
        ).astype(jnp.float32),
        lax.psum_scatter(
            summed[1].astype(jnp.bfloat16), "fsdp", scatter_dimension=2, tiled=True
        ).astype(jnp.float32),
        lax.psum_scatter(
            summed[2].astype(jnp.bfloat16), "fsdp", scatter_dimension=1, tiled=True
        ).astype(jnp.float32),
        lax.psum_scatter(
            summed[3].astype(jnp.bfloat16), "fsdp", scatter_dimension=0, tiled=True
        ).astype(jnp.float32),
        lax.psum_scatter(
            summed[4].astype(jnp.bfloat16), "fsdp", scatter_dimension=0, tiled=True
        ).astype(jnp.float32),
        lax.psum_scatter(
            summed[5].astype(jnp.bfloat16), "fsdp", scatter_dimension=0, tiled=True
        ).astype(jnp.float32),
        lax.psum_scatter(
            summed[6].astype(jnp.bfloat16), "fsdp", scatter_dimension=0, tiled=True
        ).astype(jnp.float32),
        lax.psum_scatter(
            summed[7].astype(jnp.bfloat16), "fsdp", scatter_dimension=1, tiled=True
        ).astype(jnp.float32),
        lax.psum_scatter(
            summed[8].astype(jnp.bfloat16), "fsdp", scatter_dimension=1, tiled=True
        ).astype(jnp.float32),
        lax.psum_scatter(
            summed[9].astype(jnp.bfloat16), "fsdp", scatter_dimension=0, tiled=True
        ).astype(jnp.float32),
        lax.psum_scatter(
            summed[10].astype(jnp.bfloat16), "fsdp", scatter_dimension=0, tiled=True
        ).astype(jnp.float32),
        lax.psum_scatter(
            summed[11].astype(jnp.bfloat16), "fsdp", scatter_dimension=0, tiled=True
        ).astype(jnp.float32),
    )
    layer_output = out_rows.reshape(seq_count, span, width)
    tokens_grad = grad_rows.reshape(seq_count, span, width)
    return (
        layer_output,
        tokens_grad,
        owned[0],
        owned[1],
        owned[2],
        owned[3],
        owned[4],
        owned[5],
        owned[6],
        owned[7],
        owned[8],
        owned[9],
        owned[10],
        owned[11],
    )


AXES = ("z", "core", "context", "tensor")
BF = jnp.bfloat16
F32 = jnp.float32
FINE = 128
MASKED = -1e30
NT = (((1,), (1,)), ((), ()))

def attn_fwd_kernel(
    lo_ref, hi_ref, shift_ref, q_ref, k_ref, v_ref, segk_ref, segq_ref, o_ref, lse_ref, vt_ref,
    *, fine, many, hd, scale,
):
    block = pl.program_id(0)
    shift = shift_ref[0]
    bq, pair = q_ref.shape
    pieces = k_ref.shape[0] // fine
    heads = pair // hd

    @pl.when(block == 0)
    def _():
        for j in range(pieces):
            vt_ref[j] = v_ref[j * fine : (j + 1) * fine, :].T

    at = lax.rem(block + shift // (bq // fine), pieces * fine // bq)
    low, high = lo_ref[at], hi_ref[at]
    lane = lax.broadcasted_iota(jnp.int32, (bq, pair), 1) // hd
    q = q_ref[...] * jnp.asarray(scale, BF)
    qs = [jnp.where(lane == h, q, jnp.zeros_like(q)) for h in range(heads)]
    seg_q = segq_ref[0:1, :]

    def body(i, carry):
        j = low + i * many
        spots = [lax.rem(j + u + shift, pieces) for u in range(many)]
        keys = jnp.concatenate([k_ref[aligned(spot * fine, fine), :] for spot in spots])
        values_t = jnp.concatenate([vt_ref[spot] for spot in spots], axis=1)
        seg_k = jnp.concatenate(
            [
                jnp.where(j + u < high, segk_ref[aligned(spot * fine, fine), :], -1)
                for u, spot in enumerate(spots)
            ]
        )
        same = jnp.concatenate([seg_k] * (bq // seg_k.shape[1]), axis=1) == seg_q
        scores = [jnp.where(same, mm_nt(keys, qs[h]), MASKED) for h in range(heads)]
        out = []
        for h in range(heads):
            top, total, acc = carry[h]
            new_top = jnp.maximum(top, jnp.max(scores[h], axis=0, keepdims=True))
            weights = jnp.exp(scores[h] - new_top)
            fade = jnp.exp(top - new_top)
            total = total * fade + jnp.sum(weights, axis=0, keepdims=True)
            acc = acc * fade + mm(values_t[h * hd : (h + 1) * hd, :], weights.astype(BF))
            out.append((new_top, total, acc))
        return tuple(out)

    init = (jnp.full((1, bq), MASKED, F32), jnp.zeros((1, bq), F32), jnp.zeros((hd, bq), F32))
    done = lax.fori_loop(0, (high - low + many - 1) // many, body, (init,) * heads)
    o_ref[...] = jnp.concatenate([acc / total for _, total, acc in done], axis=0).T.astype(BF)
    lse_ref[0] = jnp.concatenate([top + jnp.log(total) for top, total, _ in done], axis=0)


def attn_bwd_kernel(
    lo_ref, hi_ref, shift_ref, q_ref, k_ref, v_ref, o_ref, do_ref, lse_ref, segk_ref, segq_ref, out_ref,
    qs_ref, dos_ref, kt_ref, delta_ref, dqt_ref, dk_ref, dv_ref,
    *, bk, fine, many, hd, scale,
):
    w = pl.program_id(1)
    shift = shift_ref[0]
    rows, pair = q_ref.shape
    pieces = rows // fine
    blocks = rows // bk
    heads = pair // hd

    @pl.when(w == 0)
    def _():
        lane = lax.broadcasted_iota(jnp.int32, (bk, pair), 1) // hd
        head = lax.broadcasted_iota(jnp.int32, (8, pair), 0)
        pick = (head == lax.broadcasted_iota(jnp.int32, (8, pair), 1) // hd).astype(F32)
        factor = jnp.asarray(scale, BF)
        for j in range(blocks):
            r = slice(j * bk, (j + 1) * bk)
            q = q_ref[r, :] * factor
            do = do_ref[r, :]
            for h in range(heads):
                qs_ref[h, r, :] = jnp.where(lane == h, q, jnp.zeros_like(q))
                dos_ref[h, r, :] = jnp.where(lane == h, do, jnp.zeros_like(do))
            kt_ref[j] = (k_ref[r, :] * factor).T
            prod = do.astype(F32) * o_ref[r, :].astype(F32)
            delta_ref[:, r] = lax.dot_general(
                pick, prod, NT, preferred_element_type=F32, precision=lax.Precision.HIGHEST
            )
        dqt_ref[...] = jnp.zeros(dqt_ref.shape, F32)

        def outer(block, _):
            at = lax.rem(block + shift // (bk // fine), blocks)
            low, high = lo_ref[at], hi_ref[at]
            r = aligned(block * bk, bk)
            keys, values = k_ref[r, :], v_ref[r, :]
            seg_k = jnp.concatenate([segk_ref[r, :]] * (many * fine // segk_ref.shape[1]), axis=1)

            def inner(i, carry):
                dk, dv = carry
                j = low + i * many
                spots = [lax.rem(j + u + shift, pieces) for u in range(many)]
                cuts = [aligned(spot * fine, fine) for spot in spots]
                seg_q = jnp.concatenate(
                    [jnp.where(j + u < high, segq_ref[0:1, cut], -1) for u, cut in enumerate(cuts)], axis=1
                )
                same = seg_k == seg_q
                q = [jnp.concatenate([qs_ref[h, cut, :] for cut in cuts]) for h in range(heads)]
                do = [jnp.concatenate([dos_ref[h, cut, :] for cut in cuts]) for h in range(heads)]
                lse = jnp.concatenate([lse_ref[0, :, cut] for cut in cuts], axis=1)
                delta = jnp.concatenate([delta_ref[:, cut] for cut in cuts], axis=1)
                scores = [mm_nt(keys, q[h]) for h in range(heads)]
                dp = [mm_nt(values, do[h]) for h in range(heads)]
                p = [jnp.exp(jnp.where(same, scores[h] - lse[h : h + 1, :], MASKED)) for h in range(heads)]
                p_low = [p[h].astype(BF) for h in range(heads)]
                ds = [(p[h] * (dp[h] - delta[h : h + 1, :])).astype(BF) for h in range(heads)]
                for h in range(heads):
                    hs = slice(h * hd, (h + 1) * hd)
                    dv = dv + mm(p_low[h], do[h])
                    dk = dk + mm(ds[h], q[h])
                    dq = mm(kt_ref[block, hs, :], ds[h])
                    for u in range(many):
                        dqt_ref[spots[u], hs, :] += dq[:, u * fine : (u + 1) * fine]
                return dk, dv

            zero = jnp.zeros((bk, pair), F32)
            dk, dv = lax.fori_loop(0, (high - low + many - 1) // many, inner, (zero, zero))
            dk_ref[r, :] = dk.astype(BF)
            dv_ref[r, :] = dv.astype(BF)
            return 0

        lax.fori_loop(0, blocks, outer, 0)
        for j in range(pieces):
            out_ref[j * fine : (j + 1) * fine, :] = dqt_ref[j].T.astype(BF)

    @pl.when(w == 1)
    def _():
        out_ref[...] = dk_ref[...]

    @pl.when(w == 2)
    def _():
        out_ref[...] = dv_ref[...]


def pair_block(which, pair, group):
    return (pair // group) * 3 * group + which * group + pair % group


def attn_fwd(qkv, seg_k, seg_q, low, high, shift, pair, pairs, group, head_size, bq, many):
    rows, wide = qkv.shape[0], 2 * head_size
    spec = lambda which: pair_block(which, pair, group)
    return pl.pallas_call(
        functools.partial(
            attn_fwd_kernel, fine=FINE, many=many, hd=head_size, scale=float(head_size) ** -0.5
        ),
        out_shape=(
            jax.ShapeDtypeStruct((rows, wide), BF),
            jax.ShapeDtypeStruct((1, 2, rows), F32),
        ),
        grid_spec=pltpu.PrefetchScalarGridSpec(
            num_scalar_prefetch=3,
            grid=(rows // bq,),
            in_specs=[
                pl.BlockSpec((bq, wide), lambda i, *_: (i, spec(0))),
                pl.BlockSpec((rows, wide), lambda i, *_: (0, spec(1))),
                pl.BlockSpec((rows, wide), lambda i, *_: (0, spec(2))),
                pl.BlockSpec((rows, 128), lambda i, *_: (0, 0)),
                pl.BlockSpec((8, bq), lambda i, *_: (0, i)),
            ],
            out_specs=(
                pl.BlockSpec((bq, wide), lambda i, *_: (i, 0)),
                pl.BlockSpec((1, 2, bq), lambda i, *_: (0, 0, i)),
            ),
            scratch_shapes=[pltpu.VMEM((rows // FINE, wide, FINE), BF)],
        ),
        compiler_params=pltpu.CompilerParams(vmem_limit_bytes=24 << 20),
        cost_estimate=pl.CostEstimate(
            flops=15_000_000_000, bytes_accessed=rows * wide * 8, transcendentals=rows * rows // 2
        ),
        name="attn_fwd",
    )(low, high, shift, qkv, qkv, qkv, seg_k, seg_q)


def attn_bwd(qkv, mixed, dctx, lse, seg_k, seg_q, low, high, shift, pairs, group, head_size, bk, many):
    rows, wide = qkv.shape[0], 2 * head_size
    blocks = rows // bk
    column = lambda which: pl.BlockSpec((rows, wide), lambda p, w, *_: (0, pair_block(which, p, group)))
    own = pl.BlockSpec((rows, wide), lambda p, w, *_: (0, p))
    return pl.pallas_call(
        functools.partial(
            attn_bwd_kernel, bk=bk, fine=FINE, many=many, hd=head_size, scale=float(head_size) ** -0.5
        ),
        out_shape=jax.ShapeDtypeStruct(qkv.shape, BF),
        grid_spec=pltpu.PrefetchScalarGridSpec(
            num_scalar_prefetch=3,
            grid=(pairs, 3),
            in_specs=[
                column(0),
                column(1),
                column(2),
                own,
                own,
                pl.BlockSpec((1, 2, rows), lambda p, w, *_: (p, 0, 0)),
                pl.BlockSpec((rows, 128), lambda p, w, *_: (0, 0)),
                pl.BlockSpec((8, rows), lambda p, w, *_: (0, 0)),
            ],
            out_specs=pl.BlockSpec((rows, wide), lambda p, w, *_: (0, pair_block(w, p, group))),
            scratch_shapes=[
                pltpu.VMEM((2, rows, wide), BF),
                pltpu.VMEM((2, rows, wide), BF),
                pltpu.VMEM((blocks, wide, bk), BF),
                pltpu.VMEM((8, rows), F32),
                pltpu.VMEM((rows // FINE, wide, FINE), F32),
                pltpu.VMEM((rows, wide), BF),
                pltpu.VMEM((rows, wide), BF),
            ],
        ),
        compiler_params=pltpu.CompilerParams(vmem_limit_bytes=58 << 20),
        cost_estimate=pl.CostEstimate(
            flops=100_000_000_000, bytes_accessed=rows * wide * 64, transcendentals=2 * rows * rows
        ),
        name="attn_bwd",
    )(low, high, shift, qkv, qkv, qkv, mixed, dctx, lse, seg_k, seg_q)


def segment_bounds(seg_rows, row_block, col_block):
    blocks = seg_rows.reshape(-1, row_block)
    low = jnp.sum(seg_rows[None, :] < blocks[:, :1], axis=1) // col_block
    high = (jnp.sum(seg_rows[None, :] <= blocks[:, -1:], axis=1) + col_block - 1) // col_block
    return low.astype(jnp.int32), high.astype(jnp.int32)


def norm_forward(rows):
    mean = jnp.mean(rows, axis=-1, keepdims=True)
    centred = rows - mean
    inv = lax.rsqrt(jnp.mean(centred * centred, axis=-1, keepdims=True) + NORM_EPS)
    return centred * inv, inv


def norm_backward(grad, normed, inv):
    return inv * (
        grad
        - jnp.mean(grad, axis=-1, keepdims=True)
        - normed * jnp.mean(grad * normed, axis=-1, keepdims=True)
    )


def after(value, *others):
    return lax.optimization_barrier((value,) + others)[0]


def mm(a, b):
    return jnp.dot(a, b, preferred_element_type=F32)


def mm_nt(a, b):
    return lax.dot_general(a, b, (((1,), (1,)), ((), ())), preferred_element_type=F32)


def mm_tn(a, b):
    return lax.dot_general(a, b, (((0,), (0,)), ((), ())), preferred_element_type=F32)


def remote(src, dst, send_sem, recv_sem, device):
    return pltpu.make_async_remote_copy(
        src_ref=src,
        dst_ref=dst,
        send_sem=send_sem,
        recv_sem=recv_sem,
        device_id=device,
        device_id_type=pl.DeviceIdType.MESH,
    )


def greet(devices):
    barrier = pltpu.get_barrier_semaphore()
    for device in devices:
        pl.semaphore_signal(barrier, inc=1, device_id=device, device_id_type=pl.DeviceIdType.MESH)
    pl.semaphore_wait(barrier, len(devices))


def aligned(start, size):
    return pl.ds(pl.multiple_of(start, size), size)


def open_kernel(
    tokens, weight, small, xt_out, w_out, qkv_out, small_out,
    x, xt, w, qkv, smalls, fill_x, fill_w, x_send, x_recv, s_send, s_recv, y_sems, z_send, z_recv,
    c_send, c_recv, out_sems,
    *, nz, nt, heads, head_size, group, chunk,
):
    z, k, c, t = (lax.axis_index(name) for name in AXES)
    f = z * 2 + k
    nf = nz * 2
    span, width = tokens.shape[1:]
    dblk = weight.shape[1]
    cols = heads * head_size
    gw = group * 2 * head_size
    chunks = span // chunk
    peers = [
        (dz, dk, dt) for dz in range(nz) for dk in range(2) for dt in range(nt) if (dz, dk, dt) != (0, 0, 0)
    ]

    def peer(offset):
        dz, dk, dt = offset
        return {"z": lax.rem(z + dz, nz), "core": lax.rem(k + dk, 2), "tensor": lax.rem(t + dt, nt)}

    def block(index):
        return w.at[aligned(index * dblk, dblk), :]

    for i in range(chunks):
        r = pl.ds(i * chunk, chunk)
        pltpu.make_async_copy(tokens.at[t, r], x.at[r], fill_x.at[i]).start()
    fills = []
    for g in range(cols // gw):
        for which in range(3):
            at = (g * 3 + which) * gw
            fills.append(
                pltpu.make_async_copy(
                    weight.at[which, :, pl.ds(g * gw, gw)],
                    w.at[aligned(f * dblk, dblk), pl.ds(at, gw)],
                    fill_w.at[len(fills)],
                )
            )

    @pl.when(c == t)
    def _():
        for one in fills:
            one.start()

    greet([{"context": 1 - c}] + [peer(offset) for offset in peers])
    x_copies = [
        remote(
            tokens.at[t, pl.ds(i * chunk, chunk)],
            x.at[pl.ds(span + i * chunk, chunk)],
            x_send.at[i],
            x_recv.at[i],
            {"context": 1 - c},
        )
        for i in range(chunks)
    ]
    for one in x_copies:
        one.start()
    y_copy = remote(block(f), block(f), y_sems.at[0], y_sems.at[1], {"tensor": 1 - t})

    @pl.when(c == t)
    def _():
        for one in fills:
            one.wait()
        y_copy.start()

    def small_copy(i, source):
        return remote(small, smalls.at[source], s_send.at[i], s_recv.at[source], peer(peers[i]))

    me = f * nt + t
    for i in range(len(peers)):
        small_copy(i, me).start()
    smalls[me] = small[...]

    @pl.when(c != t)
    def _():
        y_copy.wait_recv()

    def z_copy(d, owner):
        return remote(
            block(owner * 2 + k), block(owner * 2 + k), z_send.at[d - 1], z_recv.at[owner], {"z": lax.rem(z + d, nz)}
        )

    def c_copy(owner, core):
        return remote(
            block(owner * 2 + core), block(owner * 2 + core), c_send.at[owner], c_recv.at[owner], {"core": 1 - k}
        )

    for d in range(1, nz):
        z_copy(d, z).start()
    c_copy(z, k).start()

    for i in range(chunks):
        r = pl.ds(i * chunk, chunk)
        pltpu.make_async_copy(tokens.at[t, r], x.at[r], fill_x.at[i]).wait()
        xt[:, i * chunk : (i + 1) * chunk] = x[i * chunk : (i + 1) * chunk, :].T

    for i in range(len(peers)):
        dz, dk, dt = peers[i]
        source = (lax.rem(z + nz - dz, nz) * 2 + lax.rem(k + dk, 2)) * nt + lax.rem(t + nt - dt, nt)
        small_copy(i, source).wait_recv()

    edge = head_size // nf
    lanes = small.shape[1]
    rows = jnp.concatenate([smalls[fi * nt + c, 0:1, :] for fi in range(nf)], axis=0)
    col = lax.broadcasted_iota(jnp.int32, (lanes, cols), 1)
    source = lax.broadcasted_iota(jnp.int32, (lanes, cols), 0)
    fcol = lax.broadcasted_iota(jnp.int32, (nf, cols), 1)
    mine = lax.rem(fcol, head_size) // edge == lax.broadcasted_iota(jnp.int32, (nf, cols), 0)
    biases = []
    for kind in range(2):
        pick = source == col // head_size * edge + lax.rem(col, edge) + kind * heads * edge
        spread_out = mm(rows, jnp.where(pick, 1.0, 0.0).astype(BF))
        biases.append(jnp.sum(jnp.where(mine, spread_out, 0.0), axis=0, keepdims=True))
    parts = [biases[0], jnp.zeros_like(biases[0]), biases[1]]
    bias = jnp.concatenate(
        [parts[which][:, g * gw : (g + 1) * gw] for g in range(cols // gw) for which in range(3)], axis=1
    )

    for d in range(1, nz):
        owner = lax.rem(z + nz - d, nz)
        z_copy(d, owner).wait_recv()
        c_copy(owner, k).start()
    for owner in range(nz):
        c_copy(owner, 1 - k).wait_recv()

    w_done = pltpu.make_async_copy(w, w_out, out_sems.at[0, 0])
    w_done.start()
    small_done = pltpu.make_async_copy(smalls, small_out, out_sems.at[0, 1])
    small_done.start()

    def project(i):
        r = aligned(i * chunk, chunk)
        acc = mm(x[r, :], w[...]) + bias
        qkv[r, :] = acc.astype(BF)
        pltpu.make_async_copy(qkv.at[r], qkv_out.at[r], out_sems.at[1, i]).start()

    @pl.loop(0, chunks)
    def _(i):
        project(i)

    @pl.loop(0, chunks)
    def _(i):
        remote(
            tokens.at[t, aligned(i * chunk, chunk)],
            x.at[aligned(span + i * chunk, chunk)],
            x_send.at[i],
            x_recv.at[i],
            {"context": 1 - c},
        ).wait_recv()
        r = aligned(span + i * chunk, chunk)
        xt[:, r] = x[r, :].T
        project(chunks + i)

    xt_done = pltpu.make_async_copy(xt, xt_out, out_sems.at[0, 2])
    xt_done.start()
    for i in range(2 * chunks):
        r = pl.ds(i * chunk, chunk)
        pltpu.make_async_copy(qkv.at[r], qkv_out.at[r], out_sems.at[1, i]).wait()
    for one in (w_done, small_done, xt_done):
        one.wait()
    for one in x_copies:
        one.wait_send()
    for i in range(len(peers)):
        small_copy(i, me).wait_send()
    for d in range(1, nz):
        z_copy(d, z).wait_send()
    for owner in range(nz):
        c_copy(owner, k).wait_send()

    @pl.when(c == t)
    def _():
        y_copy.wait_send()


def open_layer(tokens, weight, small, nz, nt, heads, head_size, group):
    span, width = tokens.shape[1:]
    cols = heads * head_size
    chunk = 256
    chunks = span // chunk
    nf = nz * 2
    dma = pltpu.SemaphoreType.DMA
    hbm = pl.BlockSpec(memory_space=pl.ANY)
    fixed = pl.BlockSpec(memory_space=pltpu.HBM)
    moved = 2 * (span * width * 2 + 4 * width * cols * 3)
    return pl.pallas_call(
        functools.partial(
            open_kernel, nz=nz, nt=nt, heads=heads, head_size=head_size, group=group, chunk=chunk
        ),
        out_shape=(
            jax.ShapeDtypeStruct((width, 2 * span), BF),
            jax.ShapeDtypeStruct((width, 3 * cols), BF),
            jax.ShapeDtypeStruct((2 * span, 3 * cols), BF),
            jax.ShapeDtypeStruct((nf * nt,) + small.shape, BF),
        ),
        in_specs=[fixed, fixed, pl.BlockSpec(memory_space=pltpu.VMEM)],
        out_specs=(hbm,) * 4,
        scratch_shapes=[
            pltpu.VMEM((2 * span, width), BF),
            pltpu.VMEM((width, 2 * span), BF),
            pltpu.VMEM((width, 3 * cols), BF),
            pltpu.VMEM((2 * span, 3 * cols), BF),
            pltpu.VMEM((nf * nt,) + small.shape, BF),
            dma((chunks,)),
            dma((heads // 2 // group * 3,)),
            dma((chunks,)),
            dma((chunks,)),
            dma((nf * nt,)),
            dma((nf * nt,)),
            dma((2,)),
            dma((nz,)),
            dma((nz,)),
            dma((nz,)),
            dma((nz,)),
            dma((2, max(3, 2 * chunks))),
        ],
        compiler_params=pltpu.CompilerParams(
            collective_id=0, has_side_effects=True, vmem_limit_bytes=58 << 20
        ),
        cost_estimate=pl.CostEstimate(
            flops=2 * 2 * span * width * 3 * cols, bytes_accessed=moved, transcendentals=0
        ),
        name="open_layer",
    )(tokens, weight, small)


def close_kernel(
    dqkv_in, w_in, xt_in, grad_in, vec_one, vec_two, tokens_out, grad_out, sums_out, vec_out,
    dqkv, w, xt, dres, own, xs, xr, fin, away, near, zs, zr, piece, last,
    sums, sums_near, sums_z, sums_last, vecs, vecs_near, vecs_z, vecs_last,
    fill, x_send, x_recv, y_send, y_recv, c_send, c_recv, z_send, z_recv, p_send, p_recv, o_sems,
    *, nz, chunk, tile, part,
):
    z, k, c, t = (lax.axis_index(name) for name in AXES)
    rows, wide = dqkv.shape
    span = rows // 2
    dblk = piece.shape[0]
    chunks = span // chunk
    steps = wide // tile
    x_dev, y_dev, core_dev = {"context": 1 - c}, {"tensor": 1 - t}, {"core": 1 - k}
    diag = {"context": 1 - c, "tensor": 1 - t}

    loads = [
        pltpu.make_async_copy(w_in, w, fill.at[0]),
        pltpu.make_async_copy(dqkv_in.at[pl.ds(span, span)], dqkv.at[pl.ds(span, span)], fill.at[1]),
        pltpu.make_async_copy(dqkv_in.at[pl.ds(0, span)], dqkv.at[pl.ds(0, span)], fill.at[2]),
    ]
    for kk in range(2):
        for zi in range(nz):
            source = zi * 2 + lax.rem(1 - k + kk, 2)
            loads.append(
                pltpu.make_async_copy(
                    xt_in.at[aligned(source * dblk, dblk)], xt.at[kk, pl.ds(zi * dblk, dblk)], fill.at[len(loads)]
                )
            )
    for source, dest in (
        (grad_in, dres),
        (vec_one, vecs.at[pl.ds(0, 8)]),
        (vec_two, vecs.at[pl.ds(8, 8)]),
    ):
        loads.append(pltpu.make_async_copy(source, dest, fill.at[len(loads)]))
    for one in loads:
        one.start()
    greet([x_dev, y_dev, diag, core_dev] + [{"z": lax.rem(z + d, nz)} for d in range(1, nz)])

    def x_copy(i):
        return remote(xs.at[i], xr.at[i], x_send.at[i], x_recv.at[i], x_dev)

    def y_copy(i):
        return remote(fin.at[i], tokens_out.at[t, aligned(i * chunk, chunk)], y_send.at[i], y_recv.at[i], y_dev)

    def leave(i):
        value = mm_nt(dqkv[aligned(span + i * 2 * chunk, 2 * chunk), :], w[...]).astype(BF)
        xs[2 * i] = value[:chunk]
        xs[2 * i + 1] = value[chunk:]
        x_copy(2 * i).start()
        x_copy(2 * i + 1).start()

    loads[0].wait()
    loads[1].wait()

    @pl.loop(0, 1)
    def _(i):
        leave(i)

    for one in loads[2:]:
        one.wait()
    ones = jnp.ones((8, rows), BF)
    sums[...] = jnp.zeros(sums.shape, F32)

    @pl.loop(0, steps)
    def _(j):
        value = dqkv[:, aligned(j * tile, tile)]
        away[:, aligned(j * tile, tile)] = mm(xt[0], value).astype(BF)
        total = mm(ones, value)
        for u in range(tile // 128):
            sums[pl.ds(j * (tile // 128) + u, 1), :] = total[0:1, u * 128 : (u + 1) * 128]

    core_copies = [
        remote(mine, theirs, c_send.at[i], c_recv.at[i], core_dev)
        for i, (mine, theirs) in enumerate(((away, near), (sums, sums_near), (vecs, vecs_near)))
    ]
    for one in core_copies:
        one.start()

    @pl.loop(1, chunks // 2)
    def _(i):
        leave(i)

    for one in core_copies:
        one.wait_recv()
    sums_z[z] = sums[...] + sums_near[...]
    vecs_z[z] = vecs[...] + vecs_near[...]

    @pl.loop(0, steps)
    def _(j):
        cut = aligned(j * tile, tile)
        zs[:, cut] = (mm(xt[1], dqkv[:, cut]) + near[:, cut].astype(F32)).astype(BF)

    def z_copies(d, owner):
        dev = {"z": lax.rem(z + d, nz)}
        return [
            remote(buf.at[owner], buf.at[owner], z_send.at[i, d - 1], z_recv.at[i, owner], dev)
            for i, buf in enumerate((sums_z, vecs_z))
        ]

    def ring(step):
        source = zs.at[aligned(lax.rem(z + nz - step, nz) * dblk, dblk)]
        return remote(source, zr.at[step - 1], z_send.at[2, step - 1], z_recv.at[2, step - 1], {"z": lax.rem(z + 1, nz)})

    def arrived(step):
        ring(step).wait_recv()
        spot = aligned(lax.rem(z + 2 * nz - step - 1, nz) * dblk, dblk)
        zs[spot, :] = (zs[spot, :].astype(F32) + zr[step - 1].astype(F32)).astype(BF)
        if step + 1 < nz:
            ring(step + 1).start()

    ring(1).start()
    for d in range(1, nz):
        for one in z_copies(d, z):
            one.start()

    @pl.loop(0, chunks // 2)
    def _(i):
        r = aligned(i * 2 * chunk, 2 * chunk)
        own[r, :] = mm_nt(dqkv[r, :], w[...]) + dres[r, :]

    def finish(i):
        x_copy(i).wait_recv()
        r = aligned(i * chunk, chunk)
        fin[i] = (own[r, :] + xr[i].astype(F32)).astype(BF)
        pltpu.make_async_copy(fin.at[i], tokens_out.at[t, r], o_sems.at[i]).start()
        y_copy(i).start()

    cuts = [chunks * step // nz for step in range(nz + 1)]
    for step in range(1, nz):
        pl.loop(cuts[step - 1], cuts[step])(finish)
        arrived(step)
    for d in range(1, nz):
        for one in z_copies(d, lax.rem(z + nz - d, nz)):
            one.wait_recv()
    piece[...] = zs[aligned(z * dblk, dblk), :]
    sums_last[0] = jnp.sum(sums_z[...], axis=0)
    vecs_last[0] = jnp.sum(vecs_z[...], axis=0)

    trio = ((x_dev, 0), (y_dev, 1), (diag, 2))
    p_x, p_y, p_d = (remote(piece, last.at[i], p_send.at[i], p_recv.at[i], dev) for dev, i in trio)
    everywhere = [
        remote(buf.at[0], buf.at[1 + i], p_send.at[at + i], p_recv.at[at + i], dev)
        for dev, i in trio
        for buf, at in ((sums_last, 3), (vecs_last, 6))
    ]
    for one in everywhere:
        one.start()

    @pl.when(c == t)
    def _():
        p_x.start()

    @pl.when(c != t)
    def _():
        p_y.start()
        p_d.start()

    pl.loop(cuts[nz - 1], chunks)(finish)

    def give(value):
        width = part
        for g in range(wide // (3 * width)):
            for which in range(3):
                at = (g * 3 + which) * width
                grad_out[which, :, g * width : (g + 1) * width] = value[:, at : at + width]

    for one in everywhere:
        one.wait()
    near_pair = sums_last[0] + sums_last[2]
    sums_out[...] = jnp.where(c == t, near_pair, sums_last[1] + sums_last[3])
    vec_out[...] = (vecs_last[0] + vecs_last[2]) + (vecs_last[1] + vecs_last[3])

    @pl.when(c == t)
    def _():
        p_y.wait_recv()
        give(piece[...].astype(F32) + last[1].astype(F32))
        p_x.wait_send()

    @pl.when(c != t)
    def _():
        p_x.wait_recv()
        p_d.wait_recv()
        give(last[0].astype(F32) + last[2].astype(F32))
        p_y.wait_send()
        p_d.wait_send()

    for one in core_copies:
        one.wait_send()
    for d in range(1, nz):
        ring(d).wait_send()
        for one in z_copies(d, z):
            one.wait_send()

    @pl.loop(0, chunks)
    def _(i):
        r = aligned(i * chunk, chunk)
        x_copy(i).wait_send()
        pltpu.make_async_copy(fin.at[i], tokens_out.at[t, r], o_sems.at[i]).wait()
        y_copy(i).wait_send()
        remote(fin.at[i], tokens_out.at[1 - t, r], y_send.at[i], y_recv.at[i], y_dev).wait_recv()


def close_layer(dqkv, w, xt, grad_in, vec_one, vec_two, nz, part):
    rows, wide = dqkv.shape
    width = w.shape[0]
    span = rows // 2
    dblk = width // (2 * nz)
    chunk, tile = 128, 256
    chunks = span // chunk
    dma = pltpu.SemaphoreType.DMA
    hbm = pl.BlockSpec(memory_space=pl.ANY)
    vmem = pl.BlockSpec(memory_space=pltpu.VMEM)
    sum_shape = (wide // 128 + -(wide // 128) % 8, 128)
    vec_shape = (16, width)
    return pl.pallas_call(
        functools.partial(close_kernel, nz=nz, chunk=chunk, tile=tile, part=part),
        out_shape=(
            jax.ShapeDtypeStruct((2, span, width), BF),
            jax.ShapeDtypeStruct((3, dblk, wide // 3), F32),
            jax.ShapeDtypeStruct(sum_shape, F32),
            jax.ShapeDtypeStruct(vec_shape, F32),
        ),
        in_specs=[hbm] * 6,
        out_specs=(hbm, vmem, vmem, vmem),
        scratch_shapes=[
            pltpu.VMEM((rows, wide), BF),
            pltpu.VMEM((width, wide), BF),
            pltpu.VMEM((2, nz * dblk, rows), BF),
            pltpu.VMEM((span, width), F32),
            pltpu.VMEM((span, width), F32),
            pltpu.VMEM((chunks, chunk, width), BF),
            pltpu.VMEM((chunks, chunk, width), BF),
            pltpu.VMEM((chunks, chunk, width), BF),
            pltpu.VMEM((nz * dblk, wide), BF),
            pltpu.VMEM((nz * dblk, wide), BF),
            pltpu.VMEM((nz * dblk, wide), BF),
            pltpu.VMEM((nz, dblk, wide), BF),
            pltpu.VMEM((dblk, wide), BF),
            pltpu.VMEM((3, dblk, wide), BF),
            pltpu.VMEM(sum_shape, F32),
            pltpu.VMEM(sum_shape, F32),
            pltpu.VMEM((nz,) + sum_shape, F32),
            pltpu.VMEM((4,) + sum_shape, F32),
            pltpu.VMEM(vec_shape, F32),
            pltpu.VMEM(vec_shape, F32),
            pltpu.VMEM((nz,) + vec_shape, F32),
            pltpu.VMEM((4,) + vec_shape, F32),
            dma((6 + 2 * nz,)),
            dma((chunks,)),
            dma((chunks,)),
            dma((chunks,)),
            dma((chunks,)),
            dma((3,)),
            dma((3,)),
            dma((3, nz)),
            dma((3, nz)),
            dma((9,)),
            dma((9,)),
            dma((chunks,)),
        ],
        compiler_params=pltpu.CompilerParams(
            collective_id=1, has_side_effects=True, vmem_limit_bytes=46 << 20
        ),
        cost_estimate=pl.CostEstimate(
            flops=4 * rows * width * wide, bytes_accessed=30 << 20, transcendentals=0
        ),
        name="close_layer",
    )(dqkv, w, xt, grad_in, vec_one, vec_two)


def mean_of(rows):
    return jnp.mean(rows, axis=-1, keepdims=True)


def load_blocks(stack, start, dest, sems, nt, rows_by_f):
    count, rows = stack.shape[:2]
    columns = dest.shape[1] // nt if rows_by_f else stack.shape[2]
    copies = []
    for b in range(count):
        first, second = (b // nt, b % nt) if rows_by_f else (b % nt, b // nt)
        spot = dest.at[pl.ds(first * rows, rows), pl.ds(second * columns, columns)]
        copies.append(pltpu.make_async_copy(stack.at[b, :, pl.ds(start, columns)], spot, sems.at[b]))
    return copies


def up_kernel(
    t_ref, ctx, tok, vecs, up_add, up_in, first, norm_one, inv_one, first_t, act, slope,
    up, proj, low, u, fill,
    *, nt, tile,
):
    i = pl.program_id(0)
    width, hidden = up.shape
    tiles = hidden // tile
    up_fill = load_blocks(up_in, 0, up, fill.at[0], nt, True)
    proj_fill = load_blocks(up_in, hidden // nt, proj, fill.at[1], nt, True)

    @pl.when(i == 0)
    def _():
        for one in proj_fill + up_fill:
            one.start()
        for one in proj_fill:
            one.wait()

    def vec(row):
        return vecs[row : row + 1, :]

    h = tok[0].astype(F32) + (mm_nt(ctx[...], proj[...]) + vec(0))
    centred = h - mean_of(h)
    inv = lax.rsqrt(mean_of(centred * centred) + NORM_EPS)
    normed = centred * inv
    norm_one[...] = normed
    inv_one[...] = jnp.broadcast_to(inv, inv_one.shape)
    normed = normed * vec(1) + vec(2)
    first[...] = normed
    low[...] = normed.astype(BF)
    first_t[...] = low[...].T

    @pl.when(i == 0)
    def _():
        for one in up_fill:
            one.wait()

    u[0] = mm(low[...], up[:, :tile])

    def activate(j, slot):
        cut = aligned(j * tile, tile)
        value = u[slot] + up_add[0:1, cut]
        phi = 0.5 + 0.5 * lax.erf(value * (0.5**0.5))
        act[:, cut] = (value * phi).astype(BF)
        slope[:, cut] = (phi + value * (jnp.exp(-0.5 * value * value) * ((2.0 * jnp.pi) ** -0.5))).astype(BF)

    @pl.loop(0, tiles - 1)
    def _(j):
        slot = lax.rem(j, 2)
        following = mm(low[...], up[:, aligned((j + 1) * tile, tile)])
        activate(j, slot)
        u[1 - slot] = following

    activate(tiles - 1, (tiles - 1) % 2)


def up_layer(t, ctx, tokens, vecs, up_add, up_all, nt):
    span, width = ctx.shape
    hidden = up_add.shape[1]
    block, tile = 512, 512
    hbm = pl.BlockSpec(memory_space=pl.ANY)
    rows = pl.BlockSpec((block, width), lambda i, _: (i, 0))
    wide = pl.BlockSpec((block, hidden), lambda i, _: (i, 0))
    whole = lambda shape: pl.BlockSpec(shape, lambda i, _: (0,) * len(shape))
    picked = pl.BlockSpec((1, block, width), lambda i, t_ref: (t_ref[0], i, 0))
    sds = jax.ShapeDtypeStruct
    return pl.pallas_call(
        functools.partial(up_kernel, nt=nt, tile=tile),
        out_shape=(
            sds((span, width), F32),
            sds((span, width), F32),
            sds((span, 128), F32),
            sds((width, span), BF),
            sds((span, hidden), BF),
            sds((span, hidden), BF),
        ),
        grid_spec=pltpu.PrefetchScalarGridSpec(
            num_scalar_prefetch=1,
            grid=(span // block,),
            in_specs=[rows, picked, whole(vecs.shape), whole(up_add.shape), hbm],
            out_specs=(
                rows,
                rows,
                pl.BlockSpec((block, 128), lambda i, _: (i, 0)),
                pl.BlockSpec((width, block), lambda i, _: (0, i)),
                wide,
                wide,
            ),
            scratch_shapes=[
                pltpu.VMEM((width, hidden), BF),
                pltpu.VMEM((width, width), BF),
                pltpu.VMEM((block, width), BF),
                pltpu.VMEM((2, block, tile), F32),
                pltpu.SemaphoreType.DMA((2, up_all.shape[0])),
            ],
        ),
        compiler_params=pltpu.CompilerParams(vmem_limit_bytes=60 << 20),
        cost_estimate=pl.CostEstimate(
            flops=2 * span * width * (width + hidden), bytes_accessed=40 << 20, transcendentals=2 * span * hidden
        ),
        name="up_layer",
    )(t, ctx, tokens, vecs, up_add, up_all)


def add_rows(sums, row, value):
    sums[row] += jnp.sum(value.reshape(-1, 8, value.shape[1]), axis=0)


def down_kernel(
    t_ref, cot, vecs, first, act, down_in, out, branch, branch_t, grad_second, vec_sums,
    down, acc, sums, fill,
    *, nt,
):
    i = pl.program_id(0)
    hidden, width = down.shape
    down_fill = load_blocks(down_in, 0, down, fill, nt, False)

    @pl.when(i == 0)
    def _():
        for one in down_fill:
            one.start()
        sums[...] = jnp.zeros(sums.shape, F32)

    def vec(row):
        return vecs[row : row + 1, :]

    tile = 256
    per = len(down_fill) * tile // width

    @pl.loop(0, width // tile)
    def _(j):
        for ji in range(width // tile):

            @pl.when((i == 0) & (j == ji))
            def _():
                for one in down_fill[ji * per : (ji + 1) * per]:
                    one.wait()

        cut = aligned(j * tile, tile)
        acc[:, cut] = mm(act[...], down[:, cut])

    h = first[...] + (acc[...] + vec(3))
    centred = h - mean_of(h)
    inv = lax.rsqrt(mean_of(centred * centred) + NORM_EPS)
    normed = centred * inv
    out[...] = (normed * vec(4) + vec(5)).astype(BF)
    grad = cot[0].astype(F32)
    add_rows(sums, 1, grad * normed)
    add_rows(sums, 2, grad)
    grad = grad * vec(4)
    grad = inv * (grad - mean_of(grad) - normed * mean_of(grad * normed))
    grad_second[...] = grad
    low = grad.astype(BF)
    branch[...] = low
    add_rows(sums, 0, low.astype(F32))
    branch_t[...] = low.T

    @pl.when(i == pl.num_programs(0) - 1)
    def _():
        for row in range(3):
            vec_sums[row : row + 1, :] = jnp.sum(sums[row], axis=0, keepdims=True)
        vec_sums[3:8, :] = jnp.zeros((5, width), F32)


def down_layer(t, out_grad, vecs, first, act, down_all, nt):
    span, width = first.shape
    hidden = act.shape[1]
    block = 512
    rows = pl.BlockSpec((block, width), lambda i, _: (i, 0))
    whole = lambda shape: pl.BlockSpec(shape, lambda i, _: (0,) * len(shape))
    sds = jax.ShapeDtypeStruct
    return pl.pallas_call(
        functools.partial(down_kernel, nt=nt),
        out_shape=(
            sds((span, width), BF),
            sds((span, width), BF),
            sds((width, span), BF),
            sds((span, width), F32),
            sds((8, width), F32),
        ),
        grid_spec=pltpu.PrefetchScalarGridSpec(
            num_scalar_prefetch=1,
            grid=(span // block,),
            in_specs=[
                pl.BlockSpec((1, block, width), lambda i, t_ref: (t_ref[0], i, 0)),
                whole(vecs.shape),
                rows,
                pl.BlockSpec((block, hidden), lambda i, _: (i, 0)),
                pl.BlockSpec(memory_space=pl.ANY),
            ],
            out_specs=(rows, rows, pl.BlockSpec((width, block), lambda i, _: (0, i)), rows, whole((8, width))),
            scratch_shapes=[
                pltpu.VMEM((hidden, width), BF),
                pltpu.VMEM((block, width), F32),
                pltpu.VMEM((3, 8, width), F32),
                pltpu.SemaphoreType.DMA((down_all.shape[0],)),
            ],
        ),
        compiler_params=pltpu.CompilerParams(vmem_limit_bytes=60 << 20),
        cost_estimate=pl.CostEstimate(
            flops=2 * span * width * hidden, bytes_accessed=30 << 20, transcendentals=0
        ),
        name="down_layer",
    )(t, out_grad, vecs, first, act, down_all)


def back_kernel(
    vecs, branch, grad_second, slope, norm_one, inv_one, up_in, down_in, partial,
    hid, attn_t, grad_in, grad_ctx, vec_sums, quarter,
    up, down, proj, acc, sums, sums_u, by_y, near_y, by_x, near_x, last_x, last_y,
    fill, own_fill, one_send, one_recv, two_send, two_recv,
    *, nz, nt, tile,
):
    i = pl.program_id(0)
    c, t = lax.axis_index("context"), lax.axis_index("tensor")
    x_dev, y_dev = {"context": 1 - c}, {"tensor": 1 - t}
    width, hidden = up.shape
    rest = last_x.shape[0] // nz
    half = last_x.shape[1]
    tall = nz * 2 * rest
    left, right = pl.ds(0, half), pl.ds(half, half)
    own_copies = [pltpu.make_async_copy(partial.at[aligned(t * tall, tall), left], by_y, own_fill.at[0])]
    first_copies = [
        remote(partial.at[aligned((1 - t) * tall, tall), left], near_y, one_send.at[0], one_recv.at[0], y_dev)
    ]
    for b in range(nt * nz):
        spot = pl.ds(b * rest, rest)
        own_copies.append(
            pltpu.make_async_copy(
                partial.at[aligned((b * 2 + c) * rest, rest), right], by_x.at[spot], own_fill.at[1 + b]
            )
        )
        first_copies.append(
            remote(
                partial.at[aligned((b * 2 + 1 - c) * rest, rest), right],
                near_x.at[spot],
                one_send.at[1 + b],
                one_recv.at[1 + b],
                x_dev,
            )
        )
    second_copies = [
        remote(by_x.at[aligned((1 - t) * nz * rest, nz * rest)], last_y, two_send.at[0], two_recv.at[0], y_dev)
    ]
    for zi in range(nz):
        second_copies.append(
            remote(
                by_y.at[aligned((zi * 2 + 1 - c) * rest, rest)],
                last_x.at[pl.ds(zi * rest, rest)],
                two_send.at[1 + zi],
                two_recv.at[1 + zi],
                x_dev,
            )
        )

    @pl.when(i == 0)
    def _():
        greet([x_dev, y_dev])
        for one in first_copies + own_copies:
            one.start()

    @pl.when(i == 2)
    def _():
        for one in own_copies:
            one.wait()
        for one in first_copies:
            one.wait_recv()
        by_y[...] = (by_y[...].astype(F32) + near_y[...].astype(F32)).astype(BF)
        by_x[...] = (by_x[...].astype(F32) + near_x[...].astype(F32)).astype(BF)
        for one in second_copies:
            one.start()

    down_fill = load_blocks(down_in, 0, down, fill.at[0], nt, False)
    up_fill = load_blocks(up_in, 0, up, fill.at[1], nt, True)
    proj_fill = load_blocks(up_in, hidden // nt, proj, fill.at[2], nt, True)

    @pl.when(i == 0)
    def _():
        for ti in range(nt):
            for one in down_fill[ti::nt] + up_fill[ti::nt]:
                one.start()
        for one in proj_fill:
            one.start()
        sums[...] = jnp.zeros(sums.shape, F32)
        sums_u[...] = jnp.zeros(sums_u.shape, F32)

    ones = jnp.ones((8, branch.shape[0]), BF)
    acc[...] = grad_second[...]
    per = hidden // tile // nt

    @pl.loop(0, hidden // tile)
    def _(j):
        for ti in range(nt):

            @pl.when((i == 0) & (j == ti * per))
            def _():
                for one in down_fill[ti::nt] + up_fill[ti::nt]:
                    one.wait()

        cut = aligned(j * tile, tile)
        low_hid = (mm_nt(branch[...], down[cut, :]) * slope[:, cut].astype(F32)).astype(BF)
        hid[:, cut] = low_hid
        sums_u[:, cut] += mm(ones, low_hid)
        acc[...] += mm_nt(low_hid, up[:, cut])

    grad = acc[...]
    normed = norm_one[...]
    add_rows(sums, 1, grad * normed)
    add_rows(sums, 2, grad)
    grad = grad * vecs[1:2, :]
    grad = inv_one[:, 0:1] * (grad - mean_of(grad) - normed * mean_of(grad * normed))
    grad_in[...] = grad
    low = grad.astype(BF)
    add_rows(sums, 0, low.astype(F32))
    attn_t[...] = low.T

    @pl.when(i == 0)
    def _():
        for one in proj_fill:
            one.wait()

    grad_ctx[...] = mm(low, proj[...]).astype(BF)

    @pl.when(i == pl.num_programs(0) - 1)
    def _():
        for row in range(3):
            vec_sums[row : row + 1, :] = jnp.sum(sums[row], axis=0, keepdims=True)
        vec_sums[3:8, :] = jnp.zeros((5, width), F32)
        for row in range(hidden // width):
            vec_sums[3 + row : 4 + row, :] = sums_u[0:1, row * width : (row + 1) * width]
        for one in second_copies:
            one.wait_recv()
        for zi in range(nz):
            spot = slice(zi * rest, (zi + 1) * rest)
            mine = by_y[aligned((zi * 2 + c) * rest, rest), :]
            quarter[spot, :half] = (mine.astype(F32) + last_x[spot, :].astype(F32)).astype(BF)
        mine = by_x[aligned(t * nz * rest, nz * rest), :]
        quarter[:, half:] = (mine.astype(F32) + last_y[...].astype(F32)).astype(BF)
        for one in first_copies + second_copies:
            one.wait_send()


def back_layer(vecs, branch, grad_second, slope, norm_one, inv_one, up_all, down_all, partial, nz, nt):
    span, width = branch.shape
    hidden = slope.shape[1]
    block, tile = span // 4, 512
    rest, half = partial.shape[0] // (nt * nz * 2), partial.shape[1] // 2
    quarter = (nz * rest, 2 * half)
    hbm = pl.BlockSpec(memory_space=pl.ANY)
    rows = pl.BlockSpec((block, width), lambda i: (i, 0))
    wide = pl.BlockSpec((block, hidden), lambda i: (i, 0))
    whole = lambda shape: pl.BlockSpec(shape, lambda i: (0,) * len(shape))
    sds = jax.ShapeDtypeStruct
    return pl.pallas_call(
        functools.partial(back_kernel, nz=nz, nt=nt, tile=tile),
        out_shape=(
            sds((span, hidden), BF),
            sds((width, span), BF),
            sds((span, width), F32),
            sds((span, width), BF),
            sds((8, width), F32),
            sds(quarter, BF),
        ),
        grid=(span // block,),
        in_specs=[
            whole(vecs.shape),
            rows,
            rows,
            wide,
            rows,
            pl.BlockSpec((block, 128), lambda i: (i, 0)),
            hbm,
            hbm,
            hbm,
        ],
        out_specs=(
            wide, pl.BlockSpec((width, block), lambda i: (0, i)), rows, rows, whole((8, width)), whole(quarter),
        ),
        scratch_shapes=[
            pltpu.VMEM((width, hidden), BF),
            pltpu.VMEM((hidden, width), BF),
            pltpu.VMEM((width, width), BF),
            pltpu.VMEM((block, width), F32),
            pltpu.VMEM((3, 8, width), F32),
            pltpu.VMEM((8, hidden), F32),
            pltpu.VMEM((nz * 2 * rest, half), BF),
            pltpu.VMEM((nz * 2 * rest, half), BF),
            pltpu.VMEM((nt * nz * rest, half), BF),
            pltpu.VMEM((nt * nz * rest, half), BF),
            pltpu.VMEM((nz * rest, half), BF),
            pltpu.VMEM((nz * rest, half), BF),
            pltpu.SemaphoreType.DMA((3, up_all.shape[0])),
            pltpu.SemaphoreType.DMA((1 + nt * nz,)),
            pltpu.SemaphoreType.DMA((1 + nt * nz,)),
            pltpu.SemaphoreType.DMA((1 + nt * nz,)),
            pltpu.SemaphoreType.DMA((1 + nz,)),
            pltpu.SemaphoreType.DMA((1 + nz,)),
        ],
        compiler_params=pltpu.CompilerParams(
            collective_id=4, has_side_effects=True, vmem_limit_bytes=60 << 20
        ),
        cost_estimate=pl.CostEstimate(
            flops=2 * span * width * (width + 2 * hidden), bytes_accessed=60 << 20, transcendentals=0
        ),
        name="back_layer",
    )(vecs, branch, grad_second, slope, norm_one, inv_one, up_all, down_all, partial)


def grads_kernel(*refs, pairs, nz, nt, chunk):
    lefts, rights = refs[0 : 2 * pairs : 2], refs[1 : 2 * pairs : 2]
    refs = refs[2 * pairs :]
    quarter = None
    if len(refs) > 11:
        quarter, dctx_in, packed, shard, dctx = refs[:5]
        mine, others, dctx_own, mine_fill, dctx_sems, q_send, q_recv = refs[-7:]
        refs = (packed,) + refs[5:-7]
    packed, left, right, away, near, stage, l_fill, r_fill, send, recv, out_sems = refs
    z = lax.axis_index("z")
    k = lax.axis_index("core")
    core_dev = {"core": 1 - k}
    dblk = left.shape[2] // nz
    span = right.shape[1]
    plan = []
    base = 0
    for which in range(pairs):
        size = rights[which].shape[1] // nt
        for ti in range(nt):
            for at in range(0, size, min(chunk, size)):
                step = min(chunk, size)
                plan.append((which, ti * size + at, ti, base + at, step))
        base += size

    l_copies = [
        [
            pltpu.make_async_copy(
                lefts[which].at[aligned((zi * 2 + lax.rem(k + 1 + kk, 2)) * dblk, dblk)],
                left.at[which, kk, pl.ds(zi * dblk, dblk)],
                l_fill.at[which, kk, zi],
            )
            for kk in range(2)
            for zi in range(nz)
        ]
        for which in range(pairs)
    ]
    r_copies = [
        pltpu.make_async_copy(
            rights[which].at[:, pl.ds(col, step)], right.at[n, :, pl.ds(0, step)], r_fill.at[n]
        )
        for n, (which, col, _ti, _out, step) in enumerate(plan)
    ]
    for n, (which, _col, _ti, _out, _step) in enumerate(plan):
        if n == 0 or plan[n - 1][0] != which:
            for one in l_copies[which]:
                one.start()
        r_copies[n].start()
    friends = [core_dev]
    if quarter is not None:
        c = lax.axis_index("context")
        friends += [{"context": 1 - c}]
        friends += [{"z": lax.rem(z + d, nz)} for d in range(1, nz)]
    greet(friends)
    if quarter is not None:
        rest = mine.shape[0]

        def q_copy(d, owner, target):
            return remote(
                quarter.at[aligned(target * rest, rest)],
                others.at[owner],
                q_send.at[d - 1],
                q_recv.at[owner],
                {"z": lax.rem(z + d, nz)},
            )

        cols = dctx.shape[1]
        own_in = pltpu.make_async_copy(dctx_in.at[:, aligned(c * cols, cols)], dctx_own, dctx_sems.at[0])
        own_out = pltpu.make_async_copy(dctx_own, dctx.at[pl.ds(0, span)], dctx_sems.at[1])
        dctx_copy = remote(
            dctx_in.at[:, aligned((1 - c) * cols, cols)],
            dctx.at[pl.ds(span, span)],
            dctx_sems.at[2],
            dctx_sems.at[3],
            {"context": 1 - c},
        )
        own_in.start()
        dctx_copy.start()
        own = pltpu.make_async_copy(quarter.at[aligned(z * rest, rest)], mine, mine_fill)
        own.start()

    def exchange(n):
        step = plan[n][4]
        cut = pl.ds(0, step)
        return remote(away.at[n, :, cut], near.at[n, :, cut], send.at[n], recv.at[n], core_dev)

    sub = 256
    for n, (which, _col, _ti, _out, step) in enumerate(plan):
        if n == 0 or plan[n - 1][0] != which:
            for one in l_copies[which]:
                one.wait()
        r_copies[n].wait()

        @pl.loop(0, step // sub)
        def _(j, n=n, which=which):
            cut = aligned(j * sub, sub)
            away[n, :, cut] = mm(left[which, 0], right[n, :, cut]).astype(BF)

        exchange(n).start()

    if quarter is not None:
        own_in.wait()
        own_out.start()
        for d in range(1, nz):
            q_copy(d, z, lax.rem(z + d, nz)).start()
    outs = []
    for n, (which, _col, ti, out, step) in enumerate(plan):
        exchange(n).wait_recv()
        slot = n % 2
        if n >= 2:
            outs[n - 2].wait()

        @pl.loop(0, step // sub)
        def _(j, n=n, which=which, slot=slot):
            cut = aligned(j * sub, sub)
            stage[slot, :, cut] = (
                mm(left[which, 1], right[n, :, cut]) + near[n, :, cut].astype(F32)
            ).astype(BF)

        outs.append(
            pltpu.make_async_copy(
                stage.at[slot, :, pl.ds(0, step)],
                packed.at[pl.ds(ti * nz * dblk, nz * dblk), pl.ds(out, step)],
                out_sems.at[slot],
            )
        )
        outs[n].start()
    for one in outs[-2:]:
        one.wait()
    for n in range(len(plan)):
        exchange(n).wait_send()
    if quarter is not None:
        own.wait()
        total = mine[...].astype(F32)
        for d in range(1, nz):
            owner = lax.rem(z + nz - d, nz)
            q_copy(d, owner, z).wait_recv()
            total = total + others[owner].astype(F32)
        shard[...] = total.astype(BF)
        own_out.wait()
        dctx_copy.wait()
        for d in range(1, nz):
            q_copy(d, z, lax.rem(z + d, nz)).wait_send()


def grads_layer(operands, nz, nt, collective_id, quarter=None, grad_context=None):
    pairs = len(operands) // 2
    width, span = operands[0].shape
    chunk = 1024
    dblk = width // (2 * nz)
    sizes = [one.shape[1] // nt for one in operands[1::2]]
    count = sum(nt * max(1, size // chunk) for size in sizes)
    dma = pltpu.SemaphoreType.DMA
    hbm = pl.BlockSpec(memory_space=pl.ANY)
    out_shape = [jax.ShapeDtypeStruct((nt * nz * dblk, sum(sizes)), BF)]
    out_specs, extra = [hbm], []
    if quarter is not None:
        rest = (quarter.shape[0] // nz, quarter.shape[1])
        operands = operands + [quarter, grad_context]
        dctx = (2 * span, grad_context.shape[1] // 2)
        out_shape += [jax.ShapeDtypeStruct(rest, BF), jax.ShapeDtypeStruct(dctx, BF)]
        out_specs += [pl.BlockSpec(memory_space=pltpu.VMEM), hbm]
        extra = [
            pltpu.VMEM(rest, BF),
            pltpu.VMEM((nz,) + rest, BF),
            pltpu.VMEM((span, dctx[1]), BF),
            dma(()),
            dma((4,)),
            dma((nz,)),
            dma((nz,)),
        ]
    return pl.pallas_call(
        functools.partial(grads_kernel, pairs=pairs, nz=nz, nt=nt, chunk=chunk),
        out_shape=out_shape,
        in_specs=[hbm] * len(operands),
        out_specs=out_specs,
        scratch_shapes=[
            pltpu.VMEM((pairs, 2, nz * dblk, span), BF),
            pltpu.VMEM((count, span, chunk), BF),
            pltpu.VMEM((count, nz * dblk, chunk), BF),
            pltpu.VMEM((count, nz * dblk, chunk), BF),
            pltpu.VMEM((2, nz * dblk, chunk), BF),
            dma((pairs, 2, nz)),
            dma((count,)),
            dma((count,)),
            dma((count,)),
            dma((2,)),
        ]
        + extra,
        compiler_params=pltpu.CompilerParams(
            collective_id=collective_id, has_side_effects=True, vmem_limit_bytes=60 << 20
        ),
        cost_estimate=pl.CostEstimate(
            flops=2 * span * width * nt * sum(sizes), bytes_accessed=40 << 20, transcendentals=0
        ),
        name="grads_layer",
    )(*operands)


def on_device_rows(
    sizes,
    tokens,
    segment_ids,
    qkv_weight,
    qv_bias,
    proj_weight,
    proj_bias,
    first_gain,
    first_shift,
    up_weight,
    up_bias,
    down_weight,
    down_bias,
    second_gain,
    second_shift,
    out_grad,
):
    nf, nc, nt = sizes
    nz = nf // 2
    zbits = nz.bit_length() - 1
    z, k, c, t = (lax.axis_index(name) for name in AXES)
    f = z * 2 + k

    def send(value, target):
        pairs = []
        for fi in range(nf):
            for ci in range(nc):
                for ti in range(nt):
                    to = target(fi // 2, fi % 2, ci, ti)
                    if to is not None:
                        zo, ko, co, tto = to
                        pairs.append(((fi * nc + ci) * nt + ti, ((zo * 2 + ko) * nc + co) * nt + tto))
        return lax.ppermute(value, AXES, pairs)

    def over_x(v):
        return send(v, lambda zi, ki, ci, ti: (zi, ki, 1 - ci, ti))

    def over_y(v):
        return send(v, lambda zi, ki, ci, ti: (zi, ki, ci, 1 - ti))

    def over_core(v):
        return send(v, lambda zi, ki, ci, ti: (zi, 1 - ki, ci, ti))

    def over_z(v):
        return send(v, lambda zi, ki, ci, ti: ((zi + 1) % nz, ki, ci, ti))

    def over_zbit(v, bit):
        return send(v, lambda zi, ki, ci, ti: (zi ^ (1 << bit), ki, ci, ti))

    def z_all(v):
        return [v] + [
            send(v, lambda zi, ki, ci, ti, d=d: ((zi + d) % nz, ki, ci, ti)) for d in range(1, nz)
        ]

    def z_ring(v):
        out = [v]
        for _ in range(nz - 1):
            out.append(over_z(out[-1]))
        return out

    def ordered(index, own, other, axis=0):
        return jnp.where(index == 0, jnp.concatenate([own, other], axis), jnp.concatenate([other, own], axis))

    seq_count, span, width = tokens.shape
    heads = qv_bias.shape[1]
    head_size = qv_bias.shape[2] * nf
    cols = heads * head_size
    hidden = up_weight.shape[1] * nt
    dblk = width // nf

    pairs = heads // 2
    group = max(1, pairs // 2)
    wide = 2 * head_size

    pieces = [qv_bias, up_bias, proj_bias, first_gain, first_shift, down_bias, second_gain, second_shift]
    small = jnp.concatenate([p.reshape(-1, 128) for p in pieces])
    up_at, vec_at = qv_bias.size // 128, (qv_bias.size + up_bias.size) // 128
    small = jnp.pad(small, ((0, -(small.shape[0] + 2) % 16 + 2), (0, 0)))
    own_seg = jnp.where(t == 0, segment_ids[0], segment_ids[1])
    other_seg = over_x(own_seg)
    rows_t, qkv_full, qkv, small = open_layer(tokens, qkv_weight, small, nz, nt, heads, head_size, group)
    small = small.reshape(nf, nt, -1, 128)
    edge = head_size // nf

    def interleave(rows, columns):
        col = lax.broadcasted_iota(jnp.int32, (rows.shape[1], columns), 1)
        source = lax.broadcasted_iota(jnp.int32, (rows.shape[1], columns), 0)
        spread_out = mm(rows, (source == col // head_size * edge + col % edge).astype(BF))
        col = lax.broadcasted_iota(jnp.int32, (nf, columns), 1)
        mine = col % head_size // edge == lax.broadcasted_iota(jnp.int32, (nf, columns), 0)
        return jnp.sum(jnp.where(mine, spread_out, 0.0), axis=0)

    up_add = jnp.concatenate(
        [interleave(small[:, i, up_at:vec_at].reshape(nf, -1), hidden // nt) for i in range(nt)]
    ).reshape(1, hidden)
    vecs = small[:, 0, vec_at : vec_at + 8].transpose(1, 0, 2).reshape(8, width).astype(F32)

    every = AXES[:2] + AXES[3:]
    up_shard = jnp.concatenate([up_weight, proj_weight.T], axis=1)
    up_all = lax.all_gather(up_shard, every).reshape((-1,) + up_shard.shape)
    down_all = lax.all_gather(after(down_weight, up_shard), every).reshape((-1,) + down_weight.shape)

    seg_store = jnp.concatenate([own_seg, other_seg])
    seg_global = ordered(c, own_seg, other_seg)
    total = 2 * span
    q_block, k_block = 512, 256
    bounds = segment_bounds(seg_global, q_block, FINE)
    back_bounds = segment_bounds(seg_global, k_block, FINE)
    shift = jnp.reshape(c * (total // FINE // 2), (1,)).astype(jnp.int32)
    seg_k = jnp.broadcast_to(seg_store[:, None], (total, 128))
    seg_q = jnp.broadcast_to(seg_store[None, :], (8, total))
    attn_args = (seg_k, seg_q) + bounds + (shift,)
    back_args = (seg_k, seg_q) + back_bounds + (shift,)
    mixed, lse, mixed_other = [], [], []
    for p in range(pairs):
        if p >= 2:
            attn_args = attn_args[:2] + (after(attn_args[2], mixed_other[p - 2]),) + attn_args[3:]
        out, one = attn_fwd(qkv, *attn_args, p, pairs, group, head_size, q_block, 6)
        mixed.append(out)
        lse.append(one)
        mixed_other.append(over_x(out[span:]))
    up_all, _last = lax.optimization_barrier((up_all, mixed[-1]))
    context_rows = ordered(
        c, jnp.concatenate([m[:span] for m in mixed], 1), jnp.concatenate(mixed_other, 1), 1
    )

    which = t.reshape(1)
    first, norm_one, inv_one, first_t, act_low, slope = up_layer(
        which, context_rows, tokens, vecs, up_add, up_all, nt
    )
    down_all, first = lax.optimization_barrier((down_all, first))
    out_low, branch, branch_t, grad_second, vec_two = down_layer(
        which, out_grad, vecs, first, act_low, down_all, nt
    )
    (down_sum,) = grads_layer([branch_t, act_low], nz, nt, 2)
    hidden_low, attn_t, grad_in, grad_context, vec_one, quarter = back_layer(
        vecs, branch, grad_second, slope, norm_one, inv_one, up_all, down_all, down_sum, nz, nt
    )
    out_low = after(out_low, quarter)
    out_other = over_y(out_low)
    other_sum, down_part, dctx = grads_layer([first_t, hidden_low, attn_t, context_rows], nz, nt, 3, quarter, grad_context)
    grad_down = ordered(c, down_part, over_x(down_part), 0).astype(F32).T
    part = lax.psum_scatter(other_sum, ("tensor", "z", "context"), scatter_dimension=0, tiled=True)
    part = ordered(c, part, over_x(part), 0).astype(F32)
    grad_up = part[:, : hidden // nt]
    grad_proj = part[:, hidden // nt :].T

    mixed = lax.optimization_barrier(tuple(mixed) + (quarter,))[:pairs]
    dqkv = attn_bwd(
        qkv, jnp.concatenate(mixed, axis=1), dctx, jnp.concatenate(lse), *back_args, pairs, group, head_size, k_block, 3
    )
    layer_output = ordered(t, out_low[None], out_other[None])
    dqkv, grad_down = lax.optimization_barrier((dqkv, grad_down))
    tokens_grad, grad_qkv, qv_sum, vec_sums = close_layer(
        dqkv, qkv_full, rows_t, grad_in, vec_one, vec_two, nz, group * wide
    )
    own_vecs = lax.dynamic_slice_in_dim(vec_sums, f * dblk, dblk, 1)
    vector_out = [own_vecs[row] for row in (0, 1, 2, 8, 9, 10)]
    up_rows, up_cols = up_bias.shape
    bias_up = vec_sums[3 : 3 + hidden // width].reshape(nt * up_rows, nf * up_cols)
    bias_up = lax.dynamic_slice(bias_up, (t * up_rows, f * up_cols), (up_rows, up_cols))
    per = wide // 128 * group
    kinds = [
        jnp.concatenate([qv_sum[(3 * g + which) * per :][:per] for g in range(pairs // group)])
        for which in (0, 2)
    ]
    grad_qv = jnp.stack(kinds).reshape(2, heads, head_size)
    grad_qv = lax.dynamic_slice_in_dim(grad_qv, f * (head_size // nf), head_size // nf, 2)

    return (
        layer_output,
        tokens_grad,
        grad_qkv,
        grad_qv,
        grad_proj,
        vector_out[0],
        vector_out[1],
        vector_out[2],
        grad_up,
        bias_up,
        grad_down,
        vector_out[3],
        vector_out[4],
        vector_out[5],
    )


def solution(mesh):
    sizes = tuple(mesh.shape[name] for name in ("fsdp", "context", "tensor"))
    nf, nc, nt = sizes
    shards = (
        P("fsdp", "context", None),
        P("fsdp", "context"),
        P(None, "fsdp", "tensor"),
        P(None, "tensor", "fsdp"),
        P("tensor", "fsdp"),
        P("fsdp"),
        P("fsdp"),
        P("fsdp"),
        P("fsdp", "tensor"),
        P("tensor", "fsdp"),
        P("tensor", "fsdp"),
        P("fsdp"),
        P("fsdp"),
        P("fsdp"),
    )
    in_specs = (shards[0],) + shards[1:] + (shards[0],)
    out_specs = (shards[0], shards[0]) + shards[2:]
    nz = nf // 2
    by_rows = nc == nt == 2 and nf % 2 == 0 and nz & (nz - 1) == 0
    rows_mesh = jax.sharding.Mesh(mesh.devices.reshape(nz, 2, nc, nt), AXES) if by_rows else None

    def finer(spec):
        return P(*(("z", "core") if name == "fsdp" else name for name in spec))

    def program(*args):
        if by_rows and args[0].shape[0] // nf == nt:
            return jax.shard_map(
                functools.partial(on_device_rows, sizes),
                mesh=rows_mesh,
                in_specs=tuple(finer(spec) for spec in in_specs),
                out_specs=tuple(finer(spec) for spec in out_specs),
                check_vma=False,
            )(*args)
        return jax.shard_map(
            on_device_general, mesh=mesh, in_specs=in_specs, out_specs=out_specs, check_vma=False
        )(*args)

    return program
```

```python
import functools

import jax
import jax.numpy as jnp
from jax import lax
from jax.experimental import pallas as pl
from jax.experimental.pallas import tpu as pltpu
from jax.sharding import PartitionSpec as P

NORM_EPS = 1e-05


def layer_norm(hidden_rows, norm_gain, norm_shift):
    row_mean = jnp.mean(hidden_rows, axis=-1, keepdims=True)
    centred = hidden_rows - row_mean
    variance = jnp.mean(centred * centred, axis=-1, keepdims=True)
    return centred * lax.rsqrt(variance + NORM_EPS) * norm_gain + norm_shift


def exact_gelu(values):
    return jax.nn.gelu(values, approximate=False)


def masked_logits(query_heads, key_heads, seg_query, seg_key, score_scale):
    logits = (
        jnp.einsum("qhe,khe->hqk", query_heads, key_heads, preferred_element_type=jnp.float32)
        * score_scale
    )
    same_doc = (seg_query[:, None] == seg_key[None, :])[None, :, :]
    return jnp.where(same_doc, logits, -1e30)


def on_device_general(
    tokens,
    segment_ids,
    qkv_weight,
    qv_bias,
    proj_weight,
    proj_bias,
    first_gain,
    first_shift,
    up_weight,
    up_bias,
    down_weight,
    down_bias,
    second_gain,
    second_shift,
    out_grad,
):
    seq_count, span, width = tokens.shape
    total_rows = seq_count * span
    share = total_rows // lax.axis_size("tensor")
    row_start = lax.axis_index("tensor") * share
    token_rows = tokens.reshape(total_rows, width)
    gathered = (
        lax.all_gather(qkv_weight, "fsdp", axis=1, tiled=True),
        lax.all_gather(qv_bias, "fsdp", axis=2, tiled=True),
        lax.all_gather(proj_weight, "fsdp", axis=1, tiled=True),
        lax.all_gather(proj_bias, "fsdp", axis=0, tiled=True),
        lax.all_gather(first_gain, "fsdp", axis=0, tiled=True),
        lax.all_gather(first_shift, "fsdp", axis=0, tiled=True),
        lax.all_gather(up_weight, "fsdp", axis=0, tiled=True),
        lax.all_gather(up_bias, "fsdp", axis=1, tiled=True),
        lax.all_gather(down_weight, "fsdp", axis=1, tiled=True),
        lax.all_gather(down_bias, "fsdp", axis=0, tiled=True),
        lax.all_gather(second_gain, "fsdp", axis=0, tiled=True),
        lax.all_gather(second_shift, "fsdp", axis=0, tiled=True),
    )
    qkv_full, qv_full, proj_full, proj_add, gain_one, shift_one = (
        gathered[0],
        gathered[1],
        gathered[2],
        gathered[3],
        gathered[4],
        gathered[5],
    )
    up_full, up_add, down_full, down_add, gain_two, shift_two = (
        gathered[6],
        gathered[7],
        gathered[8],
        gathered[9],
        gathered[10],
        gathered[11],
    )
    local_width = qkv_full.shape[2]
    head_count = qv_full.shape[1]
    head_size = qv_full.shape[2]
    score_scale = float(head_size) ** (-0.5)
    projected = jnp.einsum("rd,cde->cre", token_rows, qkv_full, preferred_element_type=jnp.float32)
    bias_rows = qv_full.reshape(2, local_width).astype(jnp.float32)
    head_shape = (seq_count, span, head_count, head_size)
    query_heads = (projected[0] + bias_rows[0]).astype(jnp.bfloat16).reshape(head_shape)
    key_heads = projected[1].astype(jnp.bfloat16).reshape(head_shape)
    value_heads = (projected[2] + bias_rows[1]).astype(jnp.bfloat16).reshape(head_shape)
    key_all, value_all, seg_all = (
        lax.all_gather(key_heads, "context", axis=1, tiled=True),
        lax.all_gather(value_heads, "context", axis=1, tiled=True),
        lax.all_gather(segment_ids, "context", axis=1, tiled=True),
    )

    def attend_forward(pieces):
        query_one, key_one, value_one, seg_query, seg_key = pieces
        logits = masked_logits(query_one, key_one, seg_query, seg_key, score_scale)
        row_top = jnp.max(logits, axis=-1, keepdims=True)
        weights = jnp.exp(logits - row_top)
        row_total = jnp.sum(weights, axis=-1, keepdims=True)
        soft_low = (weights / row_total).astype(jnp.bfloat16)
        mixed_one = jnp.einsum(
            "hqk,khe->qhe", soft_low, value_one, preferred_element_type=jnp.float32
        )
        return (mixed_one.astype(jnp.bfloat16), row_top + jnp.log(row_total))

    mixed, log_totals = lax.map(
        attend_forward, (query_heads, key_all, value_all, segment_ids, seg_all)
    )
    context_low = mixed.reshape(total_rows, local_width)
    attn_part = jnp.dot(context_low, proj_full, preferred_element_type=jnp.float32)
    attn_share = lax.psum_scatter(
        attn_part, "tensor", scatter_dimension=0, tiled=True
    ) + proj_add.astype(jnp.float32)
    token_share = lax.dynamic_slice_in_dim(token_rows, row_start, share, 0).astype(jnp.float32)
    first_share, first_pull = jax.vjp(
        layer_norm,
        token_share + attn_share,
        gain_one.astype(jnp.float32),
        shift_one.astype(jnp.float32),
    )
    first_low = lax.all_gather(first_share.astype(jnp.bfloat16), "tensor", axis=0, tiled=True)
    hidden_pre = jnp.dot(first_low, up_full, preferred_element_type=jnp.float32) + up_add.reshape(
        -1
    ).astype(jnp.float32)
    activation, gelu_pull = jax.vjp(exact_gelu, hidden_pre)
    act_low = activation.astype(jnp.bfloat16)
    down_part = jnp.dot(act_low, down_full, preferred_element_type=jnp.float32)
    branch_share = lax.psum_scatter(
        down_part, "tensor", scatter_dimension=0, tiled=True
    ) + down_add.astype(jnp.float32)
    output_share, second_pull = jax.vjp(
        layer_norm,
        first_share + branch_share,
        gain_two.astype(jnp.float32),
        shift_two.astype(jnp.float32),
    )
    qkv_back, proj_back, up_back, down_back = (
        lax.all_gather(qkv_weight, "fsdp", axis=1, tiled=True),
        lax.all_gather(proj_weight, "fsdp", axis=1, tiled=True),
        lax.all_gather(up_weight, "fsdp", axis=0, tiled=True),
        lax.all_gather(down_weight, "fsdp", axis=1, tiled=True),
    )
    cot_share = lax.dynamic_slice_in_dim(
        out_grad.reshape(total_rows, width), row_start, share, 0
    ).astype(jnp.float32)
    grad_second, gain_two_part, shift_two_part = second_pull(cot_share)
    branch_low = lax.all_gather(grad_second.astype(jnp.bfloat16), "tensor", axis=0, tiled=True)
    grad_down_bias = jnp.sum(branch_low.astype(jnp.float32), axis=0)
    grad_down = jnp.einsum("rf,rd->fd", act_low, branch_low, preferred_element_type=jnp.float32)
    grad_act = jnp.einsum("rd,fd->rf", branch_low, down_back, preferred_element_type=jnp.float32)
    hidden_low = gelu_pull(grad_act)[0].astype(jnp.bfloat16)
    grad_up_bias = jnp.sum(hidden_low.astype(jnp.float32), axis=0).reshape(up_add.shape)
    grad_up = jnp.einsum("rd,rf->df", first_low, hidden_low, preferred_element_type=jnp.float32)
    norm_part = jnp.einsum("rf,df->rd", hidden_low, up_back, preferred_element_type=jnp.float32)
    grad_first = grad_second + lax.psum_scatter(
        norm_part, "tensor", scatter_dimension=0, tiled=True
    )
    grad_in_one, gain_one_part, shift_one_part = first_pull(grad_first)
    attn_low = lax.all_gather(grad_in_one.astype(jnp.bfloat16), "tensor", axis=0, tiled=True)
    grad_proj_bias = jnp.sum(attn_low.astype(jnp.float32), axis=0)
    grad_proj = jnp.einsum("rl,rd->ld", context_low, attn_low, preferred_element_type=jnp.float32)
    grad_context = (
        jnp.einsum("rd,ld->rl", attn_low, proj_back, preferred_element_type=jnp.float32)
        .astype(jnp.bfloat16)
        .reshape(head_shape)
    )

    def attend_backward(pieces):
        query_one, key_one, value_one, seg_query, seg_key, log_total, context_grad = pieces
        logits = masked_logits(query_one, key_one, seg_query, seg_key, score_scale)
        soft_again = jnp.exp(logits - log_total)
        grad_soft = jnp.einsum(
            "qhe,khe->hqk", context_grad, value_one, preferred_element_type=jnp.float32
        )
        row_delta = jnp.sum(grad_soft * soft_again, axis=-1, keepdims=True)
        grad_logits = (soft_again * (grad_soft - row_delta)).astype(jnp.bfloat16)
        query_grad = (
            jnp.einsum("hqk,khe->qhe", grad_logits, key_one, preferred_element_type=jnp.float32)
            * score_scale
        ).astype(jnp.bfloat16)
        key_part = (
            jnp.einsum("hqk,qhe->khe", grad_logits, query_one, preferred_element_type=jnp.float32)
            * score_scale
        )
        value_part = jnp.einsum(
            "hqk,qhe->khe",
            soft_again.astype(jnp.bfloat16),
            context_grad,
            preferred_element_type=jnp.float32,
        )
        return (query_grad, key_part, value_part)

    grad_query, key_terms, value_terms = lax.map(
        attend_backward,
        (query_heads, key_all, value_all, segment_ids, seg_all, log_totals, grad_context),
    )
    key_grad, value_grad = (
        lax.psum_scatter(
            key_terms.astype(jnp.bfloat16), "context", scatter_dimension=1, tiled=True
        ).astype(jnp.float32),
        lax.psum_scatter(
            value_terms.astype(jnp.bfloat16), "context", scatter_dimension=1, tiled=True
        ).astype(jnp.float32),
    )
    grad_stack = jnp.stack(
        [
            grad_query.reshape(total_rows, local_width),
            key_grad.astype(jnp.bfloat16).reshape(total_rows, local_width),
            value_grad.astype(jnp.bfloat16).reshape(total_rows, local_width),
        ]
    )
    stack_sums = jnp.sum(grad_stack.astype(jnp.float32), axis=1)
    grad_qv_bias = jnp.stack([stack_sums[0], stack_sums[2]]).reshape(qv_full.shape)
    grad_qkv = jnp.einsum("rd,cre->cde", token_rows, grad_stack, preferred_element_type=jnp.float32)
    input_part = jnp.einsum("cre,cde->rd", grad_stack, qkv_back, preferred_element_type=jnp.float32)
    norm_parts = jnp.tile(
        jnp.stack([gain_one_part, shift_one_part, gain_two_part, shift_two_part]),
        (lax.axis_size("tensor"), 1),
    )
    input_share, norm_sums = (
        lax.psum_scatter(
            input_part.astype(jnp.bfloat16), "tensor", scatter_dimension=0, tiled=True
        ).astype(jnp.float32),
        lax.psum_scatter(
            norm_parts.astype(jnp.bfloat16), "tensor", scatter_dimension=0, tiled=True
        ).astype(jnp.float32),
    )
    grad_share_low = (grad_in_one + input_share).astype(jnp.bfloat16)
    out_rows, grad_rows = (
        lax.all_gather(output_share.astype(jnp.bfloat16), "tensor", axis=0, tiled=True),
        lax.all_gather(grad_share_low, "tensor", axis=0, tiled=True),
    )
    local_grads = (
        grad_qkv,
        grad_qv_bias,
        grad_proj,
        grad_proj_bias,
        norm_sums[0],
        norm_sums[1],
        grad_up,
        grad_up_bias,
        grad_down,
        grad_down_bias,
        norm_sums[2],
        norm_sums[3],
    )
    summed = (
        lax.psum(local_grads[0].astype(jnp.bfloat16), "context").astype(jnp.float32),
        lax.psum(local_grads[1].astype(jnp.bfloat16), "context").astype(jnp.float32),
        lax.psum(local_grads[2].astype(jnp.bfloat16), "context").astype(jnp.float32),
        lax.psum(local_grads[3].astype(jnp.bfloat16), "context").astype(jnp.float32),
        lax.psum(local_grads[4].astype(jnp.bfloat16), "context").astype(jnp.float32),
        lax.psum(local_grads[5].astype(jnp.bfloat16), "context").astype(jnp.float32),
        lax.psum(local_grads[6].astype(jnp.bfloat16), "context").astype(jnp.float32),
        lax.psum(local_grads[7].astype(jnp.bfloat16), "context").astype(jnp.float32),
        lax.psum(local_grads[8].astype(jnp.bfloat16), "context").astype(jnp.float32),
        lax.psum(local_grads[9].astype(jnp.bfloat16), "context").astype(jnp.float32),
        lax.psum(local_grads[10].astype(jnp.bfloat16), "context").astype(jnp.float32),
        lax.psum(local_grads[11].astype(jnp.bfloat16), "context").astype(jnp.float32),
    )
    owned = (
        lax.psum_scatter(
            summed[0].astype(jnp.bfloat16), "fsdp", scatter_dimension=1, tiled=True
        ).astype(jnp.float32),
        lax.psum_scatter(
            summed[1].astype(jnp.bfloat16), "fsdp", scatter_dimension=2, tiled=True
        ).astype(jnp.float32),
        lax.psum_scatter(
            summed[2].astype(jnp.bfloat16), "fsdp", scatter_dimension=1, tiled=True
        ).astype(jnp.float32),
        lax.psum_scatter(
            summed[3].astype(jnp.bfloat16), "fsdp", scatter_dimension=0, tiled=True
        ).astype(jnp.float32),
        lax.psum_scatter(
            summed[4].astype(jnp.bfloat16), "fsdp", scatter_dimension=0, tiled=True
        ).astype(jnp.float32),
        lax.psum_scatter(
            summed[5].astype(jnp.bfloat16), "fsdp", scatter_dimension=0, tiled=True
        ).astype(jnp.float32),
        lax.psum_scatter(
            summed[6].astype(jnp.bfloat16), "fsdp", scatter_dimension=0, tiled=True
        ).astype(jnp.float32),
        lax.psum_scatter(
            summed[7].astype(jnp.bfloat16), "fsdp", scatter_dimension=1, tiled=True
        ).astype(jnp.float32),
        lax.psum_scatter(
            summed[8].astype(jnp.bfloat16), "fsdp", scatter_dimension=1, tiled=True
        ).astype(jnp.float32),
        lax.psum_scatter(
            summed[9].astype(jnp.bfloat16), "fsdp", scatter_dimension=0, tiled=True
        ).astype(jnp.float32),
        lax.psum_scatter(
            summed[10].astype(jnp.bfloat16), "fsdp", scatter_dimension=0, tiled=True
        ).astype(jnp.float32),
        lax.psum_scatter(
            summed[11].astype(jnp.bfloat16), "fsdp", scatter_dimension=0, tiled=True
        ).astype(jnp.float32),
    )
    layer_output = out_rows.reshape(seq_count, span, width)
    tokens_grad = grad_rows.reshape(seq_count, span, width)
    return (
        layer_output,
        tokens_grad,
        owned[0],
        owned[1],
        owned[2],
        owned[3],
        owned[4],
        owned[5],
        owned[6],
        owned[7],
        owned[8],
        owned[9],
        owned[10],
        owned[11],
    )


AXES = ("z", "core", "context", "tensor")
BF = jnp.bfloat16
F32 = jnp.float32
FINE = 128
MASKED = -1e30
NT = (((1,), (1,)), ((), ()))

def attn_fwd_kernel(
    lo_ref, hi_ref, shift_ref, q_ref, k_ref, v_ref, segk_ref, segq_ref, o_ref, lse_ref, vt_ref,
    *, fine, many, hd, scale,
):
    block = pl.program_id(0)
    shift = shift_ref[0]
    bq, pair = q_ref.shape
    pieces = k_ref.shape[0] // fine
    heads = pair // hd

    @pl.when(block == 0)
    def _():
        for j in range(pieces):
            vt_ref[j] = v_ref[j * fine : (j + 1) * fine, :].T

    at = lax.rem(block + shift // (bq // fine), pieces * fine // bq)
    low, high = lo_ref[at], hi_ref[at]
    lane = lax.broadcasted_iota(jnp.int32, (bq, pair), 1) // hd
    q = q_ref[...] * jnp.asarray(scale, BF)
    qs = [jnp.where(lane == h, q, jnp.zeros_like(q)) for h in range(heads)]
    seg_q = segq_ref[0:1, :]

    def body(i, carry):
        j = low + i * many
        spots = [lax.rem(j + u + shift, pieces) for u in range(many)]
        keys = jnp.concatenate([k_ref[aligned(spot * fine, fine), :] for spot in spots])
        values_t = jnp.concatenate([vt_ref[spot] for spot in spots], axis=1)
        seg_k = jnp.concatenate(
            [
                jnp.where(j + u < high, segk_ref[aligned(spot * fine, fine), :], -1)
                for u, spot in enumerate(spots)
            ]
        )
        same = jnp.concatenate([seg_k] * (bq // seg_k.shape[1]), axis=1) == seg_q
        scores = [jnp.where(same, mm_nt(keys, qs[h]), MASKED) for h in range(heads)]
        out = []
        for h in range(heads):
            top, total, acc = carry[h]
            new_top = jnp.maximum(top, jnp.max(scores[h], axis=0, keepdims=True))
            weights = jnp.exp(scores[h] - new_top)
            fade = jnp.exp(top - new_top)
            total = total * fade + jnp.sum(weights, axis=0, keepdims=True)
            acc = acc * fade + mm(values_t[h * hd : (h + 1) * hd, :], weights.astype(BF))
            out.append((new_top, total, acc))
        return tuple(out)

    init = (jnp.full((1, bq), MASKED, F32), jnp.zeros((1, bq), F32), jnp.zeros((hd, bq), F32))
    done = lax.fori_loop(0, (high - low + many - 1) // many, body, (init,) * heads)
    o_ref[...] = jnp.concatenate([acc / total for _, total, acc in done], axis=0).T.astype(BF)
    lse_ref[0] = jnp.concatenate([top + jnp.log(total) for top, total, _ in done], axis=0)


def attn_bwd_kernel(
    lo_ref, hi_ref, shift_ref, q_ref, k_ref, v_ref, o_ref, do_ref, lse_ref, segk_ref, segq_ref, out_ref,
    qs_ref, dos_ref, kt_ref, delta_ref, dqt_ref, dk_ref, dv_ref,
    *, bk, fine, many, hd, scale,
):
    w = pl.program_id(1)
    shift = shift_ref[0]
    rows, pair = q_ref.shape
    pieces = rows // fine
    blocks = rows // bk
    heads = pair // hd

    @pl.when(w == 0)
    def _():
        lane = lax.broadcasted_iota(jnp.int32, (bk, pair), 1) // hd
        head = lax.broadcasted_iota(jnp.int32, (8, pair), 0)
        pick = (head == lax.broadcasted_iota(jnp.int32, (8, pair), 1) // hd).astype(F32)
        factor = jnp.asarray(scale, BF)
        for j in range(blocks):
            r = slice(j * bk, (j + 1) * bk)
            q = q_ref[r, :] * factor
            do = do_ref[r, :]
            for h in range(heads):
                qs_ref[h, r, :] = jnp.where(lane == h, q, jnp.zeros_like(q))
                dos_ref[h, r, :] = jnp.where(lane == h, do, jnp.zeros_like(do))
            kt_ref[j] = (k_ref[r, :] * factor).T
            prod = do.astype(F32) * o_ref[r, :].astype(F32)
            delta_ref[:, r] = lax.dot_general(
                pick, prod, NT, preferred_element_type=F32, precision=lax.Precision.HIGHEST
            )
        dqt_ref[...] = jnp.zeros(dqt_ref.shape, F32)

        def outer(block, _):
            at = lax.rem(block + shift // (bk // fine), blocks)
            low, high = lo_ref[at], hi_ref[at]
            r = aligned(block * bk, bk)
            keys, values = k_ref[r, :], v_ref[r, :]
            seg_k = jnp.concatenate([segk_ref[r, :]] * (many * fine // segk_ref.shape[1]), axis=1)

            def inner(i, carry):
                dk, dv = carry
                j = low + i * many
                spots = [lax.rem(j + u + shift, pieces) for u in range(many)]
                cuts = [aligned(spot * fine, fine) for spot in spots]
                seg_q = jnp.concatenate(
                    [jnp.where(j + u < high, segq_ref[0:1, cut], -1) for u, cut in enumerate(cuts)], axis=1
                )
                same = seg_k == seg_q
                q = [jnp.concatenate([qs_ref[h, cut, :] for cut in cuts]) for h in range(heads)]
                do = [jnp.concatenate([dos_ref[h, cut, :] for cut in cuts]) for h in range(heads)]
                lse = jnp.concatenate([lse_ref[0, :, cut] for cut in cuts], axis=1)
                delta = jnp.concatenate([delta_ref[:, cut] for cut in cuts], axis=1)
                scores = [mm_nt(keys, q[h]) for h in range(heads)]
                dp = [mm_nt(values, do[h]) for h in range(heads)]
                p = [jnp.exp(jnp.where(same, scores[h] - lse[h : h + 1, :], MASKED)) for h in range(heads)]
                p_low = [p[h].astype(BF) for h in range(heads)]
                ds = [(p[h] * (dp[h] - delta[h : h + 1, :])).astype(BF) for h in range(heads)]
                for h in range(heads):
                    hs = slice(h * hd, (h + 1) * hd)
                    dv = dv + mm(p_low[h], do[h])
                    dk = dk + mm(ds[h], q[h])
                    dq = mm(kt_ref[block, hs, :], ds[h])
                    for u in range(many):
                        dqt_ref[spots[u], hs, :] += dq[:, u * fine : (u + 1) * fine]
                return dk, dv

            zero = jnp.zeros((bk, pair), F32)
            dk, dv = lax.fori_loop(0, (high - low + many - 1) // many, inner, (zero, zero))
            dk_ref[r, :] = dk.astype(BF)
            dv_ref[r, :] = dv.astype(BF)
            return 0

        lax.fori_loop(0, blocks, outer, 0)
        for j in range(pieces):
            out_ref[j * fine : (j + 1) * fine, :] = dqt_ref[j].T.astype(BF)

    @pl.when(w == 1)
    def _():
        out_ref[...] = dk_ref[...]

    @pl.when(w == 2)
    def _():
        out_ref[...] = dv_ref[...]


def pair_block(which, pair, group):
    return (pair // group) * 3 * group + which * group + pair % group


def attn_fwd(qkv, seg_k, seg_q, low, high, shift, pair, pairs, group, head_size, bq, many):
    rows, wide = qkv.shape[0], 2 * head_size
    spec = lambda which: pair_block(which, pair, group)
    return pl.pallas_call(
        functools.partial(
            attn_fwd_kernel, fine=FINE, many=many, hd=head_size, scale=float(head_size) ** -0.5
        ),
        out_shape=(
            jax.ShapeDtypeStruct((rows, wide), BF),
            jax.ShapeDtypeStruct((1, 2, rows), F32),
        ),
        grid_spec=pltpu.PrefetchScalarGridSpec(
            num_scalar_prefetch=3,
            grid=(rows // bq,),
            in_specs=[
                pl.BlockSpec((bq, wide), lambda i, *_: (i, spec(0))),
                pl.BlockSpec((rows, wide), lambda i, *_: (0, spec(1))),
                pl.BlockSpec((rows, wide), lambda i, *_: (0, spec(2))),
                pl.BlockSpec((rows, 128), lambda i, *_: (0, 0)),
                pl.BlockSpec((8, bq), lambda i, *_: (0, i)),
            ],
            out_specs=(
                pl.BlockSpec((bq, wide), lambda i, *_: (i, 0)),
                pl.BlockSpec((1, 2, bq), lambda i, *_: (0, 0, i)),
            ),
            scratch_shapes=[pltpu.VMEM((rows // FINE, wide, FINE), BF)],
        ),
        compiler_params=pltpu.CompilerParams(vmem_limit_bytes=24 << 20),
        cost_estimate=pl.CostEstimate(
            flops=15_000_000_000, bytes_accessed=rows * wide * 8, transcendentals=rows * rows // 2
        ),
        name="attn_fwd",
    )(low, high, shift, qkv, qkv, qkv, seg_k, seg_q)


def attn_bwd(qkv, mixed, dctx, lse, seg_k, seg_q, low, high, shift, pairs, group, head_size, bk, many):
    rows, wide = qkv.shape[0], 2 * head_size
    blocks = rows // bk
    column = lambda which: pl.BlockSpec((rows, wide), lambda p, w, *_: (0, pair_block(which, p, group)))
    own = pl.BlockSpec((rows, wide), lambda p, w, *_: (0, p))
    return pl.pallas_call(
        functools.partial(
            attn_bwd_kernel, bk=bk, fine=FINE, many=many, hd=head_size, scale=float(head_size) ** -0.5
        ),
        out_shape=jax.ShapeDtypeStruct(qkv.shape, BF),
        grid_spec=pltpu.PrefetchScalarGridSpec(
            num_scalar_prefetch=3,
            grid=(pairs, 3),
            in_specs=[
                column(0),
                column(1),
                column(2),
                own,
                own,
                pl.BlockSpec((1, 2, rows), lambda p, w, *_: (p, 0, 0)),
                pl.BlockSpec((rows, 128), lambda p, w, *_: (0, 0)),
                pl.BlockSpec((8, rows), lambda p, w, *_: (0, 0)),
            ],
            out_specs=pl.BlockSpec((rows, wide), lambda p, w, *_: (0, pair_block(w, p, group))),
            scratch_shapes=[
                pltpu.VMEM((2, rows, wide), BF),
                pltpu.VMEM((2, rows, wide), BF),
                pltpu.VMEM((blocks, wide, bk), BF),
                pltpu.VMEM((8, rows), F32),
                pltpu.VMEM((rows // FINE, wide, FINE), F32),
                pltpu.VMEM((rows, wide), BF),
                pltpu.VMEM((rows, wide), BF),
            ],
        ),
        compiler_params=pltpu.CompilerParams(vmem_limit_bytes=58 << 20),
        cost_estimate=pl.CostEstimate(
            flops=100_000_000_000, bytes_accessed=rows * wide * 64, transcendentals=2 * rows * rows
        ),
        name="attn_bwd",
    )(low, high, shift, qkv, qkv, qkv, mixed, dctx, lse, seg_k, seg_q)


def segment_bounds(seg_rows, row_block, col_block):
    blocks = seg_rows.reshape(-1, row_block)
    low = jnp.sum(seg_rows[None, :] < blocks[:, :1], axis=1) // col_block
    high = (jnp.sum(seg_rows[None, :] <= blocks[:, -1:], axis=1) + col_block - 1) // col_block
    return low.astype(jnp.int32), high.astype(jnp.int32)


def norm_forward(rows):
    mean = jnp.mean(rows, axis=-1, keepdims=True)
    centred = rows - mean
    inv = lax.rsqrt(jnp.mean(centred * centred, axis=-1, keepdims=True) + NORM_EPS)
    return centred * inv, inv


def norm_backward(grad, normed, inv):
    return inv * (
        grad
        - jnp.mean(grad, axis=-1, keepdims=True)
        - normed * jnp.mean(grad * normed, axis=-1, keepdims=True)
    )


def after(value, *others):
    return lax.optimization_barrier((value,) + others)[0]


def mm(a, b):
    return jnp.dot(a, b, preferred_element_type=F32)


def mm_nt(a, b):
    return lax.dot_general(a, b, (((1,), (1,)), ((), ())), preferred_element_type=F32)


def mm_tn(a, b):
    return lax.dot_general(a, b, (((0,), (0,)), ((), ())), preferred_element_type=F32)


def remote(src, dst, send_sem, recv_sem, device):
    return pltpu.make_async_remote_copy(
        src_ref=src,
        dst_ref=dst,
        send_sem=send_sem,
        recv_sem=recv_sem,
        device_id=device,
        device_id_type=pl.DeviceIdType.MESH,
    )


def greet(devices):
    barrier = pltpu.get_barrier_semaphore()
    for device in devices:
        pl.semaphore_signal(barrier, inc=1, device_id=device, device_id_type=pl.DeviceIdType.MESH)
    pl.semaphore_wait(barrier, len(devices))


def aligned(start, size):
    return pl.ds(pl.multiple_of(start, size), size)


def open_kernel(
    tokens, weight, small, xt_out, w_out, qkv_out, small_out,
    x, xt, w, qkv, smalls, fill_x, fill_w, x_send, x_recv, s_send, s_recv, y_sems, z_send, z_recv,
    c_send, c_recv, out_sems,
    *, nz, nt, heads, head_size, group, chunk,
):
    z, k, c, t = (lax.axis_index(name) for name in AXES)
    f = z * 2 + k
    nf = nz * 2
    span, width = tokens.shape[1:]
    dblk = weight.shape[1]
    cols = heads * head_size
    gw = group * 2 * head_size
    chunks = span // chunk
    peers = [
        (dz, dk, dt) for dz in range(nz) for dk in range(2) for dt in range(nt) if (dz, dk, dt) != (0, 0, 0)
    ]

    def peer(offset):
        dz, dk, dt = offset
        return {"z": lax.rem(z + dz, nz), "core": lax.rem(k + dk, 2), "tensor": lax.rem(t + dt, nt)}

    def block(index):
        return w.at[aligned(index * dblk, dblk), :]

    for i in range(chunks):
        r = pl.ds(i * chunk, chunk)
        pltpu.make_async_copy(tokens.at[t, r], x.at[r], fill_x.at[i]).start()
    fills = []
    for g in range(cols // gw):
        for which in range(3):
            at = (g * 3 + which) * gw
            fills.append(
                pltpu.make_async_copy(
                    weight.at[which, :, pl.ds(g * gw, gw)],
                    w.at[aligned(f * dblk, dblk), pl.ds(at, gw)],
                    fill_w.at[len(fills)],
                )
            )

    @pl.when(c == t)
    def _():
        for one in fills:
            one.start()

    greet([{"context": 1 - c}] + [peer(offset) for offset in peers])
    x_copies = [
        remote(
            tokens.at[t, pl.ds(i * chunk, chunk)],
            x.at[pl.ds(span + i * chunk, chunk)],
            x_send.at[i],
            x_recv.at[i],
            {"context": 1 - c},
        )
        for i in range(chunks)
    ]
    for one in x_copies:
        one.start()
    y_copy = remote(block(f), block(f), y_sems.at[0], y_sems.at[1], {"tensor": 1 - t})

    @pl.when(c == t)
    def _():
        for one in fills:
            one.wait()
        y_copy.start()

    def small_copy(i, source):
        return remote(small, smalls.at[source], s_send.at[i], s_recv.at[source], peer(peers[i]))

    me = f * nt + t
    for i in range(len(peers)):
        small_copy(i, me).start()
    smalls[me] = small[...]

    @pl.when(c != t)
    def _():
        y_copy.wait_recv()

    def z_copy(d, owner):
        return remote(
            block(owner * 2 + k), block(owner * 2 + k), z_send.at[d - 1], z_recv.at[owner], {"z": lax.rem(z + d, nz)}
        )

    def c_copy(owner, core):
        return remote(
            block(owner * 2 + core), block(owner * 2 + core), c_send.at[owner], c_recv.at[owner], {"core": 1 - k}
        )

    for d in range(1, nz):
        z_copy(d, z).start()
    c_copy(z, k).start()

    for i in range(chunks):
        r = pl.ds(i * chunk, chunk)
        pltpu.make_async_copy(tokens.at[t, r], x.at[r], fill_x.at[i]).wait()
        xt[:, i * chunk : (i + 1) * chunk] = x[i * chunk : (i + 1) * chunk, :].T

    for i in range(len(peers)):
        dz, dk, dt = peers[i]
        source = (lax.rem(z + nz - dz, nz) * 2 + lax.rem(k + dk, 2)) * nt + lax.rem(t + nt - dt, nt)
        small_copy(i, source).wait_recv()

    edge = head_size // nf
    lanes = small.shape[1]
    rows = jnp.concatenate([smalls[fi * nt + c, 0:1, :] for fi in range(nf)], axis=0)
    col = lax.broadcasted_iota(jnp.int32, (lanes, cols), 1)
    source = lax.broadcasted_iota(jnp.int32, (lanes, cols), 0)
    fcol = lax.broadcasted_iota(jnp.int32, (nf, cols), 1)
    mine = lax.rem(fcol, head_size) // edge == lax.broadcasted_iota(jnp.int32, (nf, cols), 0)
    biases = []
    for kind in range(2):
        pick = source == col // head_size * edge + lax.rem(col, edge) + kind * heads * edge
        spread_out = mm(rows, jnp.where(pick, 1.0, 0.0).astype(BF))
        biases.append(jnp.sum(jnp.where(mine, spread_out, 0.0), axis=0, keepdims=True))
    parts = [biases[0], jnp.zeros_like(biases[0]), biases[1]]
    bias = jnp.concatenate(
        [parts[which][:, g * gw : (g + 1) * gw] for g in range(cols // gw) for which in range(3)], axis=1
    )

    for d in range(1, nz):
        owner = lax.rem(z + nz - d, nz)
        z_copy(d, owner).wait_recv()
        c_copy(owner, k).start()
    for owner in range(nz):
        c_copy(owner, 1 - k).wait_recv()

    w_done = pltpu.make_async_copy(w, w_out, out_sems.at[0, 0])
    w_done.start()
    small_done = pltpu.make_async_copy(smalls, small_out, out_sems.at[0, 1])
    small_done.start()

    def project(i):
        r = aligned(i * chunk, chunk)
        acc = mm(x[r, :], w[...]) + bias
        qkv[r, :] = acc.astype(BF)
        pltpu.make_async_copy(qkv.at[r], qkv_out.at[r], out_sems.at[1, i]).start()

    @pl.loop(0, chunks)
    def _(i):
        project(i)

    @pl.loop(0, chunks)
    def _(i):
        remote(
            tokens.at[t, aligned(i * chunk, chunk)],
            x.at[aligned(span + i * chunk, chunk)],
            x_send.at[i],
            x_recv.at[i],
            {"context": 1 - c},
        ).wait_recv()
        r = aligned(span + i * chunk, chunk)
        xt[:, r] = x[r, :].T
        project(chunks + i)

    xt_done = pltpu.make_async_copy(xt, xt_out, out_sems.at[0, 2])
    xt_done.start()
    for i in range(2 * chunks):
        r = pl.ds(i * chunk, chunk)
        pltpu.make_async_copy(qkv.at[r], qkv_out.at[r], out_sems.at[1, i]).wait()
    for one in (w_done, small_done, xt_done):
        one.wait()
    for one in x_copies:
        one.wait_send()
    for i in range(len(peers)):
        small_copy(i, me).wait_send()
    for d in range(1, nz):
        z_copy(d, z).wait_send()
    for owner in range(nz):
        c_copy(owner, k).wait_send()

    @pl.when(c == t)
    def _():
        y_copy.wait_send()


def open_layer(tokens, weight, small, nz, nt, heads, head_size, group):
    span, width = tokens.shape[1:]
    cols = heads * head_size
    chunk = 256
    chunks = span // chunk
    nf = nz * 2
    dma = pltpu.SemaphoreType.DMA
    hbm = pl.BlockSpec(memory_space=pl.ANY)
    fixed = pl.BlockSpec(memory_space=pltpu.HBM)
    moved = 2 * (span * width * 2 + 4 * width * cols * 3)
    return pl.pallas_call(
        functools.partial(
            open_kernel, nz=nz, nt=nt, heads=heads, head_size=head_size, group=group, chunk=chunk
        ),
        out_shape=(
            jax.ShapeDtypeStruct((width, 2 * span), BF),
            jax.ShapeDtypeStruct((width, 3 * cols), BF),
            jax.ShapeDtypeStruct((2 * span, 3 * cols), BF),
            jax.ShapeDtypeStruct((nf * nt,) + small.shape, BF),
        ),
        in_specs=[fixed, fixed, pl.BlockSpec(memory_space=pltpu.VMEM)],
        out_specs=(hbm,) * 4,
        scratch_shapes=[
            pltpu.VMEM((2 * span, width), BF),
            pltpu.VMEM((width, 2 * span), BF),
            pltpu.VMEM((width, 3 * cols), BF),
            pltpu.VMEM((2 * span, 3 * cols), BF),
            pltpu.VMEM((nf * nt,) + small.shape, BF),
            dma((chunks,)),
            dma((heads // 2 // group * 3,)),
            dma((chunks,)),
            dma((chunks,)),
            dma((nf * nt,)),
            dma((nf * nt,)),
            dma((2,)),
            dma((nz,)),
            dma((nz,)),
            dma((nz,)),
            dma((nz,)),
            dma((2, max(3, 2 * chunks))),
        ],
        compiler_params=pltpu.CompilerParams(
            collective_id=0, has_side_effects=True, vmem_limit_bytes=58 << 20
        ),
        cost_estimate=pl.CostEstimate(
            flops=2 * 2 * span * width * 3 * cols, bytes_accessed=moved, transcendentals=0
        ),
        name="open_layer",
    )(tokens, weight, small)


def close_kernel(
    dqkv_in, w_in, xt_in, grad_in, vec_one, vec_two, tokens_out, grad_out, sums_out, vec_out,
    dqkv, w, xt, dres, own, xs, xr, fin, away, near, zs, zr, piece, last,
    sums, sums_near, sums_z, sums_last, vecs, vecs_near, vecs_z, vecs_last,
    fill, x_send, x_recv, y_send, y_recv, c_send, c_recv, z_send, z_recv, p_send, p_recv, o_sems,
    *, nz, chunk, tile, part,
):
    z, k, c, t = (lax.axis_index(name) for name in AXES)
    rows, wide = dqkv.shape
    span = rows // 2
    dblk = piece.shape[0]
    chunks = span // chunk
    steps = wide // tile
    x_dev, y_dev, core_dev = {"context": 1 - c}, {"tensor": 1 - t}, {"core": 1 - k}
    diag = {"context": 1 - c, "tensor": 1 - t}

    loads = [
        pltpu.make_async_copy(w_in, w, fill.at[0]),
        pltpu.make_async_copy(dqkv_in.at[pl.ds(span, span)], dqkv.at[pl.ds(span, span)], fill.at[1]),
        pltpu.make_async_copy(dqkv_in.at[pl.ds(0, span)], dqkv.at[pl.ds(0, span)], fill.at[2]),
    ]
    for kk in range(2):
        for zi in range(nz):
            source = zi * 2 + lax.rem(1 - k + kk, 2)
            loads.append(
                pltpu.make_async_copy(
                    xt_in.at[aligned(source * dblk, dblk)], xt.at[kk, pl.ds(zi * dblk, dblk)], fill.at[len(loads)]
                )
            )
    for source, dest in (
        (grad_in, dres),
        (vec_one, vecs.at[pl.ds(0, 8)]),
        (vec_two, vecs.at[pl.ds(8, 8)]),
    ):
        loads.append(pltpu.make_async_copy(source, dest, fill.at[len(loads)]))
    for one in loads:
        one.start()
    greet([x_dev, y_dev, diag, core_dev] + [{"z": lax.rem(z + d, nz)} for d in range(1, nz)])

    def x_copy(i):
        return remote(xs.at[i], xr.at[i], x_send.at[i], x_recv.at[i], x_dev)

    def y_copy(i):
        return remote(fin.at[i], tokens_out.at[t, aligned(i * chunk, chunk)], y_send.at[i], y_recv.at[i], y_dev)

    def leave(i):
        value = mm_nt(dqkv[aligned(span + i * 2 * chunk, 2 * chunk), :], w[...]).astype(BF)
        xs[2 * i] = value[:chunk]
        xs[2 * i + 1] = value[chunk:]
        x_copy(2 * i).start()
        x_copy(2 * i + 1).start()

    loads[0].wait()
    loads[1].wait()

    @pl.loop(0, 1)
    def _(i):
        leave(i)

    for one in loads[2:]:
        one.wait()
    ones = jnp.ones((8, rows), BF)
    sums[...] = jnp.zeros(sums.shape, F32)

    @pl.loop(0, steps)
    def _(j):
        value = dqkv[:, aligned(j * tile, tile)]
        away[:, aligned(j * tile, tile)] = mm(xt[0], value).astype(BF)
        total = mm(ones, value)
        for u in range(tile // 128):
            sums[pl.ds(j * (tile // 128) + u, 1), :] = total[0:1, u * 128 : (u + 1) * 128]

    core_copies = [
        remote(mine, theirs, c_send.at[i], c_recv.at[i], core_dev)
        for i, (mine, theirs) in enumerate(((away, near), (sums, sums_near), (vecs, vecs_near)))
    ]
    for one in core_copies:
        one.start()

    @pl.loop(1, chunks // 2)
    def _(i):
        leave(i)

    for one in core_copies:
        one.wait_recv()
    sums_z[z] = sums[...] + sums_near[...]
    vecs_z[z] = vecs[...] + vecs_near[...]

    @pl.loop(0, steps)
    def _(j):
        cut = aligned(j * tile, tile)
        zs[:, cut] = (mm(xt[1], dqkv[:, cut]) + near[:, cut].astype(F32)).astype(BF)

    def z_copies(d, owner):
        dev = {"z": lax.rem(z + d, nz)}
        return [
            remote(buf.at[owner], buf.at[owner], z_send.at[i, d - 1], z_recv.at[i, owner], dev)
            for i, buf in enumerate((sums_z, vecs_z))
        ]

    def ring(step):
        source = zs.at[aligned(lax.rem(z + nz - step, nz) * dblk, dblk)]
        return remote(source, zr.at[step - 1], z_send.at[2, step - 1], z_recv.at[2, step - 1], {"z": lax.rem(z + 1, nz)})

    def arrived(step):
        ring(step).wait_recv()
        spot = aligned(lax.rem(z + 2 * nz - step - 1, nz) * dblk, dblk)
        zs[spot, :] = (zs[spot, :].astype(F32) + zr[step - 1].astype(F32)).astype(BF)
        if step + 1 < nz:
            ring(step + 1).start()

    ring(1).start()
    for d in range(1, nz):
        for one in z_copies(d, z):
            one.start()

    @pl.loop(0, chunks // 2)
    def _(i):
        r = aligned(i * 2 * chunk, 2 * chunk)
        own[r, :] = mm_nt(dqkv[r, :], w[...]) + dres[r, :]

    def finish(i):
        x_copy(i).wait_recv()
        r = aligned(i * chunk, chunk)
        fin[i] = (own[r, :] + xr[i].astype(F32)).astype(BF)
        pltpu.make_async_copy(fin.at[i], tokens_out.at[t, r], o_sems.at[i]).start()
        y_copy(i).start()

    cuts = [chunks * step // nz for step in range(nz + 1)]
    for step in range(1, nz):
        pl.loop(cuts[step - 1], cuts[step])(finish)
        arrived(step)
    for d in range(1, nz):
        for one in z_copies(d, lax.rem(z + nz - d, nz)):
            one.wait_recv()
    piece[...] = zs[aligned(z * dblk, dblk), :]
    sums_last[0] = jnp.sum(sums_z[...], axis=0)
    vecs_last[0] = jnp.sum(vecs_z[...], axis=0)

    trio = ((x_dev, 0), (y_dev, 1), (diag, 2))
    p_x, p_y, p_d = (remote(piece, last.at[i], p_send.at[i], p_recv.at[i], dev) for dev, i in trio)
    everywhere = [
        remote(buf.at[0], buf.at[1 + i], p_send.at[at + i], p_recv.at[at + i], dev)
        for dev, i in trio
        for buf, at in ((sums_last, 3), (vecs_last, 6))
    ]
    for one in everywhere:
        one.start()

    @pl.when(c == t)
    def _():
        p_x.start()

    @pl.when(c != t)
    def _():
        p_y.start()
        p_d.start()

    pl.loop(cuts[nz - 1], chunks)(finish)

    def give(value):
        width = part
        for g in range(wide // (3 * width)):
            for which in range(3):
                at = (g * 3 + which) * width
                grad_out[which, :, g * width : (g + 1) * width] = value[:, at : at + width]

    for one in everywhere:
        one.wait()
    near_pair = sums_last[0] + sums_last[2]
    sums_out[...] = jnp.where(c == t, near_pair, sums_last[1] + sums_last[3])
    vec_out[...] = (vecs_last[0] + vecs_last[2]) + (vecs_last[1] + vecs_last[3])

    @pl.when(c == t)
    def _():
        p_y.wait_recv()
        give(piece[...].astype(F32) + last[1].astype(F32))
        p_x.wait_send()

    @pl.when(c != t)
    def _():
        p_x.wait_recv()
        p_d.wait_recv()
        give(last[0].astype(F32) + last[2].astype(F32))
        p_y.wait_send()
        p_d.wait_send()

    for one in core_copies:
        one.wait_send()
    for d in range(1, nz):
        ring(d).wait_send()
        for one in z_copies(d, z):
            one.wait_send()

    @pl.loop(0, chunks)
    def _(i):
        r = aligned(i * chunk, chunk)
        x_copy(i).wait_send()
        pltpu.make_async_copy(fin.at[i], tokens_out.at[t, r], o_sems.at[i]).wait()
        y_copy(i).wait_send()
        remote(fin.at[i], tokens_out.at[1 - t, r], y_send.at[i], y_recv.at[i], y_dev).wait_recv()


def close_layer(dqkv, w, xt, grad_in, vec_one, vec_two, nz, part):
    rows, wide = dqkv.shape
    width = w.shape[0]
    span = rows // 2
    dblk = width // (2 * nz)
    chunk, tile = 128, 256
    chunks = span // chunk
    dma = pltpu.SemaphoreType.DMA
    hbm = pl.BlockSpec(memory_space=pl.ANY)
    vmem = pl.BlockSpec(memory_space=pltpu.VMEM)
    sum_shape = (wide // 128 + -(wide // 128) % 8, 128)
    vec_shape = (16, width)
    return pl.pallas_call(
        functools.partial(close_kernel, nz=nz, chunk=chunk, tile=tile, part=part),
        out_shape=(
            jax.ShapeDtypeStruct((2, span, width), BF),
            jax.ShapeDtypeStruct((3, dblk, wide // 3), F32),
            jax.ShapeDtypeStruct(sum_shape, F32),
            jax.ShapeDtypeStruct(vec_shape, F32),
        ),
        in_specs=[hbm] * 6,
        out_specs=(hbm, vmem, vmem, vmem),
        scratch_shapes=[
            pltpu.VMEM((rows, wide), BF),
            pltpu.VMEM((width, wide), BF),
            pltpu.VMEM((2, nz * dblk, rows), BF),
            pltpu.VMEM((span, width), F32),
            pltpu.VMEM((span, width), F32),
            pltpu.VMEM((chunks, chunk, width), BF),
            pltpu.VMEM((chunks, chunk, width), BF),
            pltpu.VMEM((chunks, chunk, width), BF),
            pltpu.VMEM((nz * dblk, wide), BF),
            pltpu.VMEM((nz * dblk, wide), BF),
            pltpu.VMEM((nz * dblk, wide), BF),
            pltpu.VMEM((nz, dblk, wide), BF),
            pltpu.VMEM((dblk, wide), BF),
            pltpu.VMEM((3, dblk, wide), BF),
            pltpu.VMEM(sum_shape, F32),
            pltpu.VMEM(sum_shape, F32),
            pltpu.VMEM((nz,) + sum_shape, F32),
            pltpu.VMEM((4,) + sum_shape, F32),
            pltpu.VMEM(vec_shape, F32),
            pltpu.VMEM(vec_shape, F32),
            pltpu.VMEM((nz,) + vec_shape, F32),
            pltpu.VMEM((4,) + vec_shape, F32),
            dma((6 + 2 * nz,)),
            dma((chunks,)),
            dma((chunks,)),
            dma((chunks,)),
            dma((chunks,)),
            dma((3,)),
            dma((3,)),
            dma((3, nz)),
            dma((3, nz)),
            dma((9,)),
            dma((9,)),
            dma((chunks,)),
        ],
        compiler_params=pltpu.CompilerParams(
            collective_id=1, has_side_effects=True, vmem_limit_bytes=46 << 20
        ),
        cost_estimate=pl.CostEstimate(
            flops=4 * rows * width * wide, bytes_accessed=30 << 20, transcendentals=0
        ),
        name="close_layer",
    )(dqkv, w, xt, grad_in, vec_one, vec_two)


def mean_of(rows):
    return jnp.mean(rows, axis=-1, keepdims=True)


def load_blocks(stack, start, dest, sems, nt, rows_by_f):
    count, rows = stack.shape[:2]
    columns = dest.shape[1] // nt if rows_by_f else stack.shape[2]
    copies = []
    for b in range(count):
        first, second = (b // nt, b % nt) if rows_by_f else (b % nt, b // nt)
        spot = dest.at[pl.ds(first * rows, rows), pl.ds(second * columns, columns)]
        copies.append(pltpu.make_async_copy(stack.at[b, :, pl.ds(start, columns)], spot, sems.at[b]))
    return copies


def up_kernel(
    t_ref, ctx, tok, vecs, up_add, up_in, first, norm_one, inv_one, first_t, act, slope,
    up, proj, low, u, fill,
    *, nt, tile,
):
    i = pl.program_id(0)
    width, hidden = up.shape
    tiles = hidden // tile
    up_fill = load_blocks(up_in, 0, up, fill.at[0], nt, True)
    proj_fill = load_blocks(up_in, hidden // nt, proj, fill.at[1], nt, True)

    @pl.when(i == 0)
    def _():
        for one in proj_fill + up_fill:
            one.start()
        for one in proj_fill:
            one.wait()

    def vec(row):
        return vecs[row : row + 1, :]

    h = tok[0].astype(F32) + (mm_nt(ctx[...], proj[...]) + vec(0))
    centred = h - mean_of(h)
    inv = lax.rsqrt(mean_of(centred * centred) + NORM_EPS)
    normed = centred * inv
    norm_one[...] = normed
    inv_one[...] = jnp.broadcast_to(inv, inv_one.shape)
    normed = normed * vec(1) + vec(2)
    first[...] = normed
    low[...] = normed.astype(BF)
    first_t[...] = low[...].T

    @pl.when(i == 0)
    def _():
        for one in up_fill:
            one.wait()

    u[0] = mm(low[...], up[:, :tile])

    def activate(j, slot):
        cut = aligned(j * tile, tile)
        value = u[slot] + up_add[0:1, cut]
        phi = 0.5 + 0.5 * lax.erf(value * (0.5**0.5))
        act[:, cut] = (value * phi).astype(BF)
        slope[:, cut] = (phi + value * (jnp.exp(-0.5 * value * value) * ((2.0 * jnp.pi) ** -0.5))).astype(BF)

    @pl.loop(0, tiles - 1)
    def _(j):
        slot = lax.rem(j, 2)
        following = mm(low[...], up[:, aligned((j + 1) * tile, tile)])
        activate(j, slot)
        u[1 - slot] = following

    activate(tiles - 1, (tiles - 1) % 2)


def up_layer(t, ctx, tokens, vecs, up_add, up_all, nt):
    span, width = ctx.shape
    hidden = up_add.shape[1]
    block, tile = 512, 512
    hbm = pl.BlockSpec(memory_space=pl.ANY)
    rows = pl.BlockSpec((block, width), lambda i, _: (i, 0))
    wide = pl.BlockSpec((block, hidden), lambda i, _: (i, 0))
    whole = lambda shape: pl.BlockSpec(shape, lambda i, _: (0,) * len(shape))
    picked = pl.BlockSpec((1, block, width), lambda i, t_ref: (t_ref[0], i, 0))
    sds = jax.ShapeDtypeStruct
    return pl.pallas_call(
        functools.partial(up_kernel, nt=nt, tile=tile),
        out_shape=(
            sds((span, width), F32),
            sds((span, width), F32),
            sds((span, 128), F32),
            sds((width, span), BF),
            sds((span, hidden), BF),
            sds((span, hidden), BF),
        ),
        grid_spec=pltpu.PrefetchScalarGridSpec(
            num_scalar_prefetch=1,
            grid=(span // block,),
            in_specs=[rows, picked, whole(vecs.shape), whole(up_add.shape), hbm],
            out_specs=(
                rows,
                rows,
                pl.BlockSpec((block, 128), lambda i, _: (i, 0)),
                pl.BlockSpec((width, block), lambda i, _: (0, i)),
                wide,
                wide,
            ),
            scratch_shapes=[
                pltpu.VMEM((width, hidden), BF),
                pltpu.VMEM((width, width), BF),
                pltpu.VMEM((block, width), BF),
                pltpu.VMEM((2, block, tile), F32),
                pltpu.SemaphoreType.DMA((2, up_all.shape[0])),
            ],
        ),
        compiler_params=pltpu.CompilerParams(vmem_limit_bytes=60 << 20),
        cost_estimate=pl.CostEstimate(
            flops=2 * span * width * (width + hidden), bytes_accessed=40 << 20, transcendentals=2 * span * hidden
        ),
        name="up_layer",
    )(t, ctx, tokens, vecs, up_add, up_all)


def add_rows(sums, row, value):
    sums[row] += jnp.sum(value.reshape(-1, 8, value.shape[1]), axis=0)


def down_kernel(
    t_ref, cot, vecs, first, act, down_in, out, branch, branch_t, grad_second, vec_sums,
    down, acc, sums, fill,
    *, nt,
):
    i = pl.program_id(0)
    hidden, width = down.shape
    down_fill = load_blocks(down_in, 0, down, fill, nt, False)

    @pl.when(i == 0)
    def _():
        for one in down_fill:
            one.start()
        sums[...] = jnp.zeros(sums.shape, F32)

    def vec(row):
        return vecs[row : row + 1, :]

    tile = 256
    per = len(down_fill) * tile // width

    @pl.loop(0, width // tile)
    def _(j):
        for ji in range(width // tile):

            @pl.when((i == 0) & (j == ji))
            def _():
                for one in down_fill[ji * per : (ji + 1) * per]:
                    one.wait()

        cut = aligned(j * tile, tile)
        acc[:, cut] = mm(act[...], down[:, cut])

    h = first[...] + (acc[...] + vec(3))
    centred = h - mean_of(h)
    inv = lax.rsqrt(mean_of(centred * centred) + NORM_EPS)
    normed = centred * inv
    out[...] = (normed * vec(4) + vec(5)).astype(BF)
    grad = cot[0].astype(F32)
    add_rows(sums, 1, grad * normed)
    add_rows(sums, 2, grad)
    grad = grad * vec(4)
    grad = inv * (grad - mean_of(grad) - normed * mean_of(grad * normed))
    grad_second[...] = grad
    low = grad.astype(BF)
    branch[...] = low
    add_rows(sums, 0, low.astype(F32))
    branch_t[...] = low.T

    @pl.when(i == pl.num_programs(0) - 1)
    def _():
        for row in range(3):
            vec_sums[row : row + 1, :] = jnp.sum(sums[row], axis=0, keepdims=True)
        vec_sums[3:8, :] = jnp.zeros((5, width), F32)


def down_layer(t, out_grad, vecs, first, act, down_all, nt):
    span, width = first.shape
    hidden = act.shape[1]
    block = 512
    rows = pl.BlockSpec((block, width), lambda i, _: (i, 0))
    whole = lambda shape: pl.BlockSpec(shape, lambda i, _: (0,) * len(shape))
    sds = jax.ShapeDtypeStruct
    return pl.pallas_call(
        functools.partial(down_kernel, nt=nt),
        out_shape=(
            sds((span, width), BF),
            sds((span, width), BF),
            sds((width, span), BF),
            sds((span, width), F32),
            sds((8, width), F32),
        ),
        grid_spec=pltpu.PrefetchScalarGridSpec(
            num_scalar_prefetch=1,
            grid=(span // block,),
            in_specs=[
                pl.BlockSpec((1, block, width), lambda i, t_ref: (t_ref[0], i, 0)),
                whole(vecs.shape),
                rows,
                pl.BlockSpec((block, hidden), lambda i, _: (i, 0)),
                pl.BlockSpec(memory_space=pl.ANY),
            ],
            out_specs=(rows, rows, pl.BlockSpec((width, block), lambda i, _: (0, i)), rows, whole((8, width))),
            scratch_shapes=[
                pltpu.VMEM((hidden, width), BF),
                pltpu.VMEM((block, width), F32),
                pltpu.VMEM((3, 8, width), F32),
                pltpu.SemaphoreType.DMA((down_all.shape[0],)),
            ],
        ),
        compiler_params=pltpu.CompilerParams(vmem_limit_bytes=60 << 20),
        cost_estimate=pl.CostEstimate(
            flops=2 * span * width * hidden, bytes_accessed=30 << 20, transcendentals=0
        ),
        name="down_layer",
    )(t, out_grad, vecs, first, act, down_all)


def back_kernel(
    vecs, branch, grad_second, slope, norm_one, inv_one, up_in, down_in, partial,
    hid, attn_t, grad_in, grad_ctx, vec_sums, quarter,
    up, down, proj, acc, sums, sums_u, by_y, near_y, by_x, near_x, last_x, last_y,
    fill, own_fill, one_send, one_recv, two_send, two_recv,
    *, nz, nt, tile,
):
    i = pl.program_id(0)
    c, t = lax.axis_index("context"), lax.axis_index("tensor")
    x_dev, y_dev = {"context": 1 - c}, {"tensor": 1 - t}
    width, hidden = up.shape
    rest = last_x.shape[0] // nz
    half = last_x.shape[1]
    tall = nz * 2 * rest
    left, right = pl.ds(0, half), pl.ds(half, half)
    own_copies = [pltpu.make_async_copy(partial.at[aligned(t * tall, tall), left], by_y, own_fill.at[0])]
    first_copies = [
        remote(partial.at[aligned((1 - t) * tall, tall), left], near_y, one_send.at[0], one_recv.at[0], y_dev)
    ]
    for b in range(nt * nz):
        spot = pl.ds(b * rest, rest)
        own_copies.append(
            pltpu.make_async_copy(
                partial.at[aligned((b * 2 + c) * rest, rest), right], by_x.at[spot], own_fill.at[1 + b]
            )
        )
        first_copies.append(
            remote(
                partial.at[aligned((b * 2 + 1 - c) * rest, rest), right],
                near_x.at[spot],
                one_send.at[1 + b],
                one_recv.at[1 + b],
                x_dev,
            )
        )
    second_copies = [
        remote(by_x.at[aligned((1 - t) * nz * rest, nz * rest)], last_y, two_send.at[0], two_recv.at[0], y_dev)
    ]
    for zi in range(nz):
        second_copies.append(
            remote(
                by_y.at[aligned((zi * 2 + 1 - c) * rest, rest)],
                last_x.at[pl.ds(zi * rest, rest)],
                two_send.at[1 + zi],
                two_recv.at[1 + zi],
                x_dev,
            )
        )

    @pl.when(i == 0)
    def _():
        greet([x_dev, y_dev])
        for one in first_copies + own_copies:
            one.start()

    @pl.when(i == 2)
    def _():
        for one in own_copies:
            one.wait()
        for one in first_copies:
            one.wait_recv()
        by_y[...] = (by_y[...].astype(F32) + near_y[...].astype(F32)).astype(BF)
        by_x[...] = (by_x[...].astype(F32) + near_x[...].astype(F32)).astype(BF)
        for one in second_copies:
            one.start()

    down_fill = load_blocks(down_in, 0, down, fill.at[0], nt, False)
    up_fill = load_blocks(up_in, 0, up, fill.at[1], nt, True)
    proj_fill = load_blocks(up_in, hidden // nt, proj, fill.at[2], nt, True)

    @pl.when(i == 0)
    def _():
        for ti in range(nt):
            for one in down_fill[ti::nt] + up_fill[ti::nt]:
                one.start()
        for one in proj_fill:
            one.start()
        sums[...] = jnp.zeros(sums.shape, F32)
        sums_u[...] = jnp.zeros(sums_u.shape, F32)

    ones = jnp.ones((8, branch.shape[0]), BF)
    acc[...] = grad_second[...]
    per = hidden // tile // nt

    @pl.loop(0, hidden // tile)
    def _(j):
        for ti in range(nt):

            @pl.when((i == 0) & (j == ti * per))
            def _():
                for one in down_fill[ti::nt] + up_fill[ti::nt]:
                    one.wait()

        cut = aligned(j * tile, tile)
        low_hid = (mm_nt(branch[...], down[cut, :]) * slope[:, cut].astype(F32)).astype(BF)
        hid[:, cut] = low_hid
        sums_u[:, cut] += mm(ones, low_hid)
        acc[...] += mm_nt(low_hid, up[:, cut])

    grad = acc[...]
    normed = norm_one[...]
    add_rows(sums, 1, grad * normed)
    add_rows(sums, 2, grad)
    grad = grad * vecs[1:2, :]
    grad = inv_one[:, 0:1] * (grad - mean_of(grad) - normed * mean_of(grad * normed))
    grad_in[...] = grad
    low = grad.astype(BF)
    add_rows(sums, 0, low.astype(F32))
    attn_t[...] = low.T

    @pl.when(i == 0)
    def _():
        for one in proj_fill:
            one.wait()

    grad_ctx[...] = mm(low, proj[...]).astype(BF)

    @pl.when(i == pl.num_programs(0) - 1)
    def _():
        for row in range(3):
            vec_sums[row : row + 1, :] = jnp.sum(sums[row], axis=0, keepdims=True)
        vec_sums[3:8, :] = jnp.zeros((5, width), F32)
        for row in range(hidden // width):
            vec_sums[3 + row : 4 + row, :] = sums_u[0:1, row * width : (row + 1) * width]
        for one in second_copies:
            one.wait_recv()
        for zi in range(nz):
            spot = slice(zi * rest, (zi + 1) * rest)
            mine = by_y[aligned((zi * 2 + c) * rest, rest), :]
            quarter[spot, :half] = (mine.astype(F32) + last_x[spot, :].astype(F32)).astype(BF)
        mine = by_x[aligned(t * nz * rest, nz * rest), :]
        quarter[:, half:] = (mine.astype(F32) + last_y[...].astype(F32)).astype(BF)
        for one in first_copies + second_copies:
            one.wait_send()


def back_layer(vecs, branch, grad_second, slope, norm_one, inv_one, up_all, down_all, partial, nz, nt):
    span, width = branch.shape
    hidden = slope.shape[1]
    block, tile = span // 4, 512
    rest, half = partial.shape[0] // (nt * nz * 2), partial.shape[1] // 2
    quarter = (nz * rest, 2 * half)
    hbm = pl.BlockSpec(memory_space=pl.ANY)
    rows = pl.BlockSpec((block, width), lambda i: (i, 0))
    wide = pl.BlockSpec((block, hidden), lambda i: (i, 0))
    whole = lambda shape: pl.BlockSpec(shape, lambda i: (0,) * len(shape))
    sds = jax.ShapeDtypeStruct
    return pl.pallas_call(
        functools.partial(back_kernel, nz=nz, nt=nt, tile=tile),
        out_shape=(
            sds((span, hidden), BF),
            sds((width, span), BF),
            sds((span, width), F32),
            sds((span, width), BF),
            sds((8, width), F32),
            sds(quarter, BF),
        ),
        grid=(span // block,),
        in_specs=[
            whole(vecs.shape),
            rows,
            rows,
            wide,
            rows,
            pl.BlockSpec((block, 128), lambda i: (i, 0)),
            hbm,
            hbm,
            hbm,
        ],
        out_specs=(
            wide, pl.BlockSpec((width, block), lambda i: (0, i)), rows, rows, whole((8, width)), whole(quarter),
        ),
        scratch_shapes=[
            pltpu.VMEM((width, hidden), BF),
            pltpu.VMEM((hidden, width), BF),
            pltpu.VMEM((width, width), BF),
            pltpu.VMEM((block, width), F32),
            pltpu.VMEM((3, 8, width), F32),
            pltpu.VMEM((8, hidden), F32),
            pltpu.VMEM((nz * 2 * rest, half), BF),
            pltpu.VMEM((nz * 2 * rest, half), BF),
            pltpu.VMEM((nt * nz * rest, half), BF),
            pltpu.VMEM((nt * nz * rest, half), BF),
            pltpu.VMEM((nz * rest, half), BF),
            pltpu.VMEM((nz * rest, half), BF),
            pltpu.SemaphoreType.DMA((3, up_all.shape[0])),
            pltpu.SemaphoreType.DMA((1 + nt * nz,)),
            pltpu.SemaphoreType.DMA((1 + nt * nz,)),
            pltpu.SemaphoreType.DMA((1 + nt * nz,)),
            pltpu.SemaphoreType.DMA((1 + nz,)),
            pltpu.SemaphoreType.DMA((1 + nz,)),
        ],
        compiler_params=pltpu.CompilerParams(
            collective_id=4, has_side_effects=True, vmem_limit_bytes=60 << 20
        ),
        cost_estimate=pl.CostEstimate(
            flops=2 * span * width * (width + 2 * hidden), bytes_accessed=60 << 20, transcendentals=0
        ),
        name="back_layer",
    )(vecs, branch, grad_second, slope, norm_one, inv_one, up_all, down_all, partial)


def grads_kernel(*refs, pairs, nz, nt, chunk):
    lefts, rights = refs[0 : 2 * pairs : 2], refs[1 : 2 * pairs : 2]
    refs = refs[2 * pairs :]
    quarter = None
    if len(refs) > 11:
        quarter, dctx_in, packed, shard, dctx = refs[:5]
        mine, others, dctx_own, mine_fill, dctx_sems, q_send, q_recv = refs[-7:]
        refs = (packed,) + refs[5:-7]
    packed, left, right, away, near, stage, l_fill, r_fill, send, recv, out_sems = refs
    z = lax.axis_index("z")
    k = lax.axis_index("core")
    core_dev = {"core": 1 - k}
    dblk = left.shape[2] // nz
    span = right.shape[1]
    plan = []
    base = 0
    for which in range(pairs):
        size = rights[which].shape[1] // nt
        for ti in range(nt):
            for at in range(0, size, min(chunk, size)):
                step = min(chunk, size)
                plan.append((which, ti * size + at, ti, base + at, step))
        base += size

    l_copies = [
        [
            pltpu.make_async_copy(
                lefts[which].at[aligned((zi * 2 + lax.rem(k + 1 + kk, 2)) * dblk, dblk)],
                left.at[which, kk, pl.ds(zi * dblk, dblk)],
                l_fill.at[which, kk, zi],
            )
            for kk in range(2)
            for zi in range(nz)
        ]
        for which in range(pairs)
    ]
    r_copies = [
        pltpu.make_async_copy(
            rights[which].at[:, pl.ds(col, step)], right.at[n, :, pl.ds(0, step)], r_fill.at[n]
        )
        for n, (which, col, _ti, _out, step) in enumerate(plan)
    ]
    for n, (which, _col, _ti, _out, _step) in enumerate(plan):
        if n == 0 or plan[n - 1][0] != which:
            for one in l_copies[which]:
                one.start()
        r_copies[n].start()
    friends = [core_dev]
    if quarter is not None:
        c = lax.axis_index("context")
        friends += [{"context": 1 - c}]
        friends += [{"z": lax.rem(z + d, nz)} for d in range(1, nz)]
    greet(friends)
    if quarter is not None:
        rest = mine.shape[0]

        def q_copy(d, owner, target):
            return remote(
                quarter.at[aligned(target * rest, rest)],
                others.at[owner],
                q_send.at[d - 1],
                q_recv.at[owner],
                {"z": lax.rem(z + d, nz)},
            )

        cols = dctx.shape[1]
        own_in = pltpu.make_async_copy(dctx_in.at[:, aligned(c * cols, cols)], dctx_own, dctx_sems.at[0])
        own_out = pltpu.make_async_copy(dctx_own, dctx.at[pl.ds(0, span)], dctx_sems.at[1])
        dctx_copy = remote(
            dctx_in.at[:, aligned((1 - c) * cols, cols)],
            dctx.at[pl.ds(span, span)],
            dctx_sems.at[2],
            dctx_sems.at[3],
            {"context": 1 - c},
        )
        own_in.start()
        dctx_copy.start()
        own = pltpu.make_async_copy(quarter.at[aligned(z * rest, rest)], mine, mine_fill)
        own.start()

    def exchange(n):
        step = plan[n][4]
        cut = pl.ds(0, step)
        return remote(away.at[n, :, cut], near.at[n, :, cut], send.at[n], recv.at[n], core_dev)

    sub = 256
    for n, (which, _col, _ti, _out, step) in enumerate(plan):
        if n == 0 or plan[n - 1][0] != which:
            for one in l_copies[which]:
                one.wait()
        r_copies[n].wait()

        @pl.loop(0, step // sub)
        def _(j, n=n, which=which):
            cut = aligned(j * sub, sub)
            away[n, :, cut] = mm(left[which, 0], right[n, :, cut]).astype(BF)

        exchange(n).start()

    if quarter is not None:
        own_in.wait()
        own_out.start()
        for d in range(1, nz):
            q_copy(d, z, lax.rem(z + d, nz)).start()
    outs = []
    for n, (which, _col, ti, out, step) in enumerate(plan):
        exchange(n).wait_recv()
        slot = n % 2
        if n >= 2:
            outs[n - 2].wait()

        @pl.loop(0, step // sub)
        def _(j, n=n, which=which, slot=slot):
            cut = aligned(j * sub, sub)
            stage[slot, :, cut] = (
                mm(left[which, 1], right[n, :, cut]) + near[n, :, cut].astype(F32)
            ).astype(BF)

        outs.append(
            pltpu.make_async_copy(
                stage.at[slot, :, pl.ds(0, step)],
                packed.at[pl.ds(ti * nz * dblk, nz * dblk), pl.ds(out, step)],
                out_sems.at[slot],
            )
        )
        outs[n].start()
    for one in outs[-2:]:
        one.wait()
    for n in range(len(plan)):
        exchange(n).wait_send()
    if quarter is not None:
        own.wait()
        total = mine[...].astype(F32)
        for d in range(1, nz):
            owner = lax.rem(z + nz - d, nz)
            q_copy(d, owner, z).wait_recv()
            total = total + others[owner].astype(F32)
        shard[...] = total.astype(BF)
        own_out.wait()
        dctx_copy.wait()
        for d in range(1, nz):
            q_copy(d, z, lax.rem(z + d, nz)).wait_send()


def grads_layer(operands, nz, nt, collective_id, quarter=None, grad_context=None):
    pairs = len(operands) // 2
    width, span = operands[0].shape
    chunk = 1024
    dblk = width // (2 * nz)
    sizes = [one.shape[1] // nt for one in operands[1::2]]
    count = sum(nt * max(1, size // chunk) for size in sizes)
    dma = pltpu.SemaphoreType.DMA
    hbm = pl.BlockSpec(memory_space=pl.ANY)
    out_shape = [jax.ShapeDtypeStruct((nt * nz * dblk, sum(sizes)), BF)]
    out_specs, extra = [hbm], []
    if quarter is not None:
        rest = (quarter.shape[0] // nz, quarter.shape[1])
        operands = operands + [quarter, grad_context]
        dctx = (2 * span, grad_context.shape[1] // 2)
        out_shape += [jax.ShapeDtypeStruct(rest, BF), jax.ShapeDtypeStruct(dctx, BF)]
        out_specs += [pl.BlockSpec(memory_space=pltpu.VMEM), hbm]
        extra = [
            pltpu.VMEM(rest, BF),
            pltpu.VMEM((nz,) + rest, BF),
            pltpu.VMEM((span, dctx[1]), BF),
            dma(()),
            dma((4,)),
            dma((nz,)),
            dma((nz,)),
        ]
    return pl.pallas_call(
        functools.partial(grads_kernel, pairs=pairs, nz=nz, nt=nt, chunk=chunk),
        out_shape=out_shape,
        in_specs=[hbm] * len(operands),
        out_specs=out_specs,
        scratch_shapes=[
            pltpu.VMEM((pairs, 2, nz * dblk, span), BF),
            pltpu.VMEM((count, span, chunk), BF),
            pltpu.VMEM((count, nz * dblk, chunk), BF),
            pltpu.VMEM((count, nz * dblk, chunk), BF),
            pltpu.VMEM((2, nz * dblk, chunk), BF),
            dma((pairs, 2, nz)),
            dma((count,)),
            dma((count,)),
            dma((count,)),
            dma((2,)),
        ]
        + extra,
        compiler_params=pltpu.CompilerParams(
            collective_id=collective_id, has_side_effects=True, vmem_limit_bytes=60 << 20
        ),
        cost_estimate=pl.CostEstimate(
            flops=2 * span * width * nt * sum(sizes), bytes_accessed=40 << 20, transcendentals=0
        ),
        name="grads_layer",
    )(*operands)


def on_device_rows(
    sizes,
    tokens,
    segment_ids,
    qkv_weight,
    qv_bias,
    proj_weight,
    proj_bias,
    first_gain,
    first_shift,
    up_weight,
    up_bias,
    down_weight,
    down_bias,
    second_gain,
    second_shift,
    out_grad,
):
    nf, nc, nt = sizes
    nz = nf // 2
    zbits = nz.bit_length() - 1
    z, k, c, t = (lax.axis_index(name) for name in AXES)
    f = z * 2 + k

    def send(value, target):
        pairs = []
        for fi in range(nf):
            for ci in range(nc):
                for ti in range(nt):
                    to = target(fi // 2, fi % 2, ci, ti)
                    if to is not None:
                        zo, ko, co, tto = to
                        pairs.append(((fi * nc + ci) * nt + ti, ((zo * 2 + ko) * nc + co) * nt + tto))
        return lax.ppermute(value, AXES, pairs)

    def over_x(v):
        return send(v, lambda zi, ki, ci, ti: (zi, ki, 1 - ci, ti))

    def over_y(v):
        return send(v, lambda zi, ki, ci, ti: (zi, ki, ci, 1 - ti))

    def over_core(v):
        return send(v, lambda zi, ki, ci, ti: (zi, 1 - ki, ci, ti))

    def over_z(v):
        return send(v, lambda zi, ki, ci, ti: ((zi + 1) % nz, ki, ci, ti))

    def over_zbit(v, bit):
        return send(v, lambda zi, ki, ci, ti: (zi ^ (1 << bit), ki, ci, ti))

    def z_all(v):
        return [v] + [
            send(v, lambda zi, ki, ci, ti, d=d: ((zi + d) % nz, ki, ci, ti)) for d in range(1, nz)
        ]

    def z_ring(v):
        out = [v]
        for _ in range(nz - 1):
            out.append(over_z(out[-1]))
        return out

    def ordered(index, own, other, axis=0):
        return jnp.where(index == 0, jnp.concatenate([own, other], axis), jnp.concatenate([other, own], axis))

    seq_count, span, width = tokens.shape
    heads = qv_bias.shape[1]
    head_size = qv_bias.shape[2] * nf
    cols = heads * head_size
    hidden = up_weight.shape[1] * nt
    dblk = width // nf

    pairs = heads // 2
    group = max(1, pairs // 2)
    wide = 2 * head_size

    pieces = [qv_bias, up_bias, proj_bias, first_gain, first_shift, down_bias, second_gain, second_shift]
    small = jnp.concatenate([p.reshape(-1, 128) for p in pieces])
    up_at, vec_at = qv_bias.size // 128, (qv_bias.size + up_bias.size) // 128
    small = jnp.pad(small, ((0, -(small.shape[0] + 2) % 16 + 2), (0, 0)))
    own_seg = jnp.where(t == 0, segment_ids[0], segment_ids[1])
    other_seg = over_x(own_seg)
    rows_t, qkv_full, qkv, small = open_layer(tokens, qkv_weight, small, nz, nt, heads, head_size, group)
    small = small.reshape(nf, nt, -1, 128)
    edge = head_size // nf

    def interleave(rows, columns):
        col = lax.broadcasted_iota(jnp.int32, (rows.shape[1], columns), 1)
        source = lax.broadcasted_iota(jnp.int32, (rows.shape[1], columns), 0)
        spread_out = mm(rows, (source == col // head_size * edge + col % edge).astype(BF))
        col = lax.broadcasted_iota(jnp.int32, (nf, columns), 1)
        mine = col % head_size // edge == lax.broadcasted_iota(jnp.int32, (nf, columns), 0)
        return jnp.sum(jnp.where(mine, spread_out, 0.0), axis=0)

    up_add = jnp.concatenate(
        [interleave(small[:, i, up_at:vec_at].reshape(nf, -1), hidden // nt) for i in range(nt)]
    ).reshape(1, hidden)
    vecs = small[:, 0, vec_at : vec_at + 8].transpose(1, 0, 2).reshape(8, width).astype(F32)

    every = AXES[:2] + AXES[3:]
    up_shard = jnp.concatenate([up_weight, proj_weight.T], axis=1)
    up_all = lax.all_gather(up_shard, every).reshape((-1,) + up_shard.shape)
    down_all = lax.all_gather(after(down_weight, up_shard), every).reshape((-1,) + down_weight.shape)

    seg_store = jnp.concatenate([own_seg, other_seg])
    seg_global = ordered(c, own_seg, other_seg)
    total = 2 * span
    q_block, k_block = 512, 256
    bounds = segment_bounds(seg_global, q_block, FINE)
    back_bounds = segment_bounds(seg_global, k_block, FINE)
    shift = jnp.reshape(c * (total // FINE // 2), (1,)).astype(jnp.int32)
    seg_k = jnp.broadcast_to(seg_store[:, None], (total, 128))
    seg_q = jnp.broadcast_to(seg_store[None, :], (8, total))
    attn_args = (seg_k, seg_q) + bounds + (shift,)
    back_args = (seg_k, seg_q) + back_bounds + (shift,)
    mixed, lse, mixed_other = [], [], []
    for p in range(pairs):
        if p > 2:
            attn_args = attn_args[:2] + (after(attn_args[2], *mixed_other[: p - 1]),) + attn_args[3:]
        out, one = attn_fwd(qkv, *attn_args, p, pairs, group, head_size, q_block, 6)
        mixed.append(out)
        lse.append(one)
        mixed_other.append(over_x(out[span:]))
    up_all, _last = lax.optimization_barrier((up_all, mixed[-1]))
    context_rows = ordered(
        c, jnp.concatenate([m[:span] for m in mixed], 1), jnp.concatenate(mixed_other, 1), 1
    )

    which = t.reshape(1)
    first, norm_one, inv_one, first_t, act_low, slope = up_layer(
        which, context_rows, tokens, vecs, up_add, up_all, nt
    )
    down_all, first = lax.optimization_barrier((down_all, first))
    out_low, branch, branch_t, grad_second, vec_two = down_layer(
        which, out_grad, vecs, first, act_low, down_all, nt
    )
    (down_sum,) = grads_layer([branch_t, act_low], nz, nt, 2)
    hidden_low, attn_t, grad_in, grad_context, vec_one, quarter = back_layer(
        vecs, branch, grad_second, slope, norm_one, inv_one, up_all, down_all, down_sum, nz, nt
    )
    out_low = after(out_low, quarter)
    out_other = over_y(out_low)
    other_sum, down_part, dctx = grads_layer([first_t, hidden_low, attn_t, context_rows], nz, nt, 3, quarter, grad_context)
    grad_down = ordered(c, down_part, over_x(down_part), 0).astype(F32).T
    part = lax.psum_scatter(other_sum, ("tensor", "z", "context"), scatter_dimension=0, tiled=True)
    part = ordered(c, part, over_x(part), 0).astype(F32)
    grad_up = part[:, : hidden // nt]
    grad_proj = part[:, hidden // nt :].T

    mixed = lax.optimization_barrier(tuple(mixed) + (quarter,))[:pairs]
    dqkv = attn_bwd(
        qkv, jnp.concatenate(mixed, axis=1), dctx, jnp.concatenate(lse), *back_args, pairs, group, head_size, k_block, 3
    )
    layer_output = ordered(t, out_low[None], out_other[None])
    dqkv, grad_down, layer_output = lax.optimization_barrier((dqkv, grad_down, layer_output))
    tokens_grad, grad_qkv, qv_sum, vec_sums = close_layer(
        dqkv, qkv_full, rows_t, grad_in, vec_one, vec_two, nz, group * wide
    )
    own_vecs = lax.dynamic_slice_in_dim(vec_sums, f * dblk, dblk, 1)
    vector_out = [own_vecs[row] for row in (0, 1, 2, 8, 9, 10)]
    up_rows, up_cols = up_bias.shape
    bias_up = vec_sums[3 : 3 + hidden // width].reshape(nt * up_rows, nf * up_cols)
    bias_up = lax.dynamic_slice(bias_up, (t * up_rows, f * up_cols), (up_rows, up_cols))
    per = wide // 128 * group
    kinds = [
        jnp.concatenate([qv_sum[(3 * g + which) * per :][:per] for g in range(pairs // group)])
        for which in (0, 2)
    ]
    grad_qv = jnp.stack(kinds).reshape(2, heads, head_size)
    grad_qv = lax.dynamic_slice_in_dim(grad_qv, f * (head_size // nf), head_size // nf, 2)

    return (
        layer_output,
        tokens_grad,
        grad_qkv,
        grad_qv,
        grad_proj,
        vector_out[0],
        vector_out[1],
        vector_out[2],
        grad_up,
        bias_up,
        grad_down,
        vector_out[3],
        vector_out[4],
        vector_out[5],
    )


def solution(mesh):
    sizes = tuple(mesh.shape[name] for name in ("fsdp", "context", "tensor"))
    nf, nc, nt = sizes
    shards = (
        P("fsdp", "context", None),
        P("fsdp", "context"),
        P(None, "fsdp", "tensor"),
        P(None, "tensor", "fsdp"),
        P("tensor", "fsdp"),
        P("fsdp"),
        P("fsdp"),
        P("fsdp"),
        P("fsdp", "tensor"),
        P("tensor", "fsdp"),
        P("tensor", "fsdp"),
        P("fsdp"),
        P("fsdp"),
        P("fsdp"),
    )
    in_specs = (shards[0],) + shards[1:] + (shards[0],)
    out_specs = (shards[0], shards[0]) + shards[2:]
    nz = nf // 2
    by_rows = nc == nt == 2 and nf % 2 == 0 and nz & (nz - 1) == 0
    rows_mesh = jax.sharding.Mesh(mesh.devices.reshape(nz, 2, nc, nt), AXES) if by_rows else None

    def finer(spec):
        return P(*(("z", "core") if name == "fsdp" else name for name in spec))

    def program(*args):
        if by_rows and args[0].shape[0] // nf == nt:
            return jax.shard_map(
                functools.partial(on_device_rows, sizes),
                mesh=rows_mesh,
                in_specs=tuple(finer(spec) for spec in in_specs),
                out_specs=tuple(finer(spec) for spec in out_specs),
                check_vma=False,
            )(*args)
        return jax.shard_map(
            on_device_general, mesh=mesh, in_specs=in_specs, out_specs=out_specs, check_vma=False
        )(*args)

    return program
```
